32 devices in a mesh: fsdp: 16 (over z, y, x), tensor: 2 (over core).
Axes of the slice: x: 2, y: 2, z: 4, core: 2. Of those that a mesh axis runs over, the one named last changes fastest.
Arguments:
- inputs: float32 [16384, 768], P(('fsdp', 'tensor')), may hold values from -6 to 6
- segment_ids: int32 [16384], P('fsdp'), may hold values from 0 to 39, never falling along the last dimension, each value on 1 to 800 neighbouring positions
- qkv_weight: float32 [3, 768, 768], P(None, 'fsdp', 'tensor'), may hold values from -0.21875 to 0.21875
- out_weight: float32 [768, 768], P('tensor', 'fsdp'), may hold values from -0.875 to 0.875
- up_weight: float32 [768, 3072], P('fsdp', 'tensor'), may hold values from -0.21875 to 0.21875
- down_weight: float32 [3072, 768], P('tensor', 'fsdp'), may hold values from -0.109375 to 0.109375
- gain_one: float32 [768], P('fsdp'), may hold values from 0.5 to 1.5
- shift_one: float32 [768], P('fsdp'), may hold values from -4 to 4
- gain_two: float32 [768], P('fsdp'), may hold values from 0.5 to 1.5
- shift_two: float32 [768], P('fsdp'), may hold values from -4 to 4
- cotangent: bfloat16 [16384, 768], P(('fsdp', 'tensor')), may hold values from -6 to 6
Outputs:
- outputs: float32 [16384, 768], P(('fsdp', 'tensor'))
- input_grad: float32 [16384, 768], P(('fsdp', 'tensor'))
- qkv_grad: float32 [3, 768, 768], P(None, 'fsdp', 'tensor')
- out_grad: float32 [768, 768], P('tensor', 'fsdp')
- up_grad: float32 [768, 3072], P('fsdp', 'tensor')
- down_grad: float32 [3072, 768], P('tensor', 'fsdp')
- gain_one_grad: float32 [768], P('fsdp')
- shift_one_grad: float32 [768], P('fsdp')
- gain_two_grad: float32 [768], P('fsdp')
- shift_two_grad: float32 [768], P('fsdp')
The draws below stay inside these ranges and needn't reach their ends.
Inputs may be any that keep to these rules, and one draw needn't show every extreme that they name: `segment_ids`: ids never fall along the tokens; each document holds 1 to 800 tokens and one holds exactly 800; a document may run past a sequence's end, and attention never crosses a sequence's end.
All inputs are finite; a program needn't handle non-finite values.
Results may differ from the reference program's by a relative error of at most 0.015.
Values may be sent and summed in bfloat16 or wider, within the bound.
No kernel may reach another device: no remote copies, remote signals or barrier semaphores. Data moves between devices by JAX's collectives and lax.ppermute only.
A program may use at most 128 MiB of HBM per device.

```python
import math
import jax
import jax.numpy as jnp
import numpy as np
from jax import lax

D = 768
H = 12
HD = 64
FF = 3072
LEN = 1024
MAXDOC = 800
TOKENS = 16384
DOCS = 40


def strengthened(entries, own_key, source, target, parts, factor):
    owner, partner = [(jnp.arange(entries.shape[dim]) // (entries.shape[dim] // parts)).reshape([-1 if axis == dim else 1 for axis in range(entries.ndim)]) for dim in (source, target)]
    chosen = jax.random.permutation(own_key, parts)[partner]
    strong = (owner == chosen) | (owner == (partner + parts // 2) % parts)
    return jnp.where(strong, factor * entries, entries)


def levels(stream_key, extent, split, least, top_value):
    level = 1.0
    for dim, shards_of in split:
        heights = jax.random.uniform(jax.random.fold_in(jax.random.fold_in(stream_key, 6), dim), (shards_of,), jnp.float32, least / len(split), top_value / len(split))
        level = level * jnp.repeat(jnp.exp(heights), extent[dim] // shards_of).reshape((-1,) + (1,) * (len(extent) - 1 - dim))
    return level


def profile(amount, total, most, skew):
    portions = [(1 << 20) // math.isqrt(grade ** skew) + 1 for grade in range(2, amount + 1)]
    spare, holding = total - most - (amount - 1), [1] * (amount - 1)
    while spare > 0:
        movable = [i for i in range(amount - 1) if holding[i] < most]
        pool, remaining = sum([portions[i] for i in movable]), spare
        for i in movable:
            extra = min(most - holding[i], max(1, remaining * portions[i] // pool), spare)
            holding[i] = holding[i] + extra
            spare = spare - extra
    return np.array([most] + holding)


def uneven_parts(key, count, total, reach, skew):
    if count == 2:
        one = jax.random.randint(key, (), max(1, total - reach), min(reach, total - 1) + 1)
        return jnp.stack([one, total - one])
    sizes = jnp.asarray(profile(count, total, reach, skew), jnp.int32)
    twos = (count - 1) // 2
    source_of, sink = sizes[1:1 + 2 * twos:2], sizes[2:2 + 2 * twos:2]
    room = jnp.minimum(source_of - 1, reach - sink)
    moved = jax.random.randint(jax.random.fold_in(key, 1), (twos,), 0, 1 << 20) % (room + 1)
    sizes = sizes.at[1:1 + 2 * twos:2].set(source_of - moved).at[2:2 + 2 * twos:2].set(sink + moved)
    return sizes[jax.random.permutation(jax.random.fold_in(key, 2), count)]


def scatter_about(own_key, extent, scale, limit, split=(), held_as=jnp.bfloat16):
    factor_of = levels(own_key, extent, split, -0.22, 0.18) if split else 1.0
    values = jax.random.normal(own_key, extent, jnp.float32) * scale * factor_of
    return jnp.minimum(jnp.maximum(values, -limit), limit).astype(held_as)


def bell_draw_with(key, extent, scale, reach, cuts, heavy, kind=jnp.bfloat16):
    drawn = scale * jax.random.normal(key, extent, jnp.float32)
    if cuts:
        drawn = drawn * levels(key, extent, cuts, -0.22, 0.18)
    return jnp.clip(strengthened(drawn, jax.random.fold_in(key, 3), *heavy), -reach, reach).astype(kind)


def setup_inputs(seed: int = 0) -> dict:
    splits = jax.random.split(jax.random.key(seed), 12)
    return {
        "inputs": bell_draw_with(splits[0], (TOKENS, D), 1.0, 6.0, ((0, 32),), (0, 1, 32, 2.75), jnp.float32),
        "segment_ids": jnp.searchsorted(jnp.cumsum(uneven_parts(splits[1], DOCS, TOKENS, MAXDOC, 2)), jnp.arange(TOKENS), side="right").astype(jnp.int32),
        "qkv_weight": scatter_about(splits[2], (3, D, D), D ** -0.5, 0.21875, ((1, 16), (2, 2)), jnp.float32),
        "out_weight": scatter_about(splits[3], (D, D), (D // 16) ** -0.5, 0.875, ((0, 2), (1, 16)), jnp.float32),
        "up_weight": scatter_about(splits[4], (D, FF), D ** -0.5, 0.21875, ((0, 16), (1, 2)), jnp.float32),
        "down_weight": scatter_about(splits[5], (FF, D), FF ** -0.5, 0.109375, ((0, 2), (1, 16)), jnp.float32),
        "gain_one": jnp.clip(1.0 + 0.1 * jax.random.normal(splits[6], (D,), jnp.float32), 0.5, 1.5),
        "shift_one": scatter_about(splits[7], (D,), 0.3, 4.0, ((0, 16),), jnp.float32),
        "gain_two": jnp.clip(1.0 + 0.1 * jax.random.normal(splits[8], (D,), jnp.float32), 0.5, 1.5),
        "shift_two": scatter_about(splits[9], (D,), 0.3, 4.0, ((0, 16),), jnp.float32),
        "cotangent": bell_draw_with(splits[10], (TOKENS, D), 1.0, 6.0, ((0, 32),), (0, 1, 32, 2.75)),
    }


HIGH = lax.Precision.HIGHEST
EPS = 1e-05

@jax.custom_vjp
def low(v):
    return lax.optimization_barrier(v.astype(jnp.bfloat16)).astype(jnp.float32)

@jax.custom_vjp
def low_back(v):
    return v

def low_keep(v):
    return (low(v), None)

def low_pass(kept, grad):
    return (grad,)

def back_keep(v):
    return (v, None)

def back_low(kept, grad):
    return (low(grad),)
low.defvjp(low_keep, low_pass)
low_back.defvjp(back_keep, back_low)

def norm_layer(values, gain, shift):
    centre = values - lax.optimization_barrier(jnp.mean(values, axis=-1, keepdims=True))
    spread = lax.optimization_barrier(jnp.mean(centre * centre, axis=-1, keepdims=True))
    return centre * lax.rsqrt(spread + EPS) * gain + shift

def one_sequence(tokens, seg, qkv_w, out_w, up_w, down_w, gain_a, shift_a, gain_b, shift_b):
    length = tokens.shape[0]
    normed_one = low(norm_layer(tokens, gain_a, shift_a))
    projected = low_back(low(jnp.einsum('td,cde->cte', normed_one, qkv_w, precision=HIGH)))
    queries = projected[0].reshape(length, H, HD)
    keys = projected[1].reshape(length, H, HD)
    values = projected[2].reshape(length, H, HD)
    scores = low_back(jnp.einsum('qhd,khd->hqk', queries, keys, precision=HIGH) * HD ** (-0.5))
    places = jnp.arange(length)
    allowed = (places[:, None] >= places[None, :]) & (seg[:, None] == seg[None, :])
    scores = jnp.where(allowed[None], scores, -1e+30)
    probs = jax.nn.softmax(scores, axis=-1)
    attended = jnp.einsum('hqk,khd->qhd', low(probs), values, precision=HIGH)
    attended = low_back(low(attended)).reshape(length, D)
    branch_attn = low_back(jnp.dot(attended, out_w, precision=HIGH))
    middle = tokens + branch_attn
    normed_two = low(norm_layer(middle, gain_b, shift_b))
    pre_act = low_back(jnp.dot(normed_two, up_w, precision=HIGH))
    activation = low(jax.nn.gelu(pre_act, approximate=True))
    branch_mlp = low_back(jnp.dot(activation, down_w, precision=HIGH))
    return middle + branch_mlp

def reference(inputs, segment_ids, qkv_weight, out_weight, up_weight, down_weight, gain_one, shift_one, gain_two, shift_two, cotangent):

    def forward(tokens, qkv_w, out_w, up_w, down_w, gain_a, shift_a, gain_b, shift_b):
        rounded = [low(w) for w in (qkv_w, out_w, up_w, down_w, gain_a, shift_a, gain_b, shift_b)]
        seqs_in = tokens.reshape(-1, LEN, D)
        seg_in = segment_ids.reshape(-1, LEN)

        def step(carry, item):
            return (carry, one_sequence(item[0], item[1], *rounded))
        _, result = lax.scan(jax.checkpoint(step), jnp.zeros((), jnp.float32), (seqs_in, seg_in))
        return result.reshape(-1, D)
    result, pull = jax.vjp(forward, inputs, qkv_weight, out_weight, up_weight, down_weight, gain_one, shift_one, gain_two, shift_two)
    grads = pull(cotangent.astype(jnp.float32))
    return (result, grads[0], grads[1], grads[2], grads[3], grads[4], grads[5], grads[6], grads[7], grads[8])
```

```python
import functools

import jax
import jax.numpy as jnp
from jax import lax
from jax.sharding import PartitionSpec as P

HD = 64
LEN = 1024
QB = 512
EPS = 1e-05
LOW = jnp.bfloat16
WIDE = jnp.float32


def norm_stats(values):
    centre = values - jnp.mean(values, axis=-1, keepdims=True)
    spread = jnp.mean(centre * centre, axis=-1, keepdims=True)
    rate = lax.rsqrt(spread + EPS)
    return centre * rate, rate


def norm_back(grad, hat, rate, gain):
    scaled = grad * gain
    return rate * (
        scaled
        - jnp.mean(scaled, axis=-1, keepdims=True)
        - hat * jnp.mean(scaled * hat, axis=-1, keepdims=True)
    )


def swap_cores(values):
    return lax.ppermute(values, "tensor", [(0, 1), (1, 0)])


def both_halves(own, core):
    other = swap_cores(own)
    return jnp.where(
        core == 0,
        jnp.concatenate([own, other], axis=0),
        jnp.concatenate([other, own], axis=0),
    )


def hop(values, bits, size):
    return lax.ppermute(values, "fsdp", [(i, i ^ bits) for i in range(size)])


def places(size, first, me):
    table = []
    for block in range(size):
        away = me ^ block
        low, mid, high = away & 1, (away >> 1) & 1, away >> 2
        lead = (low * 2 + mid) if first == 2 else (mid * 2 + low)
        table.append(lead * (size // 4) + high)
    return table


def gather_pair(left, right, size):
    def far(values):
        parts = [values] + [hop(values, 4 * k, size) for k in range(1, size // 4)]
        return jnp.concatenate(parts, axis=0)

    left, right = far(left), far(right)
    left = jnp.concatenate([left, hop(left, 2, size)], axis=0)
    right = jnp.concatenate([right, hop(right, 1, size)], axis=0)
    left = jnp.concatenate([left, hop(left, 1, size)], axis=0)
    right = jnp.concatenate([right, hop(right, 2, size)], axis=0)
    return left, right


def scatter_pair(left, right, size):
    def fold(values, bits):
        half = values.shape[0] // 2
        other = hop(values[half:], bits, size)
        return (values[:half].astype(WIDE) + other.astype(WIDE)).astype(LOW)

    left, right = fold(left, 1), fold(right, 2)
    left, right = fold(left, 2), fold(right, 1)

    def near(values):
        count = size // 4
        rows = values.shape[0] // count
        total = values[:rows].astype(WIDE)
        for k in range(1, count):
            total = total + hop(values[k * rows : (k + 1) * rows], 4 * k, size).astype(WIDE)
        return total

    return near(left), near(right)


def natural(values, table, size):
    rows = values.shape[0] // size
    return jnp.concatenate(
        [lax.dynamic_slice_in_dim(values, table[j] * rows, rows, 0) for j in range(size)], axis=0
    )


def relative(values, first, me, size):
    rows = values.shape[0] // size
    pieces = []
    for place in range(size):
        lead, high = place // (size // 4), place % (size // 4)
        one, two = lead >> 1, lead & 1
        low, mid = (one, two) if first == 2 else (two, one)
        block = me ^ (high * 4 + mid * 2 + low)
        pieces.append(lax.dynamic_slice_in_dim(values, block * rows, rows, 0))
    return jnp.concatenate(pieces, axis=0)


def gather_rows(left, right, me, size):
    if size != 16:
        return (
            lax.all_gather(left, "fsdp", axis=0, tiled=True),
            lax.all_gather(right, "fsdp", axis=0, tiled=True),
        )
    left, right = gather_pair(left, right, size)
    return natural(left, places(size, 2, me), size), natural(right, places(size, 1, me), size)


def scatter_rows(left, right, me, size):
    if size != 16:
        return (
            lax.psum_scatter(left.astype(WIDE), "fsdp", scatter_dimension=0, tiled=True),
            lax.psum_scatter(right.astype(WIDE), "fsdp", scatter_dimension=0, tiled=True),
        )
    return scatter_pair(
        relative(left.astype(LOW), 2, me, size), relative(right.astype(LOW), 1, me, size), size
    )


def block_scores(query_rows, keys, seg, start):
    spots = jnp.arange(LEN)
    scores = jnp.einsum("qd,kd->qk", query_rows, keys, preferred_element_type=WIDE) * HD**-0.5
    rows_at = lax.dynamic_slice_in_dim(spots, start, QB, 0)
    seg_rows = lax.dynamic_slice_in_dim(seg, start, QB, 0)
    allowed = (rows_at[:, None] >= spots[None, :]) & (seg_rows[:, None] == seg[None, :])
    return jnp.where(allowed, scores, -1e30)


def attend_head(item):
    queries, keys, values, seg = item
    attended, lse_rows = [], []
    for start in range(0, LEN, QB):
        scores = block_scores(queries[start : start + QB], keys, seg, start)
        top = jnp.max(scores, axis=-1, keepdims=True)
        expo = jnp.exp(scores - top)
        total = jnp.sum(expo, axis=-1, keepdims=True)
        probs = (expo / total).astype(LOW)
        attended.append(jnp.dot(probs, values, preferred_element_type=WIDE).astype(LOW))
        lse_rows.append((top + jnp.log(total))[:, 0])
    return jnp.concatenate(attended, axis=0), jnp.concatenate(lse_rows, axis=0)


def attend_back(item):
    queries, keys, values, seg, lse, head_grad = item
    key_grad = jnp.zeros(keys.shape, WIDE)
    value_grad = jnp.zeros(values.shape, WIDE)
    query_grads = []
    for start in range(0, LEN, QB):
        query_rows = queries[start : start + QB]
        grad_rows = head_grad[start : start + QB]
        scores = block_scores(query_rows, keys, seg, start)
        probs = jnp.exp(scores - lse[start : start + QB][:, None])
        value_grad = value_grad + jnp.einsum(
            "qk,qd->kd", probs.astype(LOW), grad_rows, preferred_element_type=WIDE
        )
        probs_grad = jnp.einsum("qd,kd->qk", grad_rows, values, preferred_element_type=WIDE)
        centre = jnp.sum(probs * probs_grad, axis=-1, keepdims=True)
        scores_grad = (probs * (probs_grad - centre)).astype(LOW)
        query_grads.append(jnp.dot(scores_grad, keys, preferred_element_type=WIDE) * HD**-0.5)
        key_grad = (
            key_grad
            + jnp.einsum("qk,qd->kd", scores_grad, query_rows, preferred_element_type=WIDE)
            * HD**-0.5
        )
    return jnp.concatenate(query_grads, axis=0), key_grad, value_grad


def split_heads(matrix, heads):
    return matrix.reshape(LEN, heads, HD).transpose(1, 0, 2)


def merge_heads(stacked, heads):
    return stacked.transpose(1, 0, 2).reshape(LEN, heads * HD)


def body(
    size,
    inputs,
    segment_ids,
    qkv_weight,
    out_weight,
    up_weight,
    down_weight,
    gain_one,
    shift_one,
    gain_two,
    shift_two,
    cotangent,
):
    me = lax.axis_index("fsdp")
    core = lax.axis_index("tensor")
    rows = qkv_weight.shape[1]
    width = qkv_weight.shape[2]
    heads = width // HD
    hidden = up_weight.shape[1]
    half = inputs.shape[0]

    vectors = jnp.stack([gain_one, shift_one, gain_two, shift_two], axis=1)
    first = jnp.concatenate(
        [
            qkv_weight.transpose(1, 0, 2).reshape(rows, 3 * width),
            vectors,
            jnp.zeros((rows, 124), WIDE),
        ],
        axis=1,
    ).astype(LOW)
    cut = (3 * width + 128) // 2
    first_a, first_b = gather_rows(first[:, :cut], first[:, cut:], me, size)
    second_a, second_b = gather_rows(
        jnp.concatenate([up_weight, out_weight.T], axis=1).astype(LOW),
        down_weight.T.astype(LOW),
        me,
        size,
    )
    first = jnp.concatenate([first_a, first_b], axis=1)
    qkv_w = first[:, : 3 * width]
    vectors = first[:, 3 * width : 3 * width + 4].astype(WIDE).T
    gain_a, shift_a, gain_b, shift_b = (vectors[k : k + 1] for k in range(4))
    up_w, out_wt, down_wt = second_a[:, :hidden], second_a[:, hidden:], second_b

    tokens = both_halves(inputs, core)
    grad_y = both_halves(cotangent, core)
    hat_one, rate_one = norm_stats(tokens)
    normed_one = (hat_one * gain_a + shift_a).astype(LOW)
    projected = jnp.dot(normed_one, qkv_w, preferred_element_type=WIDE).astype(LOW)
    queries, keys, values = (
        split_heads(projected[:, k * width : (k + 1) * width], heads) for k in range(3)
    )
    seg_rows = jnp.broadcast_to(segment_ids[None], (heads, LEN))
    attended, lse = lax.map(attend_head, (queries, keys, values, seg_rows))
    attended = merge_heads(attended, heads)
    part = jnp.einsum("te,de->td", attended, out_wt, preferred_element_type=WIDE).astype(LOW)
    middle = tokens + (part.astype(WIDE) + swap_cores(part).astype(WIDE))
    hat_two, rate_two = norm_stats(middle)
    normed_two = (hat_two * gain_b + shift_b).astype(LOW)
    pre_act = jnp.dot(normed_two, up_w, preferred_element_type=WIDE)
    act, gelu_pull = jax.vjp(functools.partial(jax.nn.gelu, approximate=True), pre_act)
    act = act.astype(LOW)
    branch = jnp.einsum("tf,df->td", act, down_wt, preferred_element_type=WIDE).astype(LOW)

    def own_half(values):
        return lax.dynamic_slice_in_dim(values, core * half, half, 0)

    def other_half(values):
        return lax.dynamic_slice_in_dim(values, (1 - core) * half, half, 0)

    outputs = own_half(middle) + (
        own_half(branch).astype(WIDE) + swap_cores(other_half(branch)).astype(WIDE)
    )

    down_part = jnp.einsum("td,tf->df", grad_y, act, preferred_element_type=WIDE)
    act_grad = jnp.dot(grad_y, down_wt, preferred_element_type=WIDE)
    pre_grad = gelu_pull(act_grad)[0].astype(LOW)
    up_part = jnp.einsum("td,tf->df", normed_two, pre_grad, preferred_element_type=WIDE)
    up_grad, down_grad = scatter_rows(up_part, down_part, me, size)
    part = jnp.einsum("tf,df->td", pre_grad, up_w, preferred_element_type=WIDE).astype(LOW)
    two_grad = part.astype(WIDE) + swap_cores(part).astype(WIDE)
    middle_grad = grad_y.astype(WIDE) + norm_back(two_grad, hat_two, rate_two, gain_b)
    gain_two_part = jnp.sum(two_grad * hat_two, axis=0)
    shift_two_part = jnp.sum(two_grad, axis=0)
    branch_grad = middle_grad.astype(LOW)
    out_part = jnp.einsum("td,te->de", branch_grad, attended, preferred_element_type=WIDE)
    attended_grad = jnp.dot(branch_grad, out_wt, preferred_element_type=WIDE).astype(LOW)
    query_grad, key_grad, value_grad = lax.map(
        attend_back,
        (queries, keys, values, seg_rows, lse, split_heads(attended_grad, heads)),
    )
    proj_grad = jnp.concatenate(
        [merge_heads(g.astype(LOW), heads) for g in (query_grad, key_grad, value_grad)], axis=1
    )
    qkv_part = jnp.einsum("td,te->de", normed_one, proj_grad, preferred_element_type=WIDE)
    part = jnp.einsum("te,de->td", proj_grad, qkv_w, preferred_element_type=WIDE).astype(LOW)
    one_grad = part.astype(WIDE) + swap_cores(part).astype(WIDE)
    gain_one_part = jnp.sum(one_grad * hat_one, axis=0)
    shift_one_part = jnp.sum(one_grad, axis=0)
    input_grad = own_half(middle_grad + norm_back(one_grad, hat_one, rate_one, gain_a))
    sums = jnp.stack([gain_one_part, shift_one_part, gain_two_part, shift_two_part], axis=1)
    sums = jnp.concatenate([sums, jnp.zeros((sums.shape[0], 124), WIDE)], axis=1)
    tail_a, tail_b = scatter_rows(
        jnp.concatenate([qkv_part[:, : 2 * width], sums], axis=1),
        jnp.concatenate([qkv_part[:, 2 * width :], out_part], axis=1),
        me,
        size,
    )
    qkv_grad = jnp.stack(
        [tail_a[:, :width], tail_a[:, width : 2 * width], tail_b[:, :width]], axis=0
    )
    sums = tail_a[:, 2 * width :]
    return (
        outputs,
        input_grad,
        qkv_grad,
        tail_b[:, width:].T,
        up_grad,
        down_grad.T,
        sums[:, 0],
        sums[:, 1],
        sums[:, 2],
        sums[:, 3],
    )


def solution(mesh):
    tokens = P(("fsdp", "tensor"), None)
    split = P("fsdp")
    weights = (
        P(None, "fsdp", "tensor"),
        P("tensor", "fsdp"),
        P("fsdp", "tensor"),
        P("tensor", "fsdp"),
        split,
        split,
        split,
        split,
    )
    return jax.shard_map(
        functools.partial(body, mesh.shape["fsdp"]),
        mesh=mesh,
        in_specs=(tokens, split) + weights + (tokens,),
        out_specs=(tokens, tokens) + weights,
        check_vma=False,
    )
```

```python
import functools
import math

import jax
import jax.numpy as jnp
from jax import lax
from jax.experimental import pallas as pl
from jax.experimental.pallas import tpu as pltpu
from jax.sharding import PartitionSpec as P

HD = 64
EPS = 1e-05
LOW = jnp.bfloat16
WIDE = jnp.float32
BLOCKS = 16
ROWS = 256
LANES = 128
LOG2E = math.log2(math.e)
MASKED = -1e30


def nn(a, b):
    return jnp.dot(a, b, preferred_element_type=WIDE)


def nt(a, b):
    return lax.dot_general(a, b, (((1,), (1,)), ((), ())), preferred_element_type=WIDE)


def tn(a, b):
    return lax.dot_general(a, b, (((0,), (0,)), ((), ())), preferred_element_type=WIDE)


def cost(flops, moved, special=0):
    return pl.CostEstimate(flops=int(flops), bytes_accessed=int(moved), transcendentals=int(special))


def params():
    return pltpu.CompilerParams(
        dimension_semantics=("arbitrary",), vmem_limit_bytes=60 * 1024 * 1024
    )


def fixed(shape, index=None):
    place = index or (0,) * len(shape)
    return pl.BlockSpec(shape, lambda i, *_: place, pipeline_mode=pl.Buffered(1))


def kept(shape, index=None):
    place = index or (0,) * len(shape)
    return pl.BlockSpec(shape, lambda i, *_: place)


def by_row(width, rows=ROWS):
    return pl.BlockSpec((rows, width), lambda i, *_: (i, 0))


def hat_of(values):
    centre = values - jnp.mean(values, axis=-1, keepdims=True)
    rate = lax.rsqrt(jnp.mean(centre * centre, axis=-1, keepdims=True) + EPS)
    return centre * rate, rate


def norm_back(grad, hat, rate, gain):
    scaled = grad * gain
    return rate * (
        scaled
        - jnp.mean(scaled, axis=-1, keepdims=True)
        - hat * jnp.mean(scaled * hat, axis=-1, keepdims=True)
    )


def at_block(table, place, rows):
    return pl.ds(pl.multiple_of(table[place] * rows, 16), rows)


def enter_kernel(table, own, other, wa, wb, normed, proj, whole, vectors, loose):
    step = pl.program_id(0)
    rows = wa.shape[0] // BLOCKS
    cut = wa.shape[1]
    rest = whole.shape[1] - cut

    @pl.when(step == 0)
    def _():
        for j in range(BLOCKS):
            to = slice(j * rows, (j + 1) * rows)
            whole[to, :cut] = wa[at_block(table, j, rows), :]
            late = wb[at_block(table, BLOCKS + j, rows), :]
            whole[to, cut:] = late[:, :rest]
            loose[to, :] = late[:, rest:].astype(WIDE)
        vectors[...] = loose[...].T[:8]

    mine = (step // 2) == table[2 * BLOCKS]
    values = jnp.where(mine, own[...], other[...])
    hat, _ = hat_of(values)
    low = (hat * vectors[0:1, :] + vectors[1:2, :]).astype(LOW)
    normed[...] = low
    proj[...] = nn(low, whole[...]).astype(LOW)


def enter(table, own, other, wa, wb):
    half, width = own.shape
    total = wa.shape[1] + wb.shape[1] - LANES
    steps = 2 * half // ROWS
    pair = pl.BlockSpec((ROWS, width), lambda i, *_: (i % (steps // 2), 0))
    return pl.pallas_call(
        enter_kernel,
        grid_spec=pltpu.PrefetchScalarGridSpec(
            num_scalar_prefetch=1,
            grid=(steps,),
            in_specs=[pair, pair, fixed(wa.shape), fixed(wb.shape)],
            out_specs=[by_row(width), by_row(total), kept((width, total)), kept((8, width))],
            scratch_shapes=[pltpu.VMEM((width, LANES), WIDE)],
        ),
        out_shape=[
            jax.ShapeDtypeStruct((2 * half, width), LOW),
            jax.ShapeDtypeStruct((2 * half, total), LOW),
            jax.ShapeDtypeStruct((width, total), LOW),
            jax.ShapeDtypeStruct((8, width), WIDE),
        ],
        compiler_params=params(),
        cost_estimate=cost(4 * half * width * total, 12 * half * width, 0),
        name="enter",
    )(table, own, other, wa, wb)


def build_bias(bias, seg_col, seg_row):
    length = bias.shape[0]
    for start in range(0, length, ROWS):
        lanes = slice(start, start + ROWS)
        until = start + ROWS
        shape = (until, ROWS)
        key_at = lax.broadcasted_iota(jnp.int32, shape, 0)
        query_at = lax.broadcasted_iota(jnp.int32, shape, 1) + start
        same = jnp.broadcast_to(seg_col[:until, 0:1], shape) == jnp.broadcast_to(
            seg_row[0:1, lanes], shape
        )
        bias[:until, lanes] = jnp.where((key_at <= query_at) & same, 0.0, MASKED)


def one_head(flipped, head):
    empty = jnp.zeros((HD, flipped.shape[1]), flipped.dtype)
    if head == 0:
        return jnp.concatenate([flipped[:HD], empty], axis=0)
    return jnp.concatenate([empty, flipped[HD:]], axis=0)


def attend_kernel(queries, keys, values, seg_col, seg_row, out, lse, bias):
    @pl.when(pl.program_id(0) == 0)
    def _():
        build_bias(bias, seg_col, seg_row)

    length = queries.shape[0]
    q_flip = queries[...].T
    v_flip = values[...].T
    sides = [one_head(q_flip, head) for head in range(2)]
    for start in range(0, length, ROWS):
        lanes = slice(start, start + ROWS)
        until = start + ROWS
        pieces = []
        for head in range(2):
            scores = nn(keys[:until], sides[head][:, lanes]) * (HD**-0.5 * LOG2E)
            scores = scores + bias[:until, lanes]
            top = jnp.max(scores, axis=0, keepdims=True)
            expo = jnp.exp2(scores - top)
            total = jnp.sum(expo, axis=0, keepdims=True)
            flat = nn(v_flip[head * HD : (head + 1) * HD, :until], expo.astype(LOW))
            pieces.append(flat / total)
            lse[head : head + 1, lanes] = top + jnp.log(total) * LOG2E
        out[lanes, :] = jnp.concatenate(pieces, axis=0).T.astype(LOW)


def attend(proj, seg_col, seg_row):
    length = proj.shape[0]
    pairs = proj.shape[1] // (3 * LANES)

    def part(k):
        return pl.BlockSpec((length, LANES), lambda i: (0, k * pairs + i))

    return pl.pallas_call(
        attend_kernel,
        grid=(pairs,),
        in_specs=[part(0), part(1), part(2), fixed(seg_col.shape), fixed(seg_row.shape)],
        out_specs=[
            pl.BlockSpec((length, LANES), lambda i: (0, i)),
            pl.BlockSpec((8, length), lambda i: (i, 0)),
        ],
        out_shape=[
            jax.ShapeDtypeStruct((length, pairs * LANES), LOW),
            jax.ShapeDtypeStruct((8 * pairs, length), WIDE),
        ],
        scratch_shapes=[pltpu.VMEM((length, length), WIDE)],
        compiler_params=params(),
        cost_estimate=cost(
            8 * pairs * length * length * LANES, 8 * length * pairs * LANES, pairs * length * length
        ),
        name="attend",
    )(proj, proj, proj, seg_col, seg_row)


def attend_back_kernel(
    queries, keys, values, out, grad, lse, seg_col, seg_row, result, bias, k_sum, v_sum
):
    @pl.when(pl.program_id(0) == 0)
    def _():
        build_bias(bias, seg_col, seg_row)

    length = queries.shape[0]
    scale = HD**-0.5
    q_flip = queries[...].T
    k_flip = keys[...].T
    g_flip = grad[...].T
    product = out[...].T.astype(WIDE) * g_flip.astype(WIDE)
    k_sum[...] = jnp.zeros_like(k_sum)
    v_sum[...] = jnp.zeros_like(v_sum)
    q_sides = [one_head(q_flip, head) for head in range(2)]
    g_sides = [one_head(g_flip, head) for head in range(2)]
    for start in range(0, length, ROWS):
        lanes = slice(start, start + ROWS)
        until = start + ROWS
        pieces = []
        for head in range(2):
            scores = nn(keys[:until], q_sides[head][:, lanes]) * (scale * LOG2E)
            probs = jnp.exp2(scores + bias[:until, lanes] - lse[head : head + 1, lanes])
            v_sum[head, :until] += nn(probs.astype(LOW), grad[lanes, :])
            centre = jnp.sum(
                product[head * HD : (head + 1) * HD, lanes], axis=0, keepdims=True
            )
            pull = nn(values[:until], g_sides[head][:, lanes])
            pull = (probs * (pull - centre)).astype(LOW)
            k_sum[head, :until] += nn(pull, queries[lanes, :])
            pieces.append(nn(k_flip[head * HD : (head + 1) * HD, :until], pull))
        result[0, lanes, :] = (jnp.concatenate(pieces, axis=0) * scale).T.astype(LOW)
    first = lax.broadcasted_iota(jnp.int32, (length, LANES), 1) < HD
    result[1] = (jnp.where(first, k_sum[0], k_sum[1]) * scale).astype(LOW)
    result[2] = jnp.where(first, v_sum[0], v_sum[1]).astype(LOW)


def attend_back(proj, out, grad, lse, seg_col, seg_row):
    length = proj.shape[0]
    pairs = proj.shape[1] // (3 * LANES)

    def part(k):
        return pl.BlockSpec((length, LANES), lambda i: (0, k * pairs + i))

    return pl.pallas_call(
        attend_back_kernel,
        grid=(pairs,),
        in_specs=[
            part(0),
            part(1),
            part(2),
            part(0),
            part(0),
            pl.BlockSpec((8, length), lambda i: (i, 0)),
            fixed(seg_col.shape),
            fixed(seg_row.shape),
        ],
        out_specs=pl.BlockSpec((3, length, LANES), lambda i: (0, 0, i)),
        out_shape=jax.ShapeDtypeStruct((3, length, pairs * LANES), LOW),
        scratch_shapes=[
            pltpu.VMEM((length, length), WIDE),
            pltpu.VMEM((2, length, LANES), WIDE),
            pltpu.VMEM((2, length, LANES), WIDE),
        ],
        compiler_params=params(),
        cost_estimate=cost(
            20 * pairs * length * length * LANES,
            16 * length * pairs * LANES,
            pairs * length * length,
        ),
        name="attend_back",
    )(proj, proj, proj, out, grad, lse, seg_col, seg_row)


def leave_kernel(table, att, packed, part, whole):
    rows = packed.shape[0] // BLOCKS

    @pl.when(pl.program_id(0) == 0)
    def _():
        for j in range(BLOCKS):
            whole[j * rows : (j + 1) * rows, :] = packed[at_block(table, j, rows), :]

    part[...] = nt(att[...], whole[...]).astype(LOW)


def leave(table, att, packed):
    length, inner = att.shape
    width = packed.shape[0]
    last = packed.shape[1] // inner - 1
    return pl.pallas_call(
        leave_kernel,
        grid_spec=pltpu.PrefetchScalarGridSpec(
            num_scalar_prefetch=1,
            grid=(length // ROWS,),
            in_specs=[by_row(inner), fixed((width, inner), (0, last))],
            out_specs=[by_row(width), kept((width, inner))],
        ),
        out_shape=[
            jax.ShapeDtypeStruct((length, width), LOW),
            jax.ShapeDtypeStruct((width, inner), LOW),
        ],
        compiler_params=params(),
        cost_estimate=cost(2 * length * inner * width, 4 * length * width),
        name="leave",
    )(table, att, packed)


def middle_kernel(table, own, other, part, far, vectors, middle, normed):
    mine = (pl.program_id(0) // 2) == table[2 * BLOCKS]
    tokens = jnp.where(mine, own[...], other[...])
    values = tokens + (part[...].astype(WIDE) + far[...].astype(WIDE))
    middle[...] = values
    hat, _ = hat_of(values)
    normed[...] = (hat * vectors[2:3, :] + vectors[3:4, :]).astype(LOW)


def second_norm(table, own, other, part, far, vectors):
    length, width = part.shape
    steps = length // ROWS
    pair = pl.BlockSpec((ROWS, width), lambda i, *_: (i % (steps // 2), 0))
    return pl.pallas_call(
        middle_kernel,
        grid_spec=pltpu.PrefetchScalarGridSpec(
            num_scalar_prefetch=1,
            grid=(steps,),
            in_specs=[pair, pair, by_row(width), by_row(width), fixed((8, width))],
            out_specs=[by_row(width), by_row(width)],
        ),
        out_shape=[
            jax.ShapeDtypeStruct((length, width), WIDE),
            jax.ShapeDtypeStruct((length, width), LOW),
        ],
        compiler_params=params(),
        cost_estimate=cost(20 * length * width, 18 * length * width),
        name="second_norm",
    )(table, own, other, part, far, vectors)


SIDE = 256


def feed_kernel(
    table,
    normed,
    grad_own,
    grad_other,
    up,
    down,
    branch,
    pulled,
    up_grad,
    down_grad,
    grad,
    normed_flip,
    grad_flip,
    up_whole,
    down_whole,
    act,
    pre,
    branch_sum,
    pulled_sum,
):
    step = pl.program_id(0)
    length = normed.shape[0]
    half = length // 2
    rows = up.shape[0] // BLOCKS

    @pl.when(step == 0)
    def _():
        mine = table[2 * BLOCKS]
        grad[pl.ds(pl.multiple_of(mine * half, half), half), :] = grad_own[...]
        grad[pl.ds(pl.multiple_of((1 - mine) * half, half), half), :] = grad_other[...]
        normed_flip[...] = normed[...].T
        grad_flip[...] = grad[...].T
        branch_sum[...] = jnp.zeros_like(branch_sum)
        pulled_sum[...] = jnp.zeros_like(pulled_sum)

    for j in range(BLOCKS):
        to = slice(j * rows, (j + 1) * rows)
        up_whole[to, :] = up[at_block(table, j, rows), :]
        down_whole[to, :] = down[at_block(table, BLOCKS + j, rows), :]

    for start in range(0, length, ROWS):
        at = slice(start, start + ROWS)
        wide = nn(normed[at, :], up_whole[...])
        square = wide * wide
        root = math.sqrt(2.0 / math.pi)
        bend = jnp.tanh(wide * (root + root * 0.044715 * square))
        share = 0.5 + 0.5 * bend
        slope = share + 0.5 * wide * (1.0 - bend * bend) * (
            root + 3.0 * root * 0.044715 * square
        )
        act[at, :] = (wide * share).astype(LOW)
        pre[at, :] = (nn(grad[at, :], down_whole[...]) * slope).astype(LOW)
        branch_sum[at, :] += nt(act[at, :], down_whole[...])
        pulled_sum[at, :] += nt(pre[at, :], up_whole[...])

    lifted = nn(normed_flip[...], pre[...]).astype(LOW)
    lowered = nn(grad_flip[...], act[...]).astype(LOW)
    for j in range(BLOCKS):
        take = slice(j * rows, (j + 1) * rows)
        up_grad[at_block(table, j, rows), :] = lifted[take]
        down_grad[at_block(table, BLOCKS + j, rows), :] = lowered[take]

    @pl.when(step == pl.num_programs(0) - 1)
    def _():
        branch[...] = branch_sum[...].astype(LOW)
        pulled[...] = pulled_sum[...].astype(LOW)


def feed(table, normed, grad_own, grad_other, packed, down):
    length, width = normed.shape
    hidden = down.shape[1]
    column = pl.BlockSpec((width, SIDE), lambda i, *_: (0, i))
    token = (length, width)
    return pl.pallas_call(
        feed_kernel,
        grid_spec=pltpu.PrefetchScalarGridSpec(
            num_scalar_prefetch=1,
            grid=(hidden // SIDE,),
            in_specs=[
                fixed(token),
                fixed(grad_own.shape),
                fixed(grad_other.shape),
                column,
                column,
            ],
            out_specs=[kept(token), kept(token), column, column],
            scratch_shapes=[
                pltpu.VMEM(token, LOW),
                pltpu.VMEM((width, length), LOW),
                pltpu.VMEM((width, length), LOW),
                pltpu.VMEM((width, SIDE), LOW),
                pltpu.VMEM((width, SIDE), LOW),
                pltpu.VMEM((length, SIDE), LOW),
                pltpu.VMEM((length, SIDE), LOW),
                pltpu.VMEM(token, WIDE),
                pltpu.VMEM(token, WIDE),
            ],
        ),
        out_shape=[
            jax.ShapeDtypeStruct(token, LOW),
            jax.ShapeDtypeStruct(token, LOW),
            jax.ShapeDtypeStruct((width, hidden), LOW),
            jax.ShapeDtypeStruct((width, hidden), LOW),
        ],
        compiler_params=params(),
        cost_estimate=cost(
            12 * length * width * hidden, 8 * length * width + 8 * width * hidden, length * hidden
        ),
        name="feed",
    )(table, normed, grad_own, grad_other, packed, down)


def middle_back_kernel(
    table,
    pulled,
    far,
    middle,
    grad_own,
    grad_other,
    vectors,
    out_whole,
    att,
    middle_grad,
    att_grad,
    out_grad,
    sums,
    out_sum,
):
    step = pl.program_id(0)
    rows = out_whole.shape[0] // BLOCKS

    @pl.when(step == 0)
    def _():
        out_sum[...] = jnp.zeros_like(out_sum)
        sums[...] = jnp.zeros_like(sums)

    mine = (step // 2) == table[2 * BLOCKS]
    grad = jnp.where(mine, grad_own[...].astype(WIDE), grad_other[...].astype(WIDE))
    pull = pulled[...].astype(WIDE) + far[...].astype(WIDE)
    hat, rate = hat_of(middle[...])
    whole = grad + norm_back(pull, hat, rate, vectors[2:3, :])
    middle_grad[...] = whole
    sums[0:1, :] += jnp.sum(pull * hat, axis=0, keepdims=True)
    sums[1:2, :] += jnp.sum(pull, axis=0, keepdims=True)
    low = whole.astype(LOW)
    att_grad[...] = nn(low, out_whole[...]).astype(LOW)
    out_sum[...] += tn(low, att[...])

    @pl.when(step == pl.num_programs(0) - 1)
    def _():
        for j in range(BLOCKS):
            out_grad[at_block(table, BLOCKS + j, rows), :] = out_sum[
                j * rows : (j + 1) * rows, :
            ].astype(LOW)


def middle_back(table, pulled, far, middle, grad_own, grad_other, vectors, out_whole, att):
    length, width = middle.shape
    inner = att.shape[1]
    steps = length // ROWS
    pair = pl.BlockSpec((ROWS, width), lambda i, *_: (i % (steps // 2), 0))
    return pl.pallas_call(
        middle_back_kernel,
        grid_spec=pltpu.PrefetchScalarGridSpec(
            num_scalar_prefetch=1,
            grid=(steps,),
            in_specs=[
                by_row(width),
                by_row(width),
                by_row(width),
                pair,
                pair,
                fixed((8, width)),
                fixed((width, inner)),
                by_row(inner),
            ],
            out_specs=[
                by_row(width),
                by_row(inner),
                kept((width, inner), (0, 1)),
                kept((8, width)),
            ],
            scratch_shapes=[pltpu.VMEM((width, inner), WIDE)],
        ),
        out_shape=[
            jax.ShapeDtypeStruct((length, width), WIDE),
            jax.ShapeDtypeStruct((length, inner), LOW),
            jax.ShapeDtypeStruct((width, 2 * inner), LOW),
            jax.ShapeDtypeStruct((8, width), WIDE),
        ],
        compiler_params=params(),
        cost_estimate=cost(4 * length * width * inner, 20 * length * width),
        name="middle_back",
    )(table, pulled, far, middle, grad_own, grad_other, vectors, out_whole, att)


def enter_back_kernel(
    table, proj_grad, normed, whole, held, pulled, left, right, normed_flip, pulled_sum
):
    step = pl.program_id(0)
    rows = normed.shape[1] // BLOCKS

    @pl.when(step == 0)
    def _():
        normed_flip[...] = normed[...].T
        pulled_sum[...] = jnp.zeros_like(pulled_sum)

    grad = proj_grad[0]
    weight = nn(normed_flip[...], grad).astype(LOW)

    @pl.when(step < 2)
    def _():
        for j in range(BLOCKS):
            left[at_block(table, j, rows), :] = weight[j * rows : (j + 1) * rows]

    @pl.when(step == 2)
    def _():
        for j in range(BLOCKS):
            right[at_block(table, BLOCKS + j, rows), :] = weight[j * rows : (j + 1) * rows]

    pulled_sum[...] += nt(grad, whole[...])

    @pl.when(step == 2)
    def _():
        pulled[...] = pulled_sum[...].astype(LOW)


def enter_back(table, proj_grad, normed, whole, held):
    length, width = normed.shape
    inner = proj_grad.shape[2]
    return pl.pallas_call(
        enter_back_kernel,
        grid_spec=pltpu.PrefetchScalarGridSpec(
            num_scalar_prefetch=1,
            grid=(3,),
            in_specs=[
                pl.BlockSpec((1, length, inner), lambda i, *_: (i, 0, 0)),
                fixed((length, width)),
                pl.BlockSpec((width, inner), lambda i, *_: (0, i)),
                pl.BlockSpec(memory_space=pl.ANY),
            ],
            out_specs=[
                kept((length, width)),
                pl.BlockSpec((width, inner), lambda i, *_: (0, jnp.minimum(i, 1))),
                kept((width, inner)),
            ],
            scratch_shapes=[pltpu.VMEM((width, length), LOW), pltpu.VMEM((length, width), WIDE)],
        ),
        out_shape=[
            jax.ShapeDtypeStruct((length, width), LOW),
            jax.ShapeDtypeStruct((width, 2 * inner), LOW),
            jax.ShapeDtypeStruct((width, 2 * inner), LOW),
        ],
        input_output_aliases={4: 2},
        compiler_params=params(),
        cost_estimate=cost(12 * length * width * inner, 8 * length * width),
        name="enter_back",
    )(table, proj_grad, normed, whole, held)


def exit_kernel(table, pulled, far, own, other, middle_grad, vectors, result, sums):
    step = pl.program_id(0)

    @pl.when(step == 0)
    def _():
        sums[...] = jnp.zeros_like(sums)

    mine = step >= pl.num_programs(0) // 2
    tokens = jnp.where(mine, own[...], other[...])
    pull = pulled[...].astype(WIDE) + far[...].astype(WIDE)
    hat, rate = hat_of(tokens)
    sums[0:1, :] += jnp.sum(pull * hat, axis=0, keepdims=True)
    sums[1:2, :] += jnp.sum(pull, axis=0, keepdims=True)
    result[...] = middle_grad[...] + norm_back(pull, hat, rate, vectors[0:1, :])


def leave_layer(table, pulled, far, own, other, middle_grad, vectors):
    length, width = pulled.shape
    steps = length // ROWS
    part = steps // 2
    pair = pl.BlockSpec((ROWS, width), lambda i, *_: (i % part, 0))

    def turned(i, places):
        return ((i + part * (1 - places[2 * BLOCKS])) % steps, 0)

    row = pl.BlockSpec((ROWS, width), turned)
    return pl.pallas_call(
        exit_kernel,
        grid_spec=pltpu.PrefetchScalarGridSpec(
            num_scalar_prefetch=1,
            grid=(steps,),
            in_specs=[row, row, pair, pair, row, fixed((8, width))],
            out_specs=[
                pl.BlockSpec((ROWS, width), lambda i, *_: (jnp.maximum(i - part, 0), 0)),
                kept((8, width)),
            ],
        ),
        out_shape=[
            jax.ShapeDtypeStruct((length // 2, width), WIDE),
            jax.ShapeDtypeStruct((8, width), WIDE),
        ],
        compiler_params=params(),
        cost_estimate=cost(20 * length * width, 18 * length * width),
        name="leave_layer",
    )(table, pulled, far, own, other, middle_grad, vectors)


def swap_cores(values):
    return lax.ppermute(values, "tensor", [(0, 1), (1, 0)])


def hop(values, bits, size):
    return lax.ppermute(values, "fsdp", [(i, i ^ bits) for i in range(size)])


def block_places(size, me, core):
    spots = jnp.arange(BLOCKS, dtype=jnp.int32)
    if size != BLOCKS:
        return jnp.concatenate([spots, spots, core[None]])
    away = me ^ spots
    low, mid, high = away & 1, (away >> 1) & 1, away >> 2
    return jnp.concatenate(
        [(low * 2 + mid) * 4 + high, (mid * 2 + low) * 4 + high, core[None]]
    )


def gather_rows(left, right, size):
    if size != BLOCKS:
        return tuple(lax.all_gather(v, "fsdp", axis=0, tiled=True) for v in (left, right))

    def far(values):
        parts = [values] + [hop(values, 4 * k, size) for k in range(1, 4)]
        return jnp.concatenate(parts, axis=0)

    left, right = far(left), far(right)
    for one, two in ((2, 1), (1, 2)):
        left, right = (
            jnp.concatenate([left, hop(left, one, size)], axis=0),
            jnp.concatenate([right, hop(right, two, size)], axis=0),
        )
    return left, right


def scatter_rows(left, right, size):
    if size != BLOCKS:
        return tuple(
            lax.psum_scatter(v.astype(WIDE), "fsdp", scatter_dimension=0, tiled=True)
            for v in (left, right)
        )

    def fold(values, bits):
        half = values.shape[0] // 2
        other = hop(values[half:], bits, size)
        return (values[:half].astype(WIDE) + other.astype(WIDE)).astype(LOW)

    for one, two in ((1, 2), (2, 1)):
        left, right = fold(left, one), fold(right, two)

    def near(values):
        rows = values.shape[0] // 4
        total = values[:rows].astype(WIDE)
        for k in range(1, 4):
            total = total + hop(values[k * rows : (k + 1) * rows], 4 * k, size).astype(WIDE)
        return total

    return near(left), near(right)


def sum_all(values, size):
    if size != BLOCKS:
        return lax.psum(values, "fsdp")
    for k in range(4):
        values = values + hop(values, 1 << k, size)
    return values


def body(
    size,
    inputs,
    segment_ids,
    qkv_weight,
    out_weight,
    up_weight,
    down_weight,
    gain_one,
    shift_one,
    gain_two,
    shift_two,
    cotangent,
):
    me = lax.axis_index("fsdp")
    core = lax.axis_index("tensor")
    rows, width = qkv_weight.shape[1:]
    half = inputs.shape[0]
    length = 2 * half
    table = block_places(size, me, core)

    first = jnp.concatenate(
        [
            qkv_weight.transpose(1, 0, 2).reshape(rows, 3 * width),
            jnp.stack([gain_one, shift_one, gain_two, shift_two], axis=1),
            jnp.zeros((rows, LANES - 4), WIDE),
        ],
        axis=1,
    ).astype(LOW)
    cut = (3 * width + LANES) // 2
    qkv_a, qkv_b = gather_rows(first[:, :cut], first[:, cut:], size)
    up_out, down = gather_rows(
        jnp.concatenate([up_weight, out_weight.T], axis=1).astype(LOW),
        down_weight.T.astype(LOW),
        size,
    )
    other = swap_cores(inputs)
    grad_other = swap_cores(cotangent)
    seg_col = jnp.broadcast_to(segment_ids[:, None], (length, LANES))
    seg_row = jnp.broadcast_to(segment_ids[None, :], (8, length))

    normed_one, proj, qkv_whole, vectors = enter(table, inputs, other, qkv_a, qkv_b)
    att, lse = attend(proj, seg_col, seg_row)
    part, out_whole = leave(table, att, up_out)
    middle, normed_two = second_norm(table, inputs, other, part, swap_cores(part), vectors)
    branch, pulled, up_part, down_part = feed(
        table, normed_two, cotangent, grad_other, up_out, down
    )
    up_grad, down_grad = scatter_rows(up_part, down_part, size)

    def own_half(values):
        return lax.dynamic_slice_in_dim(values, core * half, half, 0)

    far = swap_cores(lax.dynamic_slice_in_dim(branch, (1 - core) * half, half, 0))
    outputs = own_half(middle) + (own_half(branch).astype(WIDE) + far.astype(WIDE))

    middle_grad, att_grad, held, sums_two = middle_back(
        table, pulled, swap_cores(pulled), middle, cotangent, grad_other, vectors, out_whole, att
    )
    proj_grad = attend_back(proj, att, att_grad, lse, seg_col, seg_row)
    pulled, left, right = enter_back(table, proj_grad, normed_one, qkv_whole, held)
    tail_a, tail_b = scatter_rows(left, right, size)
    input_grad, sums_one = leave_layer(
        table, pulled, swap_cores(pulled), inputs, other, middle_grad, vectors
    )
    sums = sum_all(jnp.concatenate([sums_one[:2], sums_two[:2]], axis=0), size)
    sums = lax.dynamic_slice_in_dim(sums, me * rows, rows, 1)
    qkv_grad = jnp.stack([tail_a[:, :width], tail_a[:, width:], tail_b[:, :width]], axis=0)
    return (
        outputs,
        input_grad,
        qkv_grad,
        tail_b[:, width:].T,
        up_grad,
        down_grad.T,
        sums[0],
        sums[1],
        sums[2],
        sums[3],
    )


def solution(mesh):
    tokens = P(("fsdp", "tensor"), None)
    split = P("fsdp")
    weights = (
        P(None, "fsdp", "tensor"),
        P("tensor", "fsdp"),
        P("fsdp", "tensor"),
        P("tensor", "fsdp"),
        split,
        split,
        split,
        split,
    )
    return jax.shard_map(
        functools.partial(body, mesh.shape["fsdp"]),
        mesh=mesh,
        in_specs=(tokens, split) + weights + (tokens,),
        out_specs=(tokens, tokens) + weights,
        check_vma=False,
    )
```

```python
import functools
import math

import jax
import jax.numpy as jnp
from jax import lax
from jax.experimental import pallas as pl
from jax.experimental.pallas import tpu as pltpu
from jax.sharding import PartitionSpec as P

HD = 64
EPS = 1e-05
LOW = jnp.bfloat16
WIDE = jnp.float32
BLOCKS = 16
ROWS = 256
LANES = 128
LOG2E = math.log2(math.e)
LEFT, RIGHT, DOWN_LEFT, DOWN_RIGHT = (BLOCKS * k for k in range(4))
MASKED = -1e30


def nn(a, b):
    return jnp.dot(a, b, preferred_element_type=WIDE)


def nt(a, b):
    return lax.dot_general(a, b, (((1,), (1,)), ((), ())), preferred_element_type=WIDE)


def tn(a, b):
    return lax.dot_general(a, b, (((0,), (0,)), ((), ())), preferred_element_type=WIDE)


LONG = pl.CostEstimate(flops=10**13, bytes_accessed=10**9, transcendentals=0)


def params():
    return pltpu.CompilerParams(
        dimension_semantics=("arbitrary",), vmem_limit_bytes=60 * 1024 * 1024
    )


def fixed(shape, index=None):
    place = index or (0,) * len(shape)
    return pl.BlockSpec(shape, lambda i, *_: place, pipeline_mode=pl.Buffered(1))


def kept(shape, index=None):
    place = index or (0,) * len(shape)
    return pl.BlockSpec(shape, lambda i, *_: place)


def by_row(width, rows=ROWS):
    return pl.BlockSpec((rows, width), lambda i, *_: (i, 0))


def hat_of(values):
    centre = values - jnp.mean(values, axis=-1, keepdims=True)
    rate = lax.rsqrt(jnp.mean(centre * centre, axis=-1, keepdims=True) + EPS)
    return centre * rate, rate


def norm_back(grad, hat, rate, gain):
    scaled = grad * gain
    return rate * (
        scaled
        - jnp.mean(scaled, axis=-1, keepdims=True)
        - hat * jnp.mean(scaled * hat, axis=-1, keepdims=True)
    )


def take(table, entry, rows, near, far, lanes=slice(None)):
    place = table[entry]
    at = pl.ds(pl.multiple_of((place % (BLOCKS // 2)) * rows, 16), rows)
    return jnp.where(place < BLOCKS // 2, near[at, lanes], far[at, lanes])


def put(table, entry, rows, keep, send, values):
    place = table[entry]
    at = pl.ds(pl.multiple_of((place % (BLOCKS // 2)) * rows, 16), rows)

    @pl.when(place < BLOCKS // 2)
    def _():
        keep[at, :] = values

    @pl.when(place >= BLOCKS // 2)
    def _():
        send[at, :] = values


def enter_kernel(table, tokens, wa, wa2, wb, wb2, normed, proj, whole, vectors, loose):
    step = pl.program_id(0)
    rows = wa.shape[0] // (BLOCKS // 2)
    cut = wa.shape[1]
    rest = whole.shape[1] - cut

    @pl.when(step == 0)
    def _():
        for j in range(BLOCKS):
            to = slice(j * rows, (j + 1) * rows)
            whole[to, :cut] = take(table, LEFT + j, rows, wa, wa2)
            late = take(table, RIGHT + j, rows, wb, wb2)
            whole[to, cut:] = late[:, :rest]
            loose[to, :] = late[:, rest:].astype(WIDE)
        vectors[...] = loose[...].T[:8]

    hat, _ = hat_of(tokens[...])
    low = (hat * vectors[0:1, :] + vectors[1:2, :]).astype(LOW)
    normed[...] = low
    proj[...] = nn(low, whole[...]).astype(LOW)


def enter(table, tokens, *pieces):
    length, width = tokens.shape
    total = pieces[0].shape[1] + pieces[2].shape[1] - LANES
    return pl.pallas_call(
        enter_kernel,
        grid_spec=pltpu.PrefetchScalarGridSpec(
            num_scalar_prefetch=1,
            grid=(length // ROWS,),
            in_specs=[by_row(width)] + [fixed(piece.shape) for piece in pieces],
            out_specs=[by_row(width), by_row(total), kept((width, total)), kept((8, width))],
            scratch_shapes=[pltpu.VMEM((width, LANES), WIDE)],
        ),
        out_shape=[
            jax.ShapeDtypeStruct((length, width), LOW),
            jax.ShapeDtypeStruct((length, total), LOW),
            jax.ShapeDtypeStruct((width, total), LOW),
            jax.ShapeDtypeStruct((8, width), WIDE),
        ],
        compiler_params=params(),
        cost_estimate=LONG,
        name="enter",
    )(table, tokens, *pieces)


def build_bias(bias, seg_col, seg_row):
    length = bias.shape[0]
    for start in range(0, length, ROWS):
        lanes = slice(start, start + ROWS)
        until = start + ROWS
        shape = (until, ROWS)
        key_at = lax.broadcasted_iota(jnp.int32, shape, 0)
        query_at = lax.broadcasted_iota(jnp.int32, shape, 1) + start
        same = jnp.broadcast_to(seg_col[:until, 0:1], shape) == jnp.broadcast_to(
            seg_row[0:1, lanes], shape
        )
        bias[:until, lanes] = jnp.where((key_at <= query_at) & same, 0.0, MASKED)


def one_head(flipped, head):
    empty = jnp.zeros((HD, flipped.shape[1]), flipped.dtype)
    if head == 0:
        return jnp.concatenate([flipped[:HD], empty], axis=0)
    return jnp.concatenate([empty, flipped[HD:]], axis=0)


def attend_kernel(queries, keys, values, seg_col, seg_row, out, lse, bias):
    @pl.when(pl.program_id(0) == 0)
    def _():
        build_bias(bias, seg_col, seg_row)

    length = queries.shape[0]
    q_flip = queries[...].T
    v_flip = values[...].T
    sides = [one_head(q_flip, head) for head in range(2)]
    for start in range(0, length, ROWS):
        lanes = slice(start, start + ROWS)
        until = start + ROWS
        pieces = []
        for head in range(2):
            scores = nn(keys[:until], sides[head][:, lanes]) * (HD**-0.5 * LOG2E)
            scores = scores + bias[:until, lanes]
            top = jnp.max(scores, axis=0, keepdims=True)
            expo = jnp.exp2(scores - top)
            total = jnp.sum(expo, axis=0, keepdims=True)
            flat = nn(v_flip[head * HD : (head + 1) * HD, :until], expo.astype(LOW))
            pieces.append(flat / total)
            lse[head : head + 1, lanes] = top + jnp.log(total) * LOG2E
        out[lanes, :] = jnp.concatenate(pieces, axis=0).T.astype(LOW)


def attend(proj, seg_col, seg_row):
    length = proj.shape[0]
    pairs = proj.shape[1] // (3 * LANES)

    def part(k):
        return pl.BlockSpec((length, LANES), lambda i: (0, k * pairs + i))

    return pl.pallas_call(
        attend_kernel,
        grid=(pairs,),
        in_specs=[part(0), part(1), part(2), fixed(seg_col.shape), fixed(seg_row.shape)],
        out_specs=[
            pl.BlockSpec((length, LANES), lambda i: (0, i)),
            pl.BlockSpec((8, length), lambda i: (i, 0)),
        ],
        out_shape=[
            jax.ShapeDtypeStruct((length, pairs * LANES), LOW),
            jax.ShapeDtypeStruct((8 * pairs, length), WIDE),
        ],
        scratch_shapes=[pltpu.VMEM((length, length), WIDE)],
        compiler_params=params(),
        cost_estimate=LONG,
        name="attend",
    )(proj, proj, proj, seg_col, seg_row)


def attend_back_kernel(
    queries, keys, values, out, grad, lse, seg_col, seg_row, result, bias, k_sum, v_sum
):
    @pl.when(pl.program_id(0) == 0)
    def _():
        build_bias(bias, seg_col, seg_row)

    length = queries.shape[0]
    scale = HD**-0.5
    q_flip = queries[...].T
    k_flip = keys[...].T
    g_flip = grad[...].T
    product = out[...].T.astype(WIDE) * g_flip.astype(WIDE)
    k_sum[...] = jnp.zeros_like(k_sum)
    v_sum[...] = jnp.zeros_like(v_sum)
    q_sides = [one_head(q_flip, head) for head in range(2)]
    g_sides = [one_head(g_flip, head) for head in range(2)]
    for start in range(0, length, ROWS):
        lanes = slice(start, start + ROWS)
        until = start + ROWS
        pieces = []
        for head in range(2):
            scores = nn(keys[:until], q_sides[head][:, lanes]) * (scale * LOG2E)
            probs = jnp.exp2(scores + bias[:until, lanes] - lse[head : head + 1, lanes])
            v_sum[head, :until] += nn(probs.astype(LOW), grad[lanes, :])
            centre = jnp.sum(
                product[head * HD : (head + 1) * HD, lanes], axis=0, keepdims=True
            )
            pull = nn(values[:until], g_sides[head][:, lanes])
            pull = (probs * (pull - centre)).astype(LOW)
            k_sum[head, :until] += nn(pull, queries[lanes, :])
            pieces.append(nn(k_flip[head * HD : (head + 1) * HD, :until], pull))
        result[0, lanes, :] = (jnp.concatenate(pieces, axis=0) * scale).T.astype(LOW)
    first = lax.broadcasted_iota(jnp.int32, (length, LANES), 1) < HD
    result[1] = (jnp.where(first, k_sum[0], k_sum[1]) * scale).astype(LOW)
    result[2] = jnp.where(first, v_sum[0], v_sum[1]).astype(LOW)


def attend_back(proj, out, grad, lse, seg_col, seg_row):
    length = proj.shape[0]
    pairs = proj.shape[1] // (3 * LANES)

    def part(k):
        return pl.BlockSpec((length, LANES), lambda i: (0, k * pairs + i))

    return pl.pallas_call(
        attend_back_kernel,
        grid=(pairs,),
        in_specs=[
            part(0),
            part(1),
            part(2),
            part(0),
            part(0),
            pl.BlockSpec((8, length), lambda i: (i, 0)),
            fixed(seg_col.shape),
            fixed(seg_row.shape),
        ],
        out_specs=pl.BlockSpec((3, length, LANES), lambda i: (0, 0, i)),
        out_shape=jax.ShapeDtypeStruct((3, length, pairs * LANES), LOW),
        scratch_shapes=[
            pltpu.VMEM((length, length), WIDE),
            pltpu.VMEM((2, length, LANES), WIDE),
            pltpu.VMEM((2, length, LANES), WIDE),
        ],
        compiler_params=params(),
        cost_estimate=LONG,
        name="attend_back",
    )(proj, proj, proj, out, grad, lse, seg_col, seg_row)


def leave_kernel(table, att, near, far, part, whole):
    rows = near.shape[0] // (BLOCKS // 2)
    lanes = slice(near.shape[1] - whole.shape[1], None)

    @pl.when(pl.program_id(0) == 0)
    def _():
        for j in range(BLOCKS):
            whole[j * rows : (j + 1) * rows, :] = take(
                table, BLOCKS + j, rows, near, far, lanes
            )

    part[...] = nt(att[...], whole[...]).astype(LOW)


def leave(table, att, near, far):
    length, inner = att.shape
    width = near.shape[0] * 2
    return pl.pallas_call(
        leave_kernel,
        grid_spec=pltpu.PrefetchScalarGridSpec(
            num_scalar_prefetch=1,
            grid=(length // ROWS,),
            in_specs=[by_row(inner), fixed(near.shape), fixed(far.shape)],
            out_specs=[by_row(width), kept((width, inner))],
        ),
        out_shape=[
            jax.ShapeDtypeStruct((length, width), LOW),
            jax.ShapeDtypeStruct((width, inner), LOW),
        ],
        compiler_params=params(),
        cost_estimate=LONG,
        name="leave",
    )(table, att, near, far)


def middle_kernel(tokens, part, far, vectors, middle, normed):
    values = tokens[...] + (part[...].astype(WIDE) + far[...].astype(WIDE))
    middle[...] = values
    hat, _ = hat_of(values)
    normed[...] = (hat * vectors[2:3, :] + vectors[3:4, :]).astype(LOW)


def second_norm(tokens, part, far, vectors):
    length, width = part.shape
    return pl.pallas_call(
        middle_kernel,
        grid=(length // ROWS,),
        in_specs=[by_row(width), by_row(width), by_row(width), fixed((8, width))],
        out_specs=[by_row(width), by_row(width)],
        out_shape=[
            jax.ShapeDtypeStruct((length, width), WIDE),
            jax.ShapeDtypeStruct((length, width), LOW),
        ],
        compiler_params=params(),
        cost_estimate=LONG,
        name="second_norm",
    )(tokens, part, far, vectors)


SIDE = 256


def feed_kernel(
    table,
    normed,
    grad,
    up_a,
    up_a2,
    up_b,
    up_b2,
    down_a,
    down_a2,
    down_b,
    down_b2,
    branch,
    pulled,
    up_keep,
    up_send,
    down_keep,
    down_send,
    normed_flip,
    grad_flip,
    up_whole,
    down_whole,
    act,
    pre,
    branch_sum,
    pulled_sum,
):
    step = pl.program_id(0)
    length = normed.shape[0]
    rows = up_a.shape[0] // (BLOCKS // 2)

    @pl.when(step == 0)
    def _():
        normed_flip[...] = normed[...].T
        grad_flip[...] = grad[...].T
        branch_sum[...] = jnp.zeros_like(branch_sum)
        pulled_sum[...] = jnp.zeros_like(pulled_sum)
        up_cut = up_a.shape[1] // SIDE
        down_cut = down_a.shape[1] // SIDE
        for k in range(up_whole.shape[0]):
            for j in range(BLOCKS):
                to = slice(j * rows, (j + 1) * rows)
                pair, spot = ((up_a, up_a2), k) if k < up_cut else ((up_b, up_b2), k - up_cut)
                lanes = slice(spot * SIDE, (spot + 1) * SIDE)
                up_whole[k, to, :] = take(
                    table, (RIGHT if k >= up_cut else LEFT) + j, rows, *pair, lanes
                )
                pair, spot = (
                    ((down_a, down_a2), k) if k < down_cut else ((down_b, down_b2), k - down_cut)
                )
                lanes = slice(spot * SIDE, (spot + 1) * SIDE)
                down_whole[k, to, :] = take(
                    table, (DOWN_RIGHT if k >= down_cut else DOWN_LEFT) + j, rows, *pair, lanes
                )

    for start in range(0, length, ROWS):
        at = slice(start, start + ROWS)
        wide = nn(normed[at, :], up_whole[step])
        square = wide * wide
        root = math.sqrt(2.0 / math.pi)
        bend = jnp.tanh(wide * (root + root * 0.044715 * square))
        share = 0.5 + 0.5 * bend
        slope = share + 0.5 * wide * (1.0 - bend * bend) * (
            root + 3.0 * root * 0.044715 * square
        )
        act[at, :] = (wide * share).astype(LOW)
        pre[at, :] = (nn(grad[at, :], down_whole[step]) * slope).astype(LOW)
        branch_sum[at, :] += nt(act[at, :], down_whole[step])
        pulled_sum[at, :] += nt(pre[at, :], up_whole[step])

    lifted = nn(normed_flip[...], pre[...]).astype(LOW)
    lowered = nn(grad_flip[...], act[...]).astype(LOW)
    for j in range(BLOCKS):
        block = slice(j * rows, (j + 1) * rows)
        put(table, LEFT + j, rows, up_keep, up_send, lifted[block])
        put(table, RIGHT + j, rows, down_keep, down_send, lowered[block])

    @pl.when(step == pl.num_programs(0) - 1)
    def _():
        branch[...] = branch_sum[...].astype(LOW)
        pulled[...] = pulled_sum[...].astype(LOW)


def feed(table, normed, grad, *pieces):
    length, width = normed.shape
    hidden = pieces[4].shape[1] + pieces[6].shape[1]
    column = pl.BlockSpec((width // 2, SIDE), lambda i, *_: (0, i))
    token = (length, width)
    steps = hidden // SIDE
    return pl.pallas_call(
        feed_kernel,
        grid_spec=pltpu.PrefetchScalarGridSpec(
            num_scalar_prefetch=1,
            grid=(steps,),
            in_specs=[fixed(token), fixed(token)] + [fixed(piece.shape) for piece in pieces],
            out_specs=[kept(token), kept(token), column, column, column, column],
            scratch_shapes=[
                pltpu.VMEM((width, length), LOW),
                pltpu.VMEM((width, length), LOW),
                pltpu.VMEM((steps, width, SIDE), LOW),
                pltpu.VMEM((steps, width, SIDE), LOW),
                pltpu.VMEM((length, SIDE), LOW),
                pltpu.VMEM((length, SIDE), LOW),
                pltpu.VMEM(token, WIDE),
                pltpu.VMEM(token, WIDE),
            ],
        ),
        out_shape=[jax.ShapeDtypeStruct(token, LOW)] * 2
        + [jax.ShapeDtypeStruct((width // 2, hidden), LOW)] * 4,
        compiler_params=params(),
        cost_estimate=LONG,
        name="feed",
    )(table, normed, grad, *pieces)


def middle_back_kernel(
    table,
    pulled,
    far,
    middle,
    grad,
    vectors,
    out_whole,
    att,
    middle_grad,
    att_grad,
    out_keep,
    out_send,
    sums,
    out_sum,
):
    step = pl.program_id(0)
    rows = out_whole.shape[0] // BLOCKS

    @pl.when(step == 0)
    def _():
        out_sum[...] = jnp.zeros_like(out_sum)
        sums[...] = jnp.zeros_like(sums)

    pull = pulled[...].astype(WIDE) + far[...].astype(WIDE)
    hat, rate = hat_of(middle[...])
    whole = grad[...].astype(WIDE) + norm_back(pull, hat, rate, vectors[2:3, :])
    middle_grad[...] = whole
    sums[0:1, :] += jnp.sum(pull * hat, axis=0, keepdims=True)
    sums[1:2, :] += jnp.sum(pull, axis=0, keepdims=True)
    low = whole.astype(LOW)
    att_grad[...] = nn(low, out_whole[...]).astype(LOW)
    out_sum[...] += tn(low, att[...])

    @pl.when(step == pl.num_programs(0) - 1)
    def _():
        for j in range(BLOCKS):
            block = out_sum[j * rows : (j + 1) * rows, :].astype(LOW)
            put(table, RIGHT + j, rows, out_keep, out_send, block)


def middle_back(table, pulled, far, middle, grad, vectors, out_whole, att):
    length, width = middle.shape
    inner = att.shape[1]
    return pl.pallas_call(
        middle_back_kernel,
        grid_spec=pltpu.PrefetchScalarGridSpec(
            num_scalar_prefetch=1,
            grid=(length // ROWS,),
            in_specs=[
                by_row(width),
                by_row(width),
                by_row(width),
                by_row(width),
                fixed((8, width)),
                fixed((width, inner)),
                by_row(inner),
            ],
            out_specs=[
                by_row(width),
                by_row(inner),
                kept((width // 2, inner), (0, 1)),
                kept((width // 2, inner), (0, 1)),
                kept((8, width)),
            ],
            scratch_shapes=[pltpu.VMEM((width, inner), WIDE)],
        ),
        out_shape=[
            jax.ShapeDtypeStruct((length, width), WIDE),
            jax.ShapeDtypeStruct((length, inner), LOW),
            jax.ShapeDtypeStruct((width // 2, 2 * inner), LOW),
            jax.ShapeDtypeStruct((width // 2, 2 * inner), LOW),
            jax.ShapeDtypeStruct((8, width), WIDE),
        ],
        compiler_params=params(),
        cost_estimate=LONG,
        name="middle_back",
    )(table, pulled, far, middle, grad, vectors, out_whole, att)


def weight_back_kernel(
    table,
    proj_grad,
    normed,
    held_keep,
    held_send,
    left_keep,
    left_send,
    right_keep,
    right_send,
    normed_flip,
):
    step = pl.program_id(0)
    rows = normed.shape[1] // BLOCKS

    @pl.when(step == 0)
    def _():
        normed_flip[...] = normed[...].T

    weight = nn(normed_flip[...], proj_grad[0]).astype(LOW)

    @pl.when(step < 2)
    def _():
        for j in range(BLOCKS):
            put(table, LEFT + j, rows, left_keep, left_send, weight[j * rows : (j + 1) * rows])

    @pl.when(step == 2)
    def _():
        for j in range(BLOCKS):
            block = weight[j * rows : (j + 1) * rows]
            put(table, RIGHT + j, rows, right_keep, right_send, block)


def weight_back(table, proj_grad, normed, held_keep, held_send):
    length, width = normed.shape
    inner = proj_grad.shape[2]
    early = pl.BlockSpec((width // 2, inner), lambda i, *_: (0, jnp.minimum(i, 1)))
    late = kept((width // 2, inner))
    return pl.pallas_call(
        weight_back_kernel,
        grid_spec=pltpu.PrefetchScalarGridSpec(
            num_scalar_prefetch=1,
            grid=(3,),
            in_specs=[
                pl.BlockSpec((1, length, inner), lambda i, *_: (i, 0, 0)),
                fixed((length, width)),
                pl.BlockSpec(memory_space=pl.ANY),
                pl.BlockSpec(memory_space=pl.ANY),
            ],
            out_specs=[early, early, late, late],
            scratch_shapes=[pltpu.VMEM((width, length), LOW)],
        ),
        out_shape=[jax.ShapeDtypeStruct((width // 2, 2 * inner), LOW)] * 4,
        input_output_aliases={3: 2, 4: 3},
        compiler_params=params(),
        cost_estimate=LONG,
        name="weight_back",
    )(table, proj_grad, normed, held_keep, held_send)


def token_back_kernel(proj_grad, whole, pulled):
    inner = proj_grad.shape[2]
    total = nt(proj_grad[0], whole[:, :inner])
    for c in range(1, 3):
        total += nt(proj_grad[c], whole[:, c * inner : (c + 1) * inner])
    pulled[...] = total.astype(LOW)


def token_back(proj_grad, whole):
    length, inner = proj_grad.shape[1:]
    width = whole.shape[0]
    return pl.pallas_call(
        token_back_kernel,
        grid=(length // ROWS,),
        in_specs=[
            pl.BlockSpec((3, ROWS, inner), lambda i: (0, i, 0)),
            fixed(whole.shape),
        ],
        out_specs=by_row(width),
        out_shape=jax.ShapeDtypeStruct((length, width), LOW),
        compiler_params=params(),
        cost_estimate=LONG,
        name="token_back",
    )(proj_grad, whole)


def exit_kernel(core, pulled, far, tokens, middle_grad, vectors, result, sums):
    step = pl.program_id(0)

    @pl.when(step == 0)
    def _():
        sums[...] = jnp.zeros_like(sums)

    pull = pulled[...].astype(WIDE) + far[...].astype(WIDE)
    hat, rate = hat_of(tokens[...])
    sums[0:1, :] += jnp.sum(pull * hat, axis=0, keepdims=True)
    sums[1:2, :] += jnp.sum(pull, axis=0, keepdims=True)
    result[...] = middle_grad[...] + norm_back(pull, hat, rate, vectors[0:1, :])


def leave_layer(core, pulled, far, tokens, middle_grad, vectors):
    length, width = pulled.shape
    steps = length // ROWS
    part = steps // 2

    def turned(i, place):
        return ((i + part * (1 - place[0])) % steps, 0)

    row = pl.BlockSpec((ROWS, width), turned)
    return pl.pallas_call(
        exit_kernel,
        grid_spec=pltpu.PrefetchScalarGridSpec(
            num_scalar_prefetch=1,
            grid=(steps,),
            in_specs=[row, row, row, row, fixed((8, width))],
            out_specs=[
                pl.BlockSpec((ROWS, width), lambda i, *_: (jnp.maximum(i - part, 0), 0)),
                kept((8, width)),
            ],
        ),
        out_shape=[
            jax.ShapeDtypeStruct((length // 2, width), WIDE),
            jax.ShapeDtypeStruct((8, width), WIDE),
        ],
        compiler_params=params(),
        cost_estimate=LONG,
        name="leave_layer",
    )(core, pulled, far, tokens, middle_grad, vectors)


def swap_cores(values):
    return lax.ppermute(values, "tensor", [(0, 1), (1, 0)])


def hop(values, bits, size):
    return lax.ppermute(values, "fsdp", [(i, i ^ bits) for i in range(size)])


def block_places(size, me):
    spots = jnp.arange(BLOCKS, dtype=jnp.int32)
    if size != BLOCKS:
        return jnp.concatenate([spots] * 4)
    away = me ^ spots
    low, mid, high = away & 1, (away >> 1) & 1, away >> 2
    return jnp.concatenate(
        [
            low * 8 + mid * 4 + high,
            mid * 8 + low * 4 + high,
            mid * 8 + high * 2 + low,
            low * 8 + high * 2 + mid,
        ]
    )


def vmem_call(kernel, shapes, args, name):
    return pl.pallas_call(
        kernel,
        out_shape=shapes,
        compiler_params=pltpu.CompilerParams(vmem_limit_bytes=60 * 1024 * 1024),
        cost_estimate=LONG,
        name=name,
    )(*args)


def collect(pieces, cut):
    rows, width = pieces[0].shape

    def kernel(*refs):
        left, right = refs[len(pieces) :]
        for k, piece in enumerate(refs[: len(pieces)]):
            at = slice(k * rows, (k + 1) * rows)
            left[at, :] = piece[:, :cut]
            right[at, :] = piece[:, cut:]

    total = rows * len(pieces)
    return vmem_call(
        kernel,
        [jax.ShapeDtypeStruct((total, cut), LOW), jax.ShapeDtypeStruct((total, width - cut), LOW)],
        pieces,
        "collect",
    )


def join(left, left_far, right, right_far, size):
    if size != BLOCKS:
        return jnp.concatenate([left, left_far], 0), jnp.concatenate([right, right_far], 0)

    def kernel(one, one_far, two, two_far, one_out, two_out):
        rows = one.shape[0]
        one_out[:rows, :] = one[...]
        one_out[rows:, :] = one_far[...]
        two_out[:rows, :] = two[...]
        two_out[rows:, :] = two_far[...]

    shapes = [jax.ShapeDtypeStruct((2 * v.shape[0], v.shape[1]), LOW) for v in (left, right)]
    return vmem_call(kernel, shapes, (left, left_far, right, right_far), "join")


def far_rows(values, size):
    if size != BLOCKS:
        whole = lax.all_gather(values, "fsdp", axis=0, tiled=True)
        rows = whole.shape[0] // 4
        return [whole[k * rows : (k + 1) * rows] for k in range(4)]
    return [values] + [hop(values, 4 * k, size) for k in range(1, 4)]


def after(values, *done):
    return lax.optimization_barrier((values, done))[0]


def halves(whole):
    half = whole.shape[0] // 2
    return whole[:half], whole[half:]


def down_stage(left, right, size):
    if size != BLOCKS:
        return left, None, right, None
    return left, hop(left, 1, size), right, hop(right, 2, size)


def beside(left, left_far, right, right_far, size):
    if size != BLOCKS:
        return jnp.concatenate([left, right], axis=1)
    rows, cut = left.shape

    def kernel(one, one_far, two, two_far, out):
        out[:rows, :cut] = one[...]
        out[rows:, :cut] = one_far[...]
        out[:rows, cut:] = two[...]
        out[rows:, cut:] = two_far[...]

    shape = jax.ShapeDtypeStruct((2 * rows, 2 * cut), LOW)
    return vmem_call(kernel, [shape], (left, left_far, right, right_far), "beside")[0]


def in_order(own, core):
    other = swap_cores(own)
    return jnp.where(
        core == 0,
        jnp.concatenate([own, other], axis=0),
        jnp.concatenate([other, own], axis=0),
    )


def second_stage(left, right, size):
    if size != BLOCKS:
        return halves(left) + halves(right)
    return left, hop(left, 2, size), right, hop(right, 1, size)


def third_stage(left, right, size):
    if size != BLOCKS:
        return halves(left) + halves(right)
    return left, hop(left, 1, size), right, hop(right, 2, size)


def fold_half(left, left_far, right, right_far, size):
    if size != BLOCKS:
        return left, left_far, right, right_far

    def kernel(one, one_far, two, two_far, one_low, one_high, two_low, two_high):
        rows = one_low.shape[0]
        for a, b, low, high in (
            (one, one_far, one_low, one_high),
            (two, two_far, two_low, two_high),
        ):
            low[...] = (a[:rows, :].astype(WIDE) + b[:rows, :].astype(WIDE)).astype(LOW)
            high[...] = (a[rows:, :].astype(WIDE) + b[rows:, :].astype(WIDE)).astype(LOW)

    shapes = [
        jax.ShapeDtypeStruct((v.shape[0] // 2, v.shape[1]), LOW)
        for v in (left, left, right, right)
    ]
    return vmem_call(kernel, shapes, (left, left_far, right, right_far), "fold_half")


def fold_quarter(left, left_far, right, right_far, size):
    if size != BLOCKS:
        whole = jnp.concatenate(
            [jnp.concatenate([left, left_far], 0), jnp.concatenate([right, right_far], 0)], 1
        )
        return halves(whole)

    cut = left.shape[1]
    rows = left.shape[0] // 4

    def kernel(one, one_far, two, two_far, *outs):
        for k, out in enumerate(outs):
            at = slice(k * rows, (k + 1) * rows)
            out[:, :cut] = (one[at, :].astype(WIDE) + one_far[at, :].astype(WIDE)).astype(LOW)
            out[:, cut:] = (two[at, :].astype(WIDE) + two_far[at, :].astype(WIDE)).astype(LOW)

    shapes = [jax.ShapeDtypeStruct((rows, cut + right.shape[1]), LOW)] * 4
    return vmem_call(kernel, shapes, (left, left_far, right, right_far), "fold_quarter")


def first_send(left, left_send, right, right_send, size):
    if size != BLOCKS:
        return left, left_send, right, right_send
    return left, hop(left_send, 1, size), right, hop(right_send, 2, size)


def second_send(left, left_send, right, right_send, size):
    if size != BLOCKS:
        return left, left_send, right, right_send
    return left, hop(left_send, 2, size), right, hop(right_send, 1, size)


def third_send(parts, size):
    if size != BLOCKS:
        return parts
    return [parts[0]] + [hop(parts[k], 4 * k, size) for k in range(1, 4)]


def total_of(parts, size):
    if size != BLOCKS:
        whole = jnp.concatenate(parts, axis=0).astype(WIDE)
        return lax.psum_scatter(whole, "fsdp", scatter_dimension=0, tiled=True)
    total = parts[0].astype(WIDE)
    for part in parts[1:]:
        total = total + part.astype(WIDE)
    return total


def sum_all(values, size):
    if size != BLOCKS:
        return lax.psum(values, "fsdp")
    for k in range(4):
        values = values + hop(values, 1 << k, size)
    return values


def body(
    size,
    inputs,
    segment_ids,
    qkv_weight,
    out_weight,
    up_weight,
    down_weight,
    gain_one,
    shift_one,
    gain_two,
    shift_two,
    cotangent,
):
    me = lax.axis_index("fsdp")
    core = lax.axis_index("tensor")
    rows, width = qkv_weight.shape[1:]
    half = inputs.shape[0]
    length = 2 * half
    table = block_places(size, me)

    first = jnp.concatenate(
        [
            qkv_weight.transpose(1, 0, 2).reshape(rows, 3 * width),
            jnp.stack([gain_one, shift_one, gain_two, shift_two], axis=1),
            jnp.zeros((rows, LANES - 4), WIDE),
        ],
        axis=1,
    ).astype(LOW)
    second = jnp.concatenate([up_weight, out_weight.T], axis=1).astype(LOW)
    hidden = down_weight.shape[0]
    third = [v.T.astype(LOW) for v in (down_weight[: hidden // 2], down_weight[hidden // 2 :])]
    first = far_rows(first, size)
    third = down_stage(*third, size)
    tokens = in_order(inputs, core)
    qkv = collect(after(first, tokens), (3 * width + LANES) // 2)
    second = far_rows(after(second, qkv), size)
    third = beside(*third, size)
    qkv = join(*second_stage(*qkv, size), size)
    grad = in_order(cotangent, core)
    seg_col = jnp.broadcast_to(segment_ids[:, None], (length, LANES))
    seg_row = jnp.broadcast_to(segment_ids[None, :], (8, length))
    up_out = collect(after(second, qkv, grad, seg_col, seg_row), SIDE * (-(-second[0].shape[1] // (2 * SIDE))))
    third = far_rows(after(third, up_out), size)
    qkv = third_stage(*qkv, size)
    up_out = second_stage(*up_out, size)

    normed_one, proj, qkv_whole, vectors = enter(table, tokens, *qkv)
    up_out = join(*after(up_out, proj), size)
    proj = after(proj, up_out)
    up_out = third_stage(*up_out, size)
    att, lse = attend(proj, seg_col, seg_row)
    down = collect(after(third, att), hidden // 2)
    att = after(att, down, up_out)
    down = second_stage(*down, size)
    part, out_whole = leave(table, att, *up_out[2:])
    far = after(swap_cores(part), down)
    middle, normed_two = second_norm(tokens, part, far, vectors)
    branch, pulled, *parts = feed(table, normed_two, grad, *up_out, *down)
    parts = first_send(*parts, size)

    middle_grad, att_grad, *held, sums_two = middle_back(
        table, pulled, swap_cores(pulled), middle, grad, vectors, out_whole, att
    )
    proj_grad = attend_back(proj, att, att_grad, lse, seg_col, seg_row)
    parts = fold_half(*after(parts, proj_grad), size)
    proj_grad = after(proj_grad, parts)
    parts = second_send(*parts, size)
    tail = weight_back(table, proj_grad, normed_one, *held)
    parts = fold_quarter(*after(parts, tail), size)
    tail = first_send(*tail, size)
    proj_grad = after(proj_grad, parts)
    parts = third_send(parts, size)
    pulled = token_back(proj_grad, qkv_whole)
    tail = fold_half(*after(tail, pulled), size)
    far = after(swap_cores(pulled), tail)
    tail = second_send(*tail, size)
    input_grad, sums_one = leave_layer(
        core[None], pulled, far, tokens, middle_grad, vectors
    )
    tail = fold_quarter(*after(tail, input_grad), size)
    parts, branch, sums_one = after((parts, branch, sums_one), tail)
    tail = third_send(tail, size)

    def own_half(values):
        return lax.dynamic_slice_in_dim(values, core * half, half, 0)

    far = swap_cores(lax.dynamic_slice_in_dim(branch, (1 - core) * half, half, 0))
    outputs = own_half(middle) + (own_half(branch).astype(WIDE) + far.astype(WIDE))
    feed_grad = total_of(parts, size)
    sums = sum_all(jnp.concatenate([sums_one[:2], sums_two[:2]], axis=0), size)
    tail = total_of(tail, size)
    sums = lax.dynamic_slice_in_dim(sums, me * rows, rows, 1)
    qkv_grad = jnp.stack([tail[:, k * width : (k + 1) * width] for k in range(3)], axis=0)
    return (
        outputs,
        input_grad,
        qkv_grad,
        tail[:, 3 * width :].T,
        feed_grad[:, :hidden],
        feed_grad[:, hidden:].T,
        sums[0],
        sums[1],
        sums[2],
        sums[3],
    )


def solution(mesh):
    tokens = P(("fsdp", "tensor"), None)
    split = P("fsdp")
    weights = (
        P(None, "fsdp", "tensor"),
        P("tensor", "fsdp"),
        P("fsdp", "tensor"),
        P("tensor", "fsdp"),
        split,
        split,
        split,
        split,
    )
    return jax.shard_map(
        functools.partial(body, mesh.shape["fsdp"]),
        mesh=mesh,
        in_specs=(tokens, split) + weights + (tokens,),
        out_specs=(tokens, tokens) + weights,
        check_vma=False,
    )
```

```python
import functools
import math

import jax
import jax.numpy as jnp
from jax import lax
from jax.experimental import pallas as pl
from jax.experimental.pallas import tpu as pltpu
from jax.sharding import PartitionSpec as P

HD = 64
EPS = 1e-05
LOW = jnp.bfloat16
WIDE = jnp.float32
BLOCKS = 16
ROWS = 256
TILE = 32
LANES = 128
LOG2E = math.log2(math.e)
LEFT, RIGHT, DOWN_LEFT, DOWN_RIGHT = (BLOCKS * k for k in range(4))
MASKED = -1e30


def nn(a, b):
    return jnp.dot(a, b, preferred_element_type=WIDE)


def nt(a, b):
    return lax.dot_general(a, b, (((1,), (1,)), ((), ())), preferred_element_type=WIDE)


def tn(a, b):
    return lax.dot_general(a, b, (((0,), (0,)), ((), ())), preferred_element_type=WIDE)


LONG = pl.CostEstimate(flops=10**13, bytes_accessed=10**9, transcendentals=0)


def params():
    return pltpu.CompilerParams(
        dimension_semantics=("arbitrary",), vmem_limit_bytes=24 * 1024 * 1024
    )


def fixed(shape, index=None):
    place = index or (0,) * len(shape)
    return pl.BlockSpec(shape, lambda i, *_: place, pipeline_mode=pl.Buffered(1))


def kept(shape, index=None):
    place = index or (0,) * len(shape)
    return pl.BlockSpec(shape, lambda i, *_: place)


def by_row(width, rows=ROWS):
    return pl.BlockSpec((rows, width), lambda i, *_: (i, 0))


def hat_of(values):
    centre = values - jnp.mean(values, axis=-1, keepdims=True)
    rate = lax.rsqrt(jnp.mean(centre * centre, axis=-1, keepdims=True) + EPS)
    return centre * rate, rate


def tiles(rows):
    return [slice(start, start + TILE) for start in range(0, rows, TILE)]


def fold_rows(values):
    total = values[:8]
    for start in range(8, values.shape[0], 8):
        total = total + values[start : start + 8]
    return total


def norm_back(grad, hat, rate, gain):
    scaled = grad * gain
    return rate * (
        scaled
        - jnp.mean(scaled, axis=-1, keepdims=True)
        - hat * jnp.mean(scaled * hat, axis=-1, keepdims=True)
    )


def take(table, entry, rows, near, far, lanes=slice(None)):
    place = table[entry]
    at = pl.ds(pl.multiple_of((place % (BLOCKS // 2)) * rows, 16), rows)
    return jnp.where(place < BLOCKS // 2, near[at, lanes], far[at, lanes])


def put(table, entry, rows, keep, send, values):
    place = table[entry]
    at = pl.ds(pl.multiple_of((place % (BLOCKS // 2)) * rows, 16), rows)

    @pl.when(place < BLOCKS // 2)
    def _():
        keep[at, :] = values

    @pl.when(place >= BLOCKS // 2)
    def _():
        send[at, :] = values


def enter_kernel(table, tokens, wa, wa2, wb, wb2, flip, proj, whole, vectors, loose, normed):
    step = pl.program_id(0)
    rows = wa.shape[0] // (BLOCKS // 2)
    cut = wa.shape[1]
    rest = whole.shape[1] - cut

    @pl.when(step == 0)
    def _():
        for j in range(BLOCKS):
            to = slice(j * rows, (j + 1) * rows)
            whole[to, :cut] = take(table, LEFT + j, rows, wa, wa2)
            late = take(table, RIGHT + j, rows, wb, wb2)
            whole[to, cut:] = late[:, :rest]
            loose[to, :] = late[:, rest:].astype(WIDE)
        vectors[...] = loose[...].T[:8]

    for at in tiles(tokens.shape[0]):
        hat, _ = hat_of(tokens[at, :])
        normed[at, :] = (hat * vectors[0:1, :] + vectors[1:2, :]).astype(LOW)
    proj[...] = nn(normed[...], whole[...]).astype(LOW)
    flip[...] = normed[...].T


def enter(table, tokens, *pieces):
    length, width = tokens.shape
    total = pieces[0].shape[1] + pieces[2].shape[1] - LANES
    return pl.pallas_call(
        enter_kernel,
        grid_spec=pltpu.PrefetchScalarGridSpec(
            num_scalar_prefetch=1,
            grid=(length // ROWS,),
            in_specs=[by_row(width)] + [fixed(piece.shape) for piece in pieces],
            out_specs=[
                pl.BlockSpec((width, ROWS), lambda i, *_: (0, i)),
                by_row(total),
                kept((width, total)),
                kept((8, width)),
            ],
            scratch_shapes=[pltpu.VMEM((width, LANES), WIDE), pltpu.VMEM((ROWS, width), LOW)],
        ),
        out_shape=[
            jax.ShapeDtypeStruct((width, length), LOW),
            jax.ShapeDtypeStruct((length, total), LOW),
            jax.ShapeDtypeStruct((width, total), LOW),
            jax.ShapeDtypeStruct((8, width), WIDE),
        ],
        compiler_params=params(),
        cost_estimate=LONG,
        name="enter",
    )(table, tokens, *pieces)


def build_bias(bias, seg_col, seg_row):
    length = bias.shape[0]
    for start in range(0, length, ROWS):
        lanes = slice(start, start + ROWS)
        until = start + ROWS
        shape = (until, ROWS)
        key_at = lax.broadcasted_iota(jnp.int32, shape, 0)
        query_at = lax.broadcasted_iota(jnp.int32, shape, 1) + start
        same = jnp.broadcast_to(seg_col[:until, 0:1], shape) == jnp.broadcast_to(
            seg_row[0:1, lanes], shape
        )
        bias[:until, lanes] = jnp.where((key_at <= query_at) & same, 0.0, MASKED)


def one_head(flipped, head):
    empty = jnp.zeros((HD, flipped.shape[1]), flipped.dtype)
    if head == 0:
        return jnp.concatenate([flipped[:HD], empty], axis=0)
    return jnp.concatenate([empty, flipped[HD:]], axis=0)


def attend_kernel(queries, keys, values, seg_col, seg_row, out, lse, bias):
    @pl.when(pl.program_id(0) == 0)
    def _():
        build_bias(bias, seg_col, seg_row)

    length = queries.shape[0]
    q_flip = queries[...].T
    v_flip = values[...].T
    sides = [one_head(q_flip, head) for head in range(2)]
    for start in range(0, length, ROWS):
        lanes = slice(start, start + ROWS)
        until = start + ROWS
        pieces = []
        for head in range(2):
            scores = nn(keys[:until], sides[head][:, lanes]) * (HD**-0.5 * LOG2E)
            scores = scores + bias[:until, lanes]
            top = jnp.max(scores, axis=0, keepdims=True)
            expo = jnp.exp2(scores - top)
            total = jnp.sum(expo, axis=0, keepdims=True)
            flat = nn(v_flip[head * HD : (head + 1) * HD, :until], expo.astype(LOW))
            pieces.append(flat / total)
            lse[head : head + 1, lanes] = top + jnp.log(total) * LOG2E
        out[lanes, :] = jnp.concatenate(pieces, axis=0).T.astype(LOW)


def attend(proj, seg_col, seg_row):
    length = proj.shape[0]
    pairs = proj.shape[1] // (3 * LANES)

    def part(k):
        return pl.BlockSpec((length, LANES), lambda i: (0, k * pairs + i))

    return pl.pallas_call(
        attend_kernel,
        grid=(pairs,),
        in_specs=[part(0), part(1), part(2), fixed(seg_col.shape), fixed(seg_row.shape)],
        out_specs=[
            pl.BlockSpec((length, LANES), lambda i: (0, i)),
            pl.BlockSpec((8, length), lambda i: (i, 0)),
        ],
        out_shape=[
            jax.ShapeDtypeStruct((length, pairs * LANES), LOW),
            jax.ShapeDtypeStruct((8 * pairs, length), WIDE),
        ],
        scratch_shapes=[pltpu.VMEM((length, length), WIDE)],
        compiler_params=params(),
        cost_estimate=LONG,
        name="attend",
    )(proj, proj, proj, seg_col, seg_row)


def attend_back_kernel(
    queries, keys, values, out, grad, lse, seg_col, seg_row, result, bias, soft, pull
):
    @pl.when(pl.program_id(0) == 0)
    def _():
        build_bias(bias, seg_col, seg_row)

    length = queries.shape[0]
    scale = HD**-0.5
    q_flip = queries[...].T
    k_flip = keys[...].T
    g_flip = grad[...].T
    product = out[...].T.astype(WIDE) * g_flip.astype(WIDE)
    first = lax.broadcasted_iota(jnp.int32, (ROWS, LANES), 1) < HD
    starts = range(0, length, ROWS)
    for head in range(2):
        q_side = one_head(q_flip, head)
        g_side = one_head(g_flip, head)
        centre = jnp.sum(product[head * HD : (head + 1) * HD], axis=0, keepdims=True)
        level = lse[head : head + 1, :]
        for low in starts:
            at = slice(low, low + ROWS)
            for start in range(low, length, ROWS):
                lanes = slice(start, start + ROWS)
                scores = nn(keys[at], q_side[:, lanes]) * (scale * LOG2E)
                probs = jnp.exp2(scores + bias[at, lanes] - level[:, lanes])
                soft[head, at, lanes] = probs.astype(LOW)
                drawn = nn(values[at], g_side[:, lanes])
                pull[head, at, lanes] = (probs * (drawn - centre[:, lanes])).astype(LOW)
    for low in starts:
        at = slice(low, low + ROWS)
        k_parts = [nn(pull[head, at, low:], queries[low:, :]) for head in range(2)]
        v_parts = [nn(soft[head, at, low:], grad[low:, :]) for head in range(2)]
        result[1, at] = (jnp.where(first, *k_parts) * scale).astype(LOW)
        result[2, at] = jnp.where(first, *v_parts).astype(LOW)
        until = low + ROWS
        pieces = [
            nn(k_flip[head * HD : (head + 1) * HD, :until], pull[head, :until, at])
            for head in range(2)
        ]
        result[0, at] = (jnp.concatenate(pieces, axis=0) * scale).T.astype(LOW)


def attend_back(proj, out, grad, lse, seg_col, seg_row):
    length = proj.shape[0]
    pairs = proj.shape[1] // (3 * LANES)

    def part(k):
        return pl.BlockSpec((length, LANES), lambda i: (0, k * pairs + i))

    return pl.pallas_call(
        attend_back_kernel,
        grid=(pairs,),
        in_specs=[
            part(0),
            part(1),
            part(2),
            part(0),
            part(0),
            pl.BlockSpec((8, length), lambda i: (i, 0)),
            fixed(seg_col.shape),
            fixed(seg_row.shape),
        ],
        out_specs=pl.BlockSpec((3, length, LANES), lambda i: (0, 0, i)),
        out_shape=jax.ShapeDtypeStruct((3, length, pairs * LANES), LOW),
        scratch_shapes=[
            pltpu.VMEM((length, length), WIDE),
            pltpu.VMEM((2, length, length), LOW),
            pltpu.VMEM((2, length, length), LOW),
        ],
        compiler_params=params(),
        cost_estimate=LONG,
        name="attend_back",
    )(proj, proj, proj, out, grad, lse, seg_col, seg_row)


def leave_kernel(table, att, near, far, part, whole):
    rows = near.shape[0] // (BLOCKS // 2)
    lanes = slice(near.shape[1] - whole.shape[1], None)

    @pl.when(pl.program_id(0) == 0)
    def _():
        for j in range(BLOCKS):
            whole[j * rows : (j + 1) * rows, :] = take(
                table, BLOCKS + j, rows, near, far, lanes
            )

    part[...] = nt(att[...], whole[...]).astype(LOW)


def leave(table, att, near, far):
    length, inner = att.shape
    width = near.shape[0] * 2
    return pl.pallas_call(
        leave_kernel,
        grid_spec=pltpu.PrefetchScalarGridSpec(
            num_scalar_prefetch=1,
            grid=(length // ROWS,),
            in_specs=[by_row(inner), fixed(near.shape), fixed(far.shape)],
            out_specs=[by_row(width), kept((width, inner))],
        ),
        out_shape=[
            jax.ShapeDtypeStruct((length, width), LOW),
            jax.ShapeDtypeStruct((width, inner), LOW),
        ],
        compiler_params=params(),
        cost_estimate=LONG,
        name="leave",
    )(table, att, near, far)


SIDE = 256


def unpack(table, whole, left, right, near_a, far_a, near_b, far_b):
    rows = near_a.shape[0] // (BLOCKS // 2)
    cut = min(near_a.shape[1], whole.shape[1])
    for j in range(BLOCKS):
        to = slice(j * rows, (j + 1) * rows)
        whole[to, :cut] = take(table, left + j, rows, near_a, far_a)
        lanes = slice(0, whole.shape[1] - cut)
        whole[to, cut:] = take(table, right + j, rows, near_b, far_b, lanes)


def feed_first_kernel(
    table,
    tokens,
    part,
    far,
    vectors,
    up_a,
    up_a2,
    up_b,
    up_b2,
    middle,
    flip,
    act,
    slope,
    whole,
    normed,
):
    @pl.when(pl.program_id(0) == 0)
    def _():
        unpack(table, whole, LEFT, RIGHT, up_a, up_a2, up_b, up_b2)

    for at in tiles(tokens.shape[0]):
        values = tokens[at, :] + (part[at, :].astype(WIDE) + far[at, :].astype(WIDE))
        middle[at, :] = values
        hat, _ = hat_of(values)
        normed[at, :] = (hat * vectors[2:3, :] + vectors[3:4, :]).astype(LOW)
    root = math.sqrt(2.0 / math.pi)
    for start in range(0, whole.shape[1], SIDE):
        lanes = slice(start, start + SIDE)
        wide = nn(normed[...], whole[:, lanes])
        square = wide * wide
        bend = jnp.tanh(wide * (root + root * 0.044715 * square))
        share = 0.5 + 0.5 * bend
        act[:, lanes] = (wide * share).astype(LOW)
        slope[:, lanes] = (
            share + 0.5 * wide * (1.0 - bend * bend) * (root + 3.0 * root * 0.044715 * square)
        ).astype(LOW)
    flip[...] = normed[...].T


def feed_first(table, tokens, part, far, vectors, hidden, *pieces):
    length, width = part.shape
    return pl.pallas_call(
        feed_first_kernel,
        grid_spec=pltpu.PrefetchScalarGridSpec(
            num_scalar_prefetch=1,
            grid=(length // ROWS,),
            in_specs=[by_row(width), by_row(width), by_row(width), fixed((8, width))]
            + [fixed(piece.shape) for piece in pieces],
            out_specs=[
                by_row(width),
                pl.BlockSpec((width, ROWS), lambda i, *_: (0, i)),
                by_row(hidden),
                by_row(hidden),
                kept((width, hidden)),
            ],
            scratch_shapes=[pltpu.VMEM((ROWS, width), LOW)],
        ),
        out_shape=[
            jax.ShapeDtypeStruct((length, width), WIDE),
            jax.ShapeDtypeStruct((width, length), LOW),
            jax.ShapeDtypeStruct((length, hidden), LOW),
            jax.ShapeDtypeStruct((length, hidden), LOW),
            jax.ShapeDtypeStruct((width, hidden), LOW),
        ],
        compiler_params=params(),
        cost_estimate=LONG,
        name="feed_first",
    )(table, tokens, part, far, vectors, *pieces)


def feed_tokens_kernel(
    table,
    grad,
    act,
    slope,
    up,
    down_a,
    down_a2,
    down_b,
    down_b2,
    branch,
    pulled,
    pre,
    whole,
):
    @pl.when(pl.program_id(0) == 0)
    def _():
        unpack(table, whole, DOWN_LEFT, DOWN_RIGHT, down_a, down_a2, down_b, down_b2)

    for start in range(0, whole.shape[1], SIDE):
        lanes = slice(start, start + SIDE)
        drawn = nn(grad[...], whole[:, lanes])
        pre[:, lanes] = (drawn * slope[:, lanes].astype(WIDE)).astype(LOW)
    for start in range(0, whole.shape[0], SIDE):
        lanes = slice(start, start + SIDE)
        branch[:, lanes] = nt(act[...], whole[lanes, :]).astype(LOW)
        pulled[:, lanes] = nt(pre[...], up[lanes, :]).astype(LOW)


def feed_tokens(table, grad, act, slope, up, *pieces):
    length, width = grad.shape
    hidden = act.shape[1]
    return pl.pallas_call(
        feed_tokens_kernel,
        grid_spec=pltpu.PrefetchScalarGridSpec(
            num_scalar_prefetch=1,
            grid=(length // ROWS,),
            in_specs=[by_row(width), by_row(hidden), by_row(hidden), fixed(up.shape)]
            + [fixed(piece.shape) for piece in pieces],
            out_specs=[by_row(width), by_row(width), by_row(hidden)],
            scratch_shapes=[pltpu.VMEM((width, hidden), LOW)],
        ),
        out_shape=[
            jax.ShapeDtypeStruct((length, width), LOW),
            jax.ShapeDtypeStruct((length, width), LOW),
            jax.ShapeDtypeStruct((length, hidden), LOW),
        ],
        compiler_params=params(),
        cost_estimate=LONG,
        name="feed_tokens",
    )(table, grad, act, slope, up, *pieces)


def feed_weights_kernel(
    table, normed_flip, grad_flip, act, pre, up_keep, up_send, down_keep, down_send
):
    rows = normed_flip.shape[0] // BLOCKS
    lifted = nn(normed_flip[...], pre[...]).astype(LOW)
    lowered = nn(grad_flip[...], act[...]).astype(LOW)
    for j in range(BLOCKS):
        block = slice(j * rows, (j + 1) * rows)
        put(table, LEFT + j, rows, up_keep, up_send, lifted[block])
        put(table, RIGHT + j, rows, down_keep, down_send, lowered[block])


def feed_weights(table, normed_flip, grad_flip, act, pre):
    width, length = normed_flip.shape
    hidden = act.shape[1]
    column = pl.BlockSpec((length, SIDE), lambda i, *_: (0, i))
    half = pl.BlockSpec((width // 2, SIDE), lambda i, *_: (0, i))
    return pl.pallas_call(
        feed_weights_kernel,
        grid_spec=pltpu.PrefetchScalarGridSpec(
            num_scalar_prefetch=1,
            grid=(hidden // SIDE,),
            in_specs=[fixed((width, length)), fixed((width, length)), column, column],
            out_specs=[half] * 4,
        ),
        out_shape=[jax.ShapeDtypeStruct((width // 2, hidden), LOW)] * 4,
        compiler_params=params(),
        cost_estimate=LONG,
        name="feed_weights",
    )(table, normed_flip, grad_flip, act, pre)


def middle_back_kernel(
    table,
    pulled,
    far,
    middle,
    grad,
    vectors,
    out_whole,
    att,
    middle_grad,
    att_grad,
    out_keep,
    out_send,
    sums,
    out_sum,
    low,
    gathered,
):
    step = pl.program_id(0)
    rows = out_whole.shape[0] // BLOCKS

    @pl.when(step == 0)
    def _():
        out_sum[...] = jnp.zeros_like(out_sum)
        gathered[...] = jnp.zeros_like(gathered)

    for at in tiles(middle.shape[0]):
        pull = pulled[at, :].astype(WIDE) + far[at, :].astype(WIDE)
        hat, rate = hat_of(middle[at, :])
        whole = grad[at, :].astype(WIDE) + norm_back(pull, hat, rate, vectors[2:3, :])
        middle_grad[at, :] = whole
        low[at, :] = whole.astype(LOW)
        gathered[:8, :] += fold_rows(pull * hat)
        gathered[8:, :] += fold_rows(pull)
    att_grad[...] = nn(low[...], out_whole[...]).astype(LOW)
    out_sum[...] += tn(low[...], att[...])

    @pl.when(step == pl.num_programs(0) - 1)
    def _():
        for j in range(BLOCKS):
            block = out_sum[j * rows : (j + 1) * rows, :].astype(LOW)
            put(table, RIGHT + j, rows, out_keep, out_send, block)
        sums[0:1, :] = jnp.sum(gathered[:8, :], axis=0, keepdims=True)
        sums[1:2, :] = jnp.sum(gathered[8:, :], axis=0, keepdims=True)


def middle_back(table, pulled, far, middle, grad, vectors, out_whole, att):
    length, width = middle.shape
    inner = att.shape[1]
    return pl.pallas_call(
        middle_back_kernel,
        grid_spec=pltpu.PrefetchScalarGridSpec(
            num_scalar_prefetch=1,
            grid=(length // ROWS,),
            in_specs=[
                by_row(width),
                by_row(width),
                by_row(width),
                by_row(width),
                fixed((8, width)),
                fixed((width, inner)),
                by_row(inner),
            ],
            out_specs=[
                by_row(width),
                by_row(inner),
                kept((width // 2, inner), (0, 1)),
                kept((width // 2, inner), (0, 1)),
                kept((8, width)),
            ],
            scratch_shapes=[
                pltpu.VMEM((width, inner), WIDE),
                pltpu.VMEM((ROWS, width), LOW),
                pltpu.VMEM((16, width), WIDE),
            ],
        ),
        out_shape=[
            jax.ShapeDtypeStruct((length, width), WIDE),
            jax.ShapeDtypeStruct((length, inner), LOW),
            jax.ShapeDtypeStruct((width // 2, 2 * inner), LOW),
            jax.ShapeDtypeStruct((width // 2, 2 * inner), LOW),
            jax.ShapeDtypeStruct((8, width), WIDE),
        ],
        compiler_params=params(),
        cost_estimate=LONG,
        name="middle_back",
    )(table, pulled, far, middle, grad, vectors, out_whole, att)


def weight_back_kernel(
    table,
    proj_grad,
    normed_flip,
    held_keep,
    held_send,
    left_keep,
    left_send,
    right_keep,
    right_send,
):
    step = pl.program_id(0)
    rows = normed_flip.shape[0] // BLOCKS
    weight = nn(normed_flip[...], proj_grad[0]).astype(LOW)

    @pl.when(step < 2)
    def _():
        for j in range(BLOCKS):
            put(table, LEFT + j, rows, left_keep, left_send, weight[j * rows : (j + 1) * rows])

    @pl.when(step == 2)
    def _():
        for j in range(BLOCKS):
            block = weight[j * rows : (j + 1) * rows]
            put(table, RIGHT + j, rows, right_keep, right_send, block)


def weight_back(table, proj_grad, normed_flip, held_keep, held_send):
    width, length = normed_flip.shape
    inner = proj_grad.shape[2]
    early = pl.BlockSpec((width // 2, inner), lambda i, *_: (0, jnp.minimum(i, 1)))
    late = kept((width // 2, inner))
    return pl.pallas_call(
        weight_back_kernel,
        grid_spec=pltpu.PrefetchScalarGridSpec(
            num_scalar_prefetch=1,
            grid=(3,),
            in_specs=[
                pl.BlockSpec((1, length, inner), lambda i, *_: (i, 0, 0)),
                fixed((width, length)),
                pl.BlockSpec(memory_space=pl.ANY),
                pl.BlockSpec(memory_space=pl.ANY),
            ],
            out_specs=[early, early, late, late],
        ),
        out_shape=[jax.ShapeDtypeStruct((width // 2, 2 * inner), LOW)] * 4,
        input_output_aliases={3: 2, 4: 3},
        compiler_params=params(),
        cost_estimate=LONG,
        name="weight_back",
    )(table, proj_grad, normed_flip, held_keep, held_send)


def token_back_kernel(proj_grad, whole, pulled):
    inner = proj_grad.shape[2]
    total = nt(proj_grad[0], whole[:, :inner])
    for c in range(1, 3):
        total += nt(proj_grad[c], whole[:, c * inner : (c + 1) * inner])
    pulled[...] = total.astype(LOW)


def token_back(proj_grad, whole):
    length, inner = proj_grad.shape[1:]
    width = whole.shape[0]
    return pl.pallas_call(
        token_back_kernel,
        grid=(length // ROWS,),
        in_specs=[
            pl.BlockSpec((3, ROWS, inner), lambda i: (0, i, 0)),
            fixed(whole.shape),
        ],
        out_specs=by_row(width),
        out_shape=jax.ShapeDtypeStruct((length, width), LOW),
        compiler_params=params(),
        cost_estimate=LONG,
        name="token_back",
    )(proj_grad, whole)


def exit_kernel(core, pulled, far, tokens, middle_grad, vectors, result, sums, gathered):
    step = pl.program_id(0)

    @pl.when(step == 0)
    def _():
        gathered[...] = jnp.zeros_like(gathered)

    for at in tiles(tokens.shape[0]):
        pull = pulled[at, :].astype(WIDE) + far[at, :].astype(WIDE)
        hat, rate = hat_of(tokens[at, :])
        gathered[:8, :] += fold_rows(pull * hat)
        gathered[8:, :] += fold_rows(pull)
        result[at, :] = middle_grad[at, :] + norm_back(pull, hat, rate, vectors[0:1, :])

    @pl.when(step == pl.num_programs(0) - 1)
    def _():
        sums[0:1, :] = jnp.sum(gathered[:8, :], axis=0, keepdims=True)
        sums[1:2, :] = jnp.sum(gathered[8:, :], axis=0, keepdims=True)


def leave_layer(core, pulled, far, tokens, middle_grad, vectors):
    length, width = pulled.shape
    steps = length // ROWS
    part = steps // 2

    def turned(i, place):
        return ((i + part * (1 - place[0])) % steps, 0)

    row = pl.BlockSpec((ROWS, width), turned)
    return pl.pallas_call(
        exit_kernel,
        grid_spec=pltpu.PrefetchScalarGridSpec(
            num_scalar_prefetch=1,
            grid=(steps,),
            in_specs=[row, row, row, row, fixed((8, width))],
            out_specs=[
                pl.BlockSpec((ROWS, width), lambda i, *_: (jnp.maximum(i - part, 0), 0)),
                kept((8, width)),
            ],
            scratch_shapes=[pltpu.VMEM((16, width), WIDE)],
        ),
        out_shape=[
            jax.ShapeDtypeStruct((length // 2, width), WIDE),
            jax.ShapeDtypeStruct((8, width), WIDE),
        ],
        compiler_params=params(),
        cost_estimate=LONG,
        name="leave_layer",
    )(core, pulled, far, tokens, middle_grad, vectors)


def swap_cores(values):
    return lax.ppermute(values, "tensor", [(0, 1), (1, 0)])


def hop(values, bits, size):
    return lax.ppermute(values, "fsdp", [(i, i ^ bits) for i in range(size)])


def block_places(size, me):
    spots = jnp.arange(BLOCKS, dtype=jnp.int32)
    if size != BLOCKS:
        return jnp.concatenate([spots] * 4)
    away = me ^ spots
    low, mid, high = away & 1, (away >> 1) & 1, away >> 2
    return jnp.concatenate(
        [
            low * 8 + mid * 4 + high,
            mid * 8 + low * 4 + high,
            mid * 8 + high * 2 + low,
            low * 8 + high * 2 + mid,
        ]
    )


def vmem_call(kernel, shapes, args, name):
    return pl.pallas_call(
        kernel,
        out_shape=shapes,
        compiler_params=pltpu.CompilerParams(vmem_limit_bytes=24 * 1024 * 1024),
        cost_estimate=LONG,
        name=name,
    )(*args)


def collect(pieces, cut):
    rows, width = pieces[0].shape

    def kernel(*refs):
        left, right = refs[len(pieces) :]
        for k, piece in enumerate(refs[: len(pieces)]):
            at = slice(k * rows, (k + 1) * rows)
            left[at, :] = piece[:, :cut]
            right[at, :] = piece[:, cut:]

    total = rows * len(pieces)
    return vmem_call(
        kernel,
        [jax.ShapeDtypeStruct((total, cut), LOW), jax.ShapeDtypeStruct((total, width - cut), LOW)],
        pieces,
        "collect",
    )


def join(left, left_far, right, right_far, size):
    if size != BLOCKS:
        return jnp.concatenate([left, left_far], 0), jnp.concatenate([right, right_far], 0)

    def kernel(one, one_far, two, two_far, one_out, two_out):
        rows = one.shape[0]
        one_out[:rows, :] = one[...]
        one_out[rows:, :] = one_far[...]
        two_out[:rows, :] = two[...]
        two_out[rows:, :] = two_far[...]

    shapes = [jax.ShapeDtypeStruct((2 * v.shape[0], v.shape[1]), LOW) for v in (left, right)]
    return vmem_call(kernel, shapes, (left, left_far, right, right_far), "join")


def far_rows(values, size):
    if size != BLOCKS:
        whole = lax.all_gather(values, "fsdp", axis=0, tiled=True)
        rows = whole.shape[0] // 4
        return [whole[k * rows : (k + 1) * rows] for k in range(4)]
    return [values] + [hop(values, 4 * k, size) for k in range(1, 4)]


def after(values, *done):
    return lax.optimization_barrier((values, done))[0]


def halves(whole):
    half = whole.shape[0] // 2
    return whole[:half], whole[half:]


def down_stage(left, right, size):
    if size != BLOCKS:
        return left, None, right, None
    return left, hop(left, 1, size), right, hop(right, 2, size)


def beside(left, left_far, right, right_far, size):
    if size != BLOCKS:
        return jnp.concatenate([left, right], axis=1)
    rows, cut = left.shape

    def kernel(one, one_far, two, two_far, out):
        out[:rows, :cut] = one[...]
        out[rows:, :cut] = one_far[...]
        out[:rows, cut:] = two[...]
        out[rows:, cut:] = two_far[...]

    shape = jax.ShapeDtypeStruct((2 * rows, 2 * cut), LOW)
    return vmem_call(kernel, [shape], (left, left_far, right, right_far), "beside")[0]


def in_order(own, core):
    other = swap_cores(own)
    return jnp.where(
        core == 0,
        jnp.concatenate([own, other], axis=0),
        jnp.concatenate([other, own], axis=0),
    )


def second_stage(left, right, size):
    if size != BLOCKS:
        return halves(left) + halves(right)
    return left, hop(left, 2, size), right, hop(right, 1, size)


def third_stage(left, right, size):
    if size != BLOCKS:
        return halves(left) + halves(right)
    return left, hop(left, 1, size), right, hop(right, 2, size)


def fold_half(left, left_far, right, right_far, size):
    if size != BLOCKS:
        return left, left_far, right, right_far

    def kernel(one, one_far, two, two_far, one_low, one_high, two_low, two_high):
        rows = one_low.shape[0]
        for a, b, low, high in (
            (one, one_far, one_low, one_high),
            (two, two_far, two_low, two_high),
        ):
            low[...] = (a[:rows, :].astype(WIDE) + b[:rows, :].astype(WIDE)).astype(LOW)
            high[...] = (a[rows:, :].astype(WIDE) + b[rows:, :].astype(WIDE)).astype(LOW)

    shapes = [
        jax.ShapeDtypeStruct((v.shape[0] // 2, v.shape[1]), LOW)
        for v in (left, left, right, right)
    ]
    return vmem_call(kernel, shapes, (left, left_far, right, right_far), "fold_half")


def fold_quarter(left, left_far, right, right_far, size):
    if size != BLOCKS:
        whole = jnp.concatenate(
            [jnp.concatenate([left, left_far], 0), jnp.concatenate([right, right_far], 0)], 1
        )
        return halves(whole)

    cut = left.shape[1]
    rows = left.shape[0] // 4

    def kernel(one, one_far, two, two_far, *outs):
        for k, out in enumerate(outs):
            at = slice(k * rows, (k + 1) * rows)
            out[:, :cut] = (one[at, :].astype(WIDE) + one_far[at, :].astype(WIDE)).astype(LOW)
            out[:, cut:] = (two[at, :].astype(WIDE) + two_far[at, :].astype(WIDE)).astype(LOW)

    shapes = [jax.ShapeDtypeStruct((rows, cut + right.shape[1]), LOW)] * 4
    return vmem_call(kernel, shapes, (left, left_far, right, right_far), "fold_quarter")


def first_send(left, left_send, right, right_send, size):
    if size != BLOCKS:
        return left, left_send, right, right_send
    return left, hop(left_send, 1, size), right, hop(right_send, 2, size)


def second_send(left, left_send, right, right_send, size):
    if size != BLOCKS:
        return left, left_send, right, right_send
    return left, hop(left_send, 2, size), right, hop(right_send, 1, size)


def third_send(parts, size):
    if size != BLOCKS:
        return parts
    return [parts[0]] + [hop(parts[k], 4 * k, size) for k in range(1, 4)]


def total_of(parts, size):
    if size != BLOCKS:
        whole = jnp.concatenate(parts, axis=0).astype(WIDE)
        return lax.psum_scatter(whole, "fsdp", scatter_dimension=0, tiled=True)
    total = parts[0].astype(WIDE)
    for part in parts[1:]:
        total = total + part.astype(WIDE)
    return total


def sum_all(values, size):
    if size != BLOCKS:
        return lax.psum(values, "fsdp")
    for k in range(4):
        values = values + hop(values, 1 << k, size)
    return values


def body(
    size,
    inputs,
    segment_ids,
    qkv_weight,
    out_weight,
    up_weight,
    down_weight,
    gain_one,
    shift_one,
    gain_two,
    shift_two,
    cotangent,
):
    me = lax.axis_index("fsdp")
    core = lax.axis_index("tensor")
    rows, width = qkv_weight.shape[1:]
    half = inputs.shape[0]
    length = 2 * half
    table = block_places(size, me)

    first = jnp.concatenate(
        [
            qkv_weight.transpose(1, 0, 2).reshape(rows, 3 * width),
            jnp.stack([gain_one, shift_one, gain_two, shift_two], axis=1),
            jnp.zeros((rows, LANES - 4), WIDE),
        ],
        axis=1,
    ).astype(LOW)
    second = jnp.concatenate([up_weight, out_weight.T], axis=1).astype(LOW)
    hidden = down_weight.shape[0]
    third = [v.T.astype(LOW) for v in (down_weight[: hidden // 2], down_weight[hidden // 2 :])]
    first = far_rows(first, size)
    third = down_stage(*third, size)
    tokens = in_order(inputs, core)
    qkv = collect(after(first, tokens), (3 * width + LANES) // 2)
    second = far_rows(after(second, qkv), size)
    third = beside(*third, size)
    qkv = join(*second_stage(*qkv, size), size)
    grad = in_order(cotangent, core)
    grad_flip = grad.T
    seg_col = jnp.broadcast_to(segment_ids[:, None], (length, LANES))
    seg_row = jnp.broadcast_to(segment_ids[None, :], (8, length))
    up_out = collect(after(second, qkv, grad, grad_flip, seg_col, seg_row), SIDE * (-(-second[0].shape[1] // (2 * SIDE))))
    third = far_rows(after(third, up_out), size)
    qkv = third_stage(*qkv, size)
    up_out = second_stage(*up_out, size)

    one_flip, proj, qkv_whole, vectors = enter(table, tokens, *qkv)
    up_out = join(*after(up_out, proj), size)
    proj = after(proj, up_out)
    up_out = third_stage(*up_out, size)
    att, lse = attend(proj, seg_col, seg_row)
    down = collect(after(third, att), hidden // 2)
    att = after(att, down, up_out)
    down = second_stage(*down, size)
    part, out_whole = leave(table, att, *up_out[2:])
    far = swap_cores(part)
    middle, two_flip, act, slope, up_whole = feed_first(
        table, tokens, part, far, vectors, hidden, *up_out
    )
    branch, pulled, pre = feed_tokens(table, grad, act, slope, up_whole, *after(down, act))
    parts = feed_weights(table, two_flip, grad_flip, act, pre)
    far = after(swap_cores(pulled), parts)
    parts = first_send(*parts, size)

    middle_grad, att_grad, *held, sums_two = middle_back(
        table, pulled, far, middle, grad, vectors, out_whole, att
    )
    proj_grad = attend_back(proj, att, att_grad, lse, seg_col, seg_row)
    parts = fold_half(*after(parts, proj_grad), size)
    proj_grad = after(proj_grad, parts)
    parts = second_send(*parts, size)
    tail = weight_back(table, proj_grad, one_flip, *held)
    parts = fold_quarter(*after(parts, tail), size)
    tail = first_send(*tail, size)
    proj_grad = after(proj_grad, parts)
    parts = third_send(parts, size)
    pulled = token_back(proj_grad, qkv_whole)
    tail = fold_half(*after(tail, pulled), size)
    far = after(swap_cores(pulled), tail)
    tail = second_send(*tail, size)
    input_grad, sums_one = leave_layer(
        core[None], pulled, far, tokens, middle_grad, vectors
    )
    tail = fold_quarter(*after(tail, input_grad), size)
    parts, branch, sums_one = after((parts, branch, sums_one), tail)
    tail = third_send(tail, size)

    def own_half(values):
        return lax.dynamic_slice_in_dim(values, core * half, half, 0)

    far = swap_cores(lax.dynamic_slice_in_dim(branch, (1 - core) * half, half, 0))
    outputs = own_half(middle) + (own_half(branch).astype(WIDE) + far.astype(WIDE))
    feed_grad = total_of(parts, size)
    sums = sum_all(jnp.concatenate([sums_one[:2], sums_two[:2]], axis=0), size)
    tail = total_of(tail, size)
    sums = lax.dynamic_slice_in_dim(sums, me * rows, rows, 1)
    qkv_grad = jnp.stack([tail[:, k * width : (k + 1) * width] for k in range(3)], axis=0)
    return (
        outputs,
        input_grad,
        qkv_grad,
        tail[:, 3 * width :].T,
        feed_grad[:, :hidden],
        feed_grad[:, hidden:].T,
        sums[0],
        sums[1],
        sums[2],
        sums[3],
    )


def solution(mesh):
    tokens = P(("fsdp", "tensor"), None)
    split = P("fsdp")
    weights = (
        P(None, "fsdp", "tensor"),
        P("tensor", "fsdp"),
        P("fsdp", "tensor"),
        P("tensor", "fsdp"),
        split,
        split,
        split,
        split,
    )
    return jax.shard_map(
        functools.partial(body, mesh.shape["fsdp"]),
        mesh=mesh,
        in_specs=(tokens, split) + weights + (tokens,),
        out_specs=(tokens, tokens) + weights,
        check_vma=False,
    )
```

```python
import functools
import math

import jax
import jax.numpy as jnp
from jax import lax
from jax.experimental import pallas as pl
from jax.experimental.pallas import tpu as pltpu
from jax.sharding import PartitionSpec as P

HD = 64
EPS = 1e-05
LOW = jnp.bfloat16
WIDE = jnp.float32
BLOCKS = 16
ROWS = 256
TILE = 32
LANES = 128
LOG2E = math.log2(math.e)
LEFT, RIGHT, DOWN_LEFT, DOWN_RIGHT = (BLOCKS * k for k in range(4))
MASKED = -1e30


def nn(a, b):
    return jnp.dot(a, b, preferred_element_type=WIDE)


def nt(a, b):
    return lax.dot_general(a, b, (((1,), (1,)), ((), ())), preferred_element_type=WIDE)


def tn(a, b):
    return lax.dot_general(a, b, (((0,), (0,)), ((), ())), preferred_element_type=WIDE)


LONG = pl.CostEstimate(flops=10**13, bytes_accessed=10**9, transcendentals=0)


def params():
    return pltpu.CompilerParams(
        dimension_semantics=("arbitrary",), vmem_limit_bytes=24 * 1024 * 1024
    )


def fixed(shape):
    del shape
    return pl.BlockSpec(memory_space=pltpu.VMEM)


def kept(shape, index=None):
    place = index or (0,) * len(shape)
    return pl.BlockSpec(shape, lambda i, *_: place)


def by_row(width, rows=ROWS):
    return pl.BlockSpec((rows, width), lambda i, *_: (i, 0))


def hat_of(values):
    centre = values - jnp.mean(values, axis=-1, keepdims=True)
    rate = lax.rsqrt(jnp.mean(centre * centre, axis=-1, keepdims=True) + EPS)
    return centre * rate, rate


def tiles(rows):
    return [slice(start, start + TILE) for start in range(0, rows, TILE)]


def fold_rows(values):
    total = values[:8]
    for start in range(8, values.shape[0], 8):
        total = total + values[start : start + 8]
    return total


def norm_back(grad, hat, rate, gain):
    scaled = grad * gain
    return rate * (
        scaled
        - jnp.mean(scaled, axis=-1, keepdims=True)
        - hat * jnp.mean(scaled * hat, axis=-1, keepdims=True)
    )


def take(table, entry, rows, pieces, lanes=slice(None)):
    each = BLOCKS // len(pieces)
    place = table[entry]
    at = pl.ds(pl.multiple_of((place % each) * rows, 16), rows)
    block = pieces[0][at, lanes]
    for k in range(1, len(pieces)):
        block = jnp.where(place >= k * each, pieces[k][at, lanes], block)
    return block


def put(table, entry, bit, rows, keep, send, whole):
    for j in range(BLOCKS):
        if j & bit:
            continue
        blocks = [whole[k * rows : (k + 1) * rows] for k in (j, j | bit)]
        place = table[entry + j]
        stays = place < BLOCKS // 2
        at = pl.ds(pl.multiple_of((place % (BLOCKS // 2)) * rows, 16), rows)
        keep[at, :] = jnp.where(stays, blocks[0], blocks[1])
        send[at, :] = jnp.where(stays, blocks[1], blocks[0])


def side_bits(size):
    return (1, 2) if size == BLOCKS else (BLOCKS // 2, BLOCKS // 2)


def enter_kernel(
    share, table, tokens, wa, wb, wc, wd, we, wf, wg, wh, flip, proj, whole, vectors, loose, normed
):
    step = pl.program_id(0)
    lefts, rights = (wa, wb, wc, wd), (we, wf, wg, wh)
    rows = wa.shape[0] // (BLOCKS // 4)
    cut = wa.shape[1]
    rest = whole.shape[1] - cut

    @pl.when(step == 0)
    def _():
        for j in range(BLOCKS):
            to = slice(j * rows, (j + 1) * rows)
            whole[to, :cut] = take(table, LEFT + j, rows, lefts)
            late = take(table, RIGHT + j, rows, rights)
            whole[to, cut:] = late[:, :rest]
            loose[to, :] = late[:, rest:].astype(WIDE)
        total = jnp.zeros(vectors.shape, WIDE)
        beyond = jnp.zeros((4, vectors.shape[1] - LANES), WIDE)
        for start in range(0, vectors.shape[1], share):
            piece = jnp.concatenate([loose[start : start + 4, :], beyond], axis=1)
            piece = jnp.concatenate([piece, jnp.zeros_like(piece)], axis=0)
            total = total + pltpu.roll(piece, start, 1)
        vectors[...] = total

    for at in tiles(tokens.shape[0]):
        hat, _ = hat_of(tokens[at, :])
        normed[at, :] = (hat * vectors[0:1, :] + vectors[1:2, :]).astype(LOW)
    proj[...] = nn(normed[...], whole[...]).astype(LOW)
    flip[...] = normed[...].T


def enter(share, table, tokens, *pieces):
    length, width = tokens.shape
    total = pieces[0].shape[1] + pieces[4].shape[1] - LANES
    return pl.pallas_call(
        functools.partial(enter_kernel, share),
        grid_spec=pltpu.PrefetchScalarGridSpec(
            num_scalar_prefetch=1,
            grid=(length // ROWS,),
            in_specs=[by_row(width)] + [fixed(piece.shape) for piece in pieces],
            out_specs=[
                pl.BlockSpec((width, ROWS), lambda i, *_: (0, i)),
                by_row(total),
                kept((width, total)),
                kept((8, width)),
            ],
            scratch_shapes=[pltpu.VMEM((width, LANES), WIDE), pltpu.VMEM((ROWS, width), LOW)],
        ),
        out_shape=[
            jax.ShapeDtypeStruct((width, length), LOW),
            jax.ShapeDtypeStruct((length, total), LOW),
            jax.ShapeDtypeStruct((width, total), LOW),
            jax.ShapeDtypeStruct((8, width), WIDE),
        ],
        compiler_params=params(),
        cost_estimate=LONG,
        name="enter",
    )(table, tokens, *pieces)


def build_bias(bias, seg_col, seg_row):
    length = bias.shape[0]
    for start in range(0, length, ROWS):
        lanes = slice(start, start + ROWS)
        until = start + ROWS
        shape = (until, ROWS)
        key_at = lax.broadcasted_iota(jnp.int32, shape, 0)
        query_at = lax.broadcasted_iota(jnp.int32, shape, 1) + start
        same = jnp.broadcast_to(seg_col[:until, 0:1], shape) == jnp.broadcast_to(
            seg_row[0:1, lanes], shape
        )
        bias[:until, lanes] = jnp.where((key_at <= query_at) & same, 0.0, MASKED)


def one_head(flipped, head):
    empty = jnp.zeros((HD, flipped.shape[1]), flipped.dtype)
    if head == 0:
        return jnp.concatenate([flipped[:HD], empty], axis=0)
    return jnp.concatenate([empty, flipped[HD:]], axis=0)


def attend_kernel(queries, keys, values, seg_col, seg_row, *refs):
    out, lse, bias = refs[-3:]

    @pl.when(pl.program_id(0) == 0)
    def _():
        build_bias(bias, seg_col, seg_row)

    length = queries.shape[0]
    q_flip = queries[...].T
    v_flip = values[...].T
    sides = [one_head(q_flip, head) for head in range(2)]
    for start in range(0, length, ROWS):
        lanes = slice(start, start + ROWS)
        until = start + ROWS
        pieces = []
        for head in range(2):
            scores = nn(keys[:until], sides[head][:, lanes]) * (HD**-0.5 * LOG2E)
            scores = scores + bias[:until, lanes]
            top = jnp.max(scores, axis=0, keepdims=True)
            expo = jnp.exp2(scores - top)
            total = jnp.sum(expo, axis=0, keepdims=True)
            flat = nn(v_flip[head * HD : (head + 1) * HD, :until], expo.astype(LOW))
            pieces.append(flat / total)
            lse[head : head + 1, lanes] = top + jnp.log(total) * LOG2E
        out[lanes, :] = jnp.concatenate(pieces, axis=0).T.astype(LOW)


def attend(proj, seg_col, seg_row, begin, end, held=()):
    length = proj.shape[0]
    pairs = proj.shape[1] // (3 * LANES)

    def part(k):
        return pl.BlockSpec((length, LANES), lambda i: (0, k * pairs + begin + i))

    return pl.pallas_call(
        attend_kernel,
        grid=(end - begin,),
        in_specs=[part(0), part(1), part(2), fixed(seg_col.shape), fixed(seg_row.shape)]
        + [pl.BlockSpec(memory_space=pl.ANY) for _ in held],
        out_specs=[
            pl.BlockSpec((length, LANES), lambda i: (0, begin + i)),
            pl.BlockSpec((8, length), lambda i: (begin + i, 0)),
        ],
        out_shape=[
            jax.ShapeDtypeStruct((length, pairs * LANES), LOW),
            jax.ShapeDtypeStruct((8 * pairs, length), WIDE),
        ],
        input_output_aliases={5 + k: k for k in range(len(held))},
        scratch_shapes=[pltpu.VMEM((length, length), WIDE)],
        compiler_params=params(),
        cost_estimate=LONG,
        name="attend",
    )(proj, proj, proj, seg_col, seg_row, *held)


def attend_back_kernel(queries, keys, values, out, grad, lse, seg_col, seg_row, *refs):
    result, bias, soft, pull = refs[-4:]

    @pl.when(pl.program_id(0) == 0)
    def _():
        build_bias(bias, seg_col, seg_row)

    length = queries.shape[0]
    scale = HD**-0.5
    q_flip = queries[...].T
    k_flip = keys[...].T
    g_flip = grad[...].T
    product = out[...].T.astype(WIDE) * g_flip.astype(WIDE)
    first = lax.broadcasted_iota(jnp.int32, (ROWS, LANES), 1) < HD
    starts = range(0, length, ROWS)
    for head in range(2):
        q_side = one_head(q_flip, head)
        g_side = one_head(g_flip, head)
        centre = jnp.sum(product[head * HD : (head + 1) * HD], axis=0, keepdims=True)
        level = lse[head : head + 1, :]
        for low in starts:
            at = slice(low, low + ROWS)
            for start in range(low, length, ROWS):
                lanes = slice(start, start + ROWS)
                scores = nn(keys[at], q_side[:, lanes]) * (scale * LOG2E)
                probs = jnp.exp2(scores + bias[at, lanes] - level[:, lanes])
                soft[head, at, lanes] = probs.astype(LOW)
                drawn = nn(values[at], g_side[:, lanes])
                pull[head, at, lanes] = (probs * (drawn - centre[:, lanes])).astype(LOW)
    for low in starts:
        at = slice(low, low + ROWS)
        k_parts = [nn(pull[head, at, low:], queries[low:, :]) for head in range(2)]
        v_parts = [nn(soft[head, at, low:], grad[low:, :]) for head in range(2)]
        result[1, at] = (jnp.where(first, *k_parts) * scale).astype(LOW)
        result[2, at] = jnp.where(first, *v_parts).astype(LOW)
        until = low + ROWS
        pieces = [
            nn(k_flip[head * HD : (head + 1) * HD, :until], pull[head, :until, at])
            for head in range(2)
        ]
        result[0, at] = (jnp.concatenate(pieces, axis=0) * scale).T.astype(LOW)


def attend_back(proj, out, grad, lse, seg_col, seg_row, begin, end, held=()):
    length = proj.shape[0]
    pairs = proj.shape[1] // (3 * LANES)

    def part(k):
        return pl.BlockSpec((length, LANES), lambda i: (0, k * pairs + begin + i))

    return pl.pallas_call(
        attend_back_kernel,
        grid=(end - begin,),
        in_specs=[
            part(0),
            part(1),
            part(2),
            part(0),
            part(0),
            pl.BlockSpec((8, length), lambda i: (begin + i, 0)),
            fixed(seg_col.shape),
            fixed(seg_row.shape),
        ]
        + [pl.BlockSpec(memory_space=pl.ANY) for _ in held],
        out_specs=pl.BlockSpec((3, length, LANES), lambda i: (0, 0, begin + i)),
        out_shape=jax.ShapeDtypeStruct((3, length, pairs * LANES), LOW),
        input_output_aliases={8 + k: k for k in range(len(held))},
        scratch_shapes=[
            pltpu.VMEM((length, length), WIDE),
            pltpu.VMEM((2, length, length), LOW),
            pltpu.VMEM((2, length, length), LOW),
        ],
        compiler_params=params(),
        cost_estimate=LONG,
        name="attend_back",
    )(proj, proj, proj, out, grad, lse, seg_col, seg_row, *held)


def leave_kernel(table, att, wa, wb, wc, wd, part, whole):
    rows = wa.shape[0] // (BLOCKS // 4)
    lanes = slice(wa.shape[1] - whole.shape[1], None)

    @pl.when(pl.program_id(0) == 0)
    def _():
        for j in range(BLOCKS):
            whole[j * rows : (j + 1) * rows, :] = take(
                table, RIGHT + j, rows, (wa, wb, wc, wd), lanes
            )

    part[...] = nt(att[...], whole[...]).astype(LOW)


def leave(table, att, *pieces):
    length, inner = att.shape
    width = pieces[0].shape[0] * 4
    return pl.pallas_call(
        leave_kernel,
        grid_spec=pltpu.PrefetchScalarGridSpec(
            num_scalar_prefetch=1,
            grid=(length // ROWS,),
            in_specs=[by_row(inner)] + [fixed(piece.shape) for piece in pieces],
            out_specs=[by_row(width), kept((width, inner))],
        ),
        out_shape=[
            jax.ShapeDtypeStruct((length, width), LOW),
            jax.ShapeDtypeStruct((width, inner), LOW),
        ],
        compiler_params=params(),
        cost_estimate=LONG,
        name="leave",
    )(table, att, *pieces)


SIDE = 256


def unpack(table, whole, left, right, lefts, rights):
    rows = whole.shape[0] // BLOCKS
    cut = min(lefts[0].shape[1], whole.shape[1])
    for j in range(BLOCKS):
        to = slice(j * rows, (j + 1) * rows)
        whole[to, :cut] = take(table, left + j, rows, lefts)
        lanes = slice(0, whole.shape[1] - cut)
        whole[to, cut:] = take(table, right + j, rows, rights, lanes)


def feed_first_kernel(
    table,
    tokens,
    part,
    far,
    vectors,
    wa,
    wb,
    wc,
    wd,
    we,
    wf,
    wg,
    wh,
    middle,
    flip,
    act,
    slope,
    whole,
    normed,
):
    @pl.when(pl.program_id(0) == 0)
    def _():
        unpack(table, whole, LEFT, RIGHT, (wa, wb, wc, wd), (we, wf, wg, wh))

    for at in tiles(tokens.shape[0]):
        values = tokens[at, :] + (part[at, :].astype(WIDE) + far[at, :].astype(WIDE))
        middle[at, :] = values
        hat, _ = hat_of(values)
        normed[at, :] = (hat * vectors[2:3, :] + vectors[3:4, :]).astype(LOW)
    root = math.sqrt(2.0 / math.pi)
    for start in range(0, whole.shape[1], SIDE):
        lanes = slice(start, start + SIDE)
        wide = nn(normed[...], whole[:, lanes])
        square = wide * wide
        bend = jnp.tanh(wide * (root + root * 0.044715 * square))
        share = 0.5 + 0.5 * bend
        act[:, lanes] = (wide * share).astype(LOW)
        slope[:, lanes] = (
            share + 0.5 * wide * (1.0 - bend * bend) * (root + 3.0 * root * 0.044715 * square)
        ).astype(LOW)
    flip[...] = normed[...].T


def feed_first(table, tokens, part, far, vectors, hidden, *pieces):
    length, width = part.shape
    return pl.pallas_call(
        feed_first_kernel,
        grid_spec=pltpu.PrefetchScalarGridSpec(
            num_scalar_prefetch=1,
            grid=(length // ROWS,),
            in_specs=[by_row(width), by_row(width), by_row(width), fixed((8, width))]
            + [fixed(piece.shape) for piece in pieces],
            out_specs=[
                by_row(width),
                pl.BlockSpec((width, ROWS), lambda i, *_: (0, i)),
                by_row(hidden),
                by_row(hidden),
                kept((width, hidden)),
            ],
            scratch_shapes=[pltpu.VMEM((ROWS, width), LOW)],
        ),
        out_shape=[
            jax.ShapeDtypeStruct((length, width), WIDE),
            jax.ShapeDtypeStruct((width, length), LOW),
            jax.ShapeDtypeStruct((length, hidden), LOW),
            jax.ShapeDtypeStruct((length, hidden), LOW),
            jax.ShapeDtypeStruct((width, hidden), LOW),
        ],
        compiler_params=params(),
        cost_estimate=LONG,
        name="feed_first",
    )(table, tokens, part, far, vectors, *pieces)


def feed_tokens_kernel(
    table,
    grad,
    act,
    slope,
    up,
    down_a,
    down_a2,
    down_b,
    down_b2,
    branch,
    pulled,
    pre,
    whole,
):
    @pl.when(pl.program_id(0) == 0)
    def _():
        unpack(
            table, whole, DOWN_LEFT, DOWN_RIGHT, (down_a, down_a2), (down_b, down_b2)
        )

    for start in range(0, whole.shape[1], SIDE):
        lanes = slice(start, start + SIDE)
        drawn = nn(grad[...], whole[:, lanes])
        pre[:, lanes] = (drawn * slope[:, lanes].astype(WIDE)).astype(LOW)
    for start in range(0, whole.shape[0], SIDE):
        lanes = slice(start, start + SIDE)
        branch[:, lanes] = nt(act[...], whole[lanes, :]).astype(LOW)
        pulled[:, lanes] = nt(pre[...], up[lanes, :]).astype(LOW)


def feed_tokens(table, grad, act, slope, up, *pieces):
    length, width = grad.shape
    hidden = act.shape[1]
    return pl.pallas_call(
        feed_tokens_kernel,
        grid_spec=pltpu.PrefetchScalarGridSpec(
            num_scalar_prefetch=1,
            grid=(length // ROWS,),
            in_specs=[by_row(width), by_row(hidden), by_row(hidden), fixed(up.shape)]
            + [fixed(piece.shape) for piece in pieces],
            out_specs=[by_row(width), by_row(width), by_row(hidden)],
            scratch_shapes=[pltpu.VMEM((width, hidden), LOW)],
        ),
        out_shape=[
            jax.ShapeDtypeStruct((length, width), LOW),
            jax.ShapeDtypeStruct((length, width), LOW),
            jax.ShapeDtypeStruct((length, hidden), LOW),
        ],
        compiler_params=params(),
        cost_estimate=LONG,
        name="feed_tokens",
    )(table, grad, act, slope, up, *pieces)


def feed_weight_kernel(bits, table, flip, side, left_keep, left_send, right_keep, right_send):
    step = pl.program_id(0)
    rows = flip.shape[0] // BLOCKS
    middle = pl.num_programs(0) // 2

    @pl.when(step < middle)
    def _():
        whole = nn(flip[...], side[...]).astype(LOW)
        put(table, LEFT, bits[0], rows, left_keep, left_send, whole)

    @pl.when(step >= middle)
    def _():
        whole = nn(flip[...], side[...]).astype(LOW)
        put(table, RIGHT, bits[1], rows, right_keep, right_send, whole)


def feed_weight(size, table, flip, side):
    width, length = flip.shape
    hidden = side.shape[1]
    middle = hidden // SIDE // 2
    left = pl.BlockSpec((width // 2, SIDE), lambda i, *_: (0, jnp.minimum(i, middle - 1)))
    right = pl.BlockSpec((width // 2, SIDE), lambda i, *_: (0, jnp.maximum(i - middle, 0)))
    return pl.pallas_call(
        functools.partial(feed_weight_kernel, side_bits(size)),
        grid_spec=pltpu.PrefetchScalarGridSpec(
            num_scalar_prefetch=1,
            grid=(hidden // SIDE,),
            in_specs=[fixed((width, length)), pl.BlockSpec((length, SIDE), lambda i, *_: (0, i))],
            out_specs=[left, left, right, right],
        ),
        out_shape=[jax.ShapeDtypeStruct((width // 2, hidden // 2), LOW)] * 4,
        compiler_params=params(),
        cost_estimate=LONG,
        name="feed_weight",
    )(table, flip, side)


def middle_back_kernel(
    bits,
    table,
    pulled,
    far,
    middle,
    grad,
    vectors,
    out_whole,
    att,
    middle_grad,
    att_grad,
    out_keep,
    out_send,
    sums,
    out_sum,
    low,
    gathered,
):
    step = pl.program_id(0)
    rows = out_whole.shape[0] // BLOCKS

    @pl.when(step == 0)
    def _():
        out_sum[...] = jnp.zeros_like(out_sum)
        gathered[...] = jnp.zeros_like(gathered)

    gains, shifts = gathered[:8, :], gathered[8:, :]
    for at in tiles(middle.shape[0]):
        pull = pulled[at, :].astype(WIDE) + far[at, :].astype(WIDE)
        hat, rate = hat_of(middle[at, :])
        whole = grad[at, :].astype(WIDE) + norm_back(pull, hat, rate, vectors[2:3, :])
        middle_grad[at, :] = whole
        low[at, :] = whole.astype(LOW)
        gains += fold_rows(pull * hat)
        shifts += fold_rows(pull)
    gathered[:8, :] = gains
    gathered[8:, :] = shifts
    att_grad[...] = nn(low[...], out_whole[...]).astype(LOW)
    out_sum[...] += tn(low[...], att[...])

    @pl.when(step == pl.num_programs(0) - 1)
    def _():
        put(table, RIGHT, bits[1], rows, out_keep, out_send, out_sum[...].astype(LOW))
        sums[0:1, :] = jnp.sum(gathered[:8, :], axis=0, keepdims=True)
        sums[1:2, :] = jnp.sum(gathered[8:, :], axis=0, keepdims=True)


def middle_back(size, table, pulled, far, middle, grad, vectors, out_whole, att):
    length, width = middle.shape
    inner = att.shape[1]
    return pl.pallas_call(
        functools.partial(middle_back_kernel, side_bits(size)),
        grid_spec=pltpu.PrefetchScalarGridSpec(
            num_scalar_prefetch=1,
            grid=(length // ROWS,),
            in_specs=[
                by_row(width),
                by_row(width),
                by_row(width),
                by_row(width),
                fixed((8, width)),
                fixed((width, inner)),
                by_row(inner),
            ],
            out_specs=[
                by_row(width),
                by_row(inner),
                kept((width // 2, inner), (0, 1)),
                kept((width // 2, inner), (0, 1)),
                kept((8, width)),
            ],
            scratch_shapes=[
                pltpu.VMEM((width, inner), WIDE),
                pltpu.VMEM((ROWS, width), LOW),
                pltpu.VMEM((16, width), WIDE),
            ],
        ),
        out_shape=[
            jax.ShapeDtypeStruct((length, width), WIDE),
            jax.ShapeDtypeStruct((length, inner), LOW),
            jax.ShapeDtypeStruct((width // 2, 2 * inner), LOW),
            jax.ShapeDtypeStruct((width // 2, 2 * inner), LOW),
            jax.ShapeDtypeStruct((8, width), WIDE),
        ],
        compiler_params=params(),
        cost_estimate=LONG,
        name="middle_back",
    )(table, pulled, far, middle, grad, vectors, out_whole, att)


def weight_back_kernel(
    bits,
    table,
    proj_grad,
    normed_flip,
    held_keep,
    held_send,
    left_keep,
    left_send,
    right_keep,
    right_send,
):
    step = pl.program_id(0)
    rows = normed_flip.shape[0] // BLOCKS

    @pl.when(step < 2)
    def _():
        weight = nn(normed_flip[...], proj_grad[0]).astype(LOW)
        put(table, LEFT, bits[0], rows, left_keep, left_send, weight)

    @pl.when(step == 2)
    def _():
        weight = nn(normed_flip[...], proj_grad[0]).astype(LOW)
        put(table, RIGHT, bits[1], rows, right_keep, right_send, weight)


def weight_back(size, table, proj_grad, normed_flip, held_keep, held_send):
    width, length = normed_flip.shape
    inner = proj_grad.shape[2]
    early = pl.BlockSpec((width // 2, inner), lambda i, *_: (0, jnp.minimum(i, 1)))
    late = kept((width // 2, inner))
    return pl.pallas_call(
        functools.partial(weight_back_kernel, side_bits(size)),
        grid_spec=pltpu.PrefetchScalarGridSpec(
            num_scalar_prefetch=1,
            grid=(3,),
            in_specs=[
                pl.BlockSpec((1, length, inner), lambda i, *_: (i, 0, 0)),
                fixed((width, length)),
                pl.BlockSpec(memory_space=pl.ANY),
                pl.BlockSpec(memory_space=pl.ANY),
            ],
            out_specs=[early, early, late, late],
        ),
        out_shape=[jax.ShapeDtypeStruct((width // 2, 2 * inner), LOW)] * 4,
        input_output_aliases={3: 2, 4: 3},
        compiler_params=params(),
        cost_estimate=LONG,
        name="weight_back",
    )(table, proj_grad, normed_flip, held_keep, held_send)


def token_back_kernel(proj_grad, whole, pulled):
    inner = proj_grad.shape[2]
    total = nt(proj_grad[0], whole[:, :inner])
    for c in range(1, 3):
        total += nt(proj_grad[c], whole[:, c * inner : (c + 1) * inner])
    pulled[...] = total.astype(LOW)


def token_back(proj_grad, whole):
    length, inner = proj_grad.shape[1:]
    width = whole.shape[0]
    return pl.pallas_call(
        token_back_kernel,
        grid=(length // ROWS,),
        in_specs=[
            pl.BlockSpec((3, ROWS, inner), lambda i: (0, i, 0)),
            fixed(whole.shape),
        ],
        out_specs=by_row(width),
        out_shape=jax.ShapeDtypeStruct((length, width), LOW),
        compiler_params=params(),
        cost_estimate=LONG,
        name="token_back",
    )(proj_grad, whole)


def exit_kernel(core, pulled, far, tokens, middle_grad, vectors, result, sums, gathered):
    step = pl.program_id(0)

    @pl.when(step == 0)
    def _():
        gathered[...] = jnp.zeros_like(gathered)

    gains, shifts = gathered[:8, :], gathered[8:, :]
    for at in tiles(tokens.shape[0]):
        pull = pulled[at, :].astype(WIDE) + far[at, :].astype(WIDE)
        hat, rate = hat_of(tokens[at, :])
        gains += fold_rows(pull * hat)
        shifts += fold_rows(pull)
        result[at, :] = middle_grad[at, :] + norm_back(pull, hat, rate, vectors[0:1, :])
    gathered[:8, :] = gains
    gathered[8:, :] = shifts

    @pl.when(step == pl.num_programs(0) - 1)
    def _():
        sums[0:1, :] = jnp.sum(gathered[:8, :], axis=0, keepdims=True)
        sums[1:2, :] = jnp.sum(gathered[8:, :], axis=0, keepdims=True)


def leave_layer(core, pulled, far, tokens, middle_grad, vectors):
    length, width = pulled.shape
    steps = length // ROWS
    part = steps // 2

    def turned(i, place):
        return ((i + part * (1 - place[0])) % steps, 0)

    row = pl.BlockSpec((ROWS, width), turned)
    return pl.pallas_call(
        exit_kernel,
        grid_spec=pltpu.PrefetchScalarGridSpec(
            num_scalar_prefetch=1,
            grid=(steps,),
            in_specs=[row, row, row, row, fixed((8, width))],
            out_specs=[
                pl.BlockSpec((ROWS, width), lambda i, *_: (jnp.maximum(i - part, 0), 0)),
                kept((8, width)),
            ],
            scratch_shapes=[pltpu.VMEM((16, width), WIDE)],
        ),
        out_shape=[
            jax.ShapeDtypeStruct((length // 2, width), WIDE),
            jax.ShapeDtypeStruct((8, width), WIDE),
        ],
        compiler_params=params(),
        cost_estimate=LONG,
        name="leave_layer",
    )(core, pulled, far, tokens, middle_grad, vectors)


def swap_cores(values):
    return lax.ppermute(values, "tensor", [(0, 1), (1, 0)])


def hop(values, bits, size):
    return lax.ppermute(values, "fsdp", [(i, i ^ bits) for i in range(size)])


def block_places(size, me):
    spots = jnp.arange(BLOCKS, dtype=jnp.int32)
    if size != BLOCKS:
        return jnp.concatenate([spots] * 4)
    away = me ^ spots
    low, mid, high = away & 1, (away >> 1) & 1, away >> 2
    return jnp.concatenate(
        [
            low * 8 + mid * 4 + high,
            mid * 8 + low * 4 + high,
            mid * 8 + high * 2 + low,
            low * 8 + high * 2 + mid,
        ]
    )


def vmem_call(kernel, shapes, args, name):
    return pl.pallas_call(
        kernel,
        out_shape=shapes,
        compiler_params=pltpu.CompilerParams(vmem_limit_bytes=24 * 1024 * 1024),
        cost_estimate=LONG,
        name=name,
    )(*args)


def collect(pieces, cut):
    rows, width = pieces[0].shape

    def kernel(*refs):
        left, right = refs[len(pieces) :]
        for k, piece in enumerate(refs[: len(pieces)]):
            at = slice(k * rows, (k + 1) * rows)
            left[at, :] = piece[:, :cut]
            right[at, :] = piece[:, cut:]

    total = rows * len(pieces)
    return vmem_call(
        kernel,
        [jax.ShapeDtypeStruct((total, cut), LOW), jax.ShapeDtypeStruct((total, width - cut), LOW)],
        pieces,
        "collect",
    )


def far_rows(values, size):
    if size != BLOCKS:
        whole = lax.all_gather(values, "fsdp", axis=0, tiled=True)
        rows = whole.shape[0] // 4
        return [whole[k * rows : (k + 1) * rows] for k in range(4)]
    return [values] + [hop(values, 4 * k, size) for k in range(1, 4)]


def after(values, *done):
    return lax.optimization_barrier((values, done))[0]


def halves(whole):
    half = whole.shape[0] // 2
    return whole[:half], whole[half:]


def down_stage(left, right, size):
    if size != BLOCKS:
        return left, None, right, None
    return left, hop(left, 1, size), right, hop(right, 2, size)


def beside(left, left_far, right, right_far, size):
    if size != BLOCKS:
        return jnp.concatenate([left, right], axis=1)
    rows, cut = left.shape

    def kernel(one, one_far, two, two_far, out):
        out[:rows, :cut] = one[...]
        out[rows:, :cut] = one_far[...]
        out[:rows, cut:] = two[...]
        out[rows:, cut:] = two_far[...]

    shape = jax.ShapeDtypeStruct((2 * rows, 2 * cut), LOW)
    return vmem_call(kernel, [shape], (left, left_far, right, right_far), "beside")[0]


def in_order(own, core):
    other = swap_cores(own)
    return jnp.where(
        core == 0,
        jnp.concatenate([own, other], axis=0),
        jnp.concatenate([other, own], axis=0),
    )


def quarters(whole):
    rows = whole.shape[0] // 4
    return [whole[k * rows : (k + 1) * rows] for k in range(4)]


def spread(left, right, size):
    if size != BLOCKS:
        return quarters(left) + quarters(right)
    left_next, right_next = hop(left, 2, size), hop(right, 1, size)
    return [
        left,
        left_next,
        hop(left, 1, size),
        hop(left_next, 1, size),
        right,
        right_next,
        hop(right, 2, size),
        hop(right_next, 2, size),
    ]


def last_stage(left, right, size):
    if size != BLOCKS:
        return halves(left) + halves(right)
    return left, hop(left, 2, size), right, hop(right, 1, size)


def fold_half(groups, size):
    if size != BLOCKS:
        return [jnp.concatenate(part, axis=1) for part in zip(*groups)]
    count = len(groups)

    def kernel(*refs):
        low, high, low_two, high_two = refs[4 * count :]
        rows = low.shape[0]
        start = 0
        for k in range(count):
            one, one_far, two, two_far = refs[4 * k : 4 * k + 4]
            for a, b, to_low, to_high in (
                (one, one_far, low, high),
                (two, two_far, low_two, high_two),
            ):
                at = slice(start, start + a.shape[1]) if count > 1 else slice(None)
                to_low[:, at] = (a[:rows, :].astype(WIDE) + b[:rows, :].astype(WIDE)).astype(LOW)
                to_high[:, at] = (a[rows:, :].astype(WIDE) + b[rows:, :].astype(WIDE)).astype(LOW)
            start += one.shape[1]

    rows = groups[0][0].shape[0] // 2
    left = sum(group[0].shape[1] for group in groups)
    right = sum(group[2].shape[1] for group in groups)
    shapes = [jax.ShapeDtypeStruct((rows, n), LOW) for n in (left, left, right, right)]
    return vmem_call(kernel, shapes, [v for group in groups for v in group], "fold_half")


def fold_quarter(left, left_far, right, right_far, size):
    if size != BLOCKS:
        whole = jnp.concatenate(
            [jnp.concatenate([left, left_far], 0), jnp.concatenate([right, right_far], 0)], 1
        )
        return halves(whole)

    cut = left.shape[1]
    rows = left.shape[0] // 4

    def kernel(one, one_far, two, two_far, *outs):
        for k, out in enumerate(outs):
            at = slice(k * rows, (k + 1) * rows)
            out[:, :cut] = (one[at, :].astype(WIDE) + one_far[at, :].astype(WIDE)).astype(LOW)
            out[:, cut:] = (two[at, :].astype(WIDE) + two_far[at, :].astype(WIDE)).astype(LOW)

    shapes = [jax.ShapeDtypeStruct((rows, cut + right.shape[1]), LOW)] * 4
    return vmem_call(kernel, shapes, (left, left_far, right, right_far), "fold_quarter")


def first_send(left, left_send, right, right_send, size):
    if size != BLOCKS:
        return left, left_send, right, right_send
    return left, hop(left_send, 1, size), right, hop(right_send, 2, size)


def second_send(left, left_send, right, right_send, size):
    if size != BLOCKS:
        return left, left_send, right, right_send
    return left, hop(left_send, 2, size), right, hop(right_send, 1, size)


def third_send(parts, size):
    if size != BLOCKS:
        return parts
    return [parts[0]] + [hop(parts[k], 4 * k, size) for k in (3, 2, 1)]


def total_of(parts, size):
    if size != BLOCKS:
        whole = jnp.concatenate(parts, axis=0).astype(WIDE)
        return lax.psum_scatter(whole, "fsdp", scatter_dimension=0, tiled=True)
    total = parts[0].astype(WIDE)
    for part in parts[1:]:
        total = total + part.astype(WIDE)
    return total


def sum_near(values, size):
    if size != BLOCKS:
        return values
    for k in range(2):
        values = values + hop(values, 1 << k, size)
    return values


def sum_far(values, size):
    if size != BLOCKS:
        return lax.psum(values, "fsdp")
    for other in [hop(values, 4 * k, size) for k in range(1, 4)]:
        values = values + other
    return values


def body(
    size,
    inputs,
    segment_ids,
    qkv_weight,
    out_weight,
    up_weight,
    down_weight,
    gain_one,
    shift_one,
    gain_two,
    shift_two,
    cotangent,
):
    me = lax.axis_index("fsdp")
    core = lax.axis_index("tensor")
    rows, width = qkv_weight.shape[1:]
    half = inputs.shape[0]
    length = 2 * half
    table = block_places(size, me)

    norms = jnp.stack([gain_one, shift_one, gain_two, shift_two], axis=0)
    first = jnp.concatenate(
        [qkv_weight[0], qkv_weight[1], qkv_weight[2]]
        + [jnp.pad(norms, ((0, rows - 4), (0, LANES - rows)))],
        axis=1,
    ).astype(LOW)
    second = jnp.concatenate([up_weight, out_weight.T], axis=1).astype(LOW)
    hidden = down_weight.shape[0]
    third = [v.T.astype(LOW) for v in (down_weight[: hidden // 2], down_weight[hidden // 2 :])]
    first = far_rows(first, size)
    third = down_stage(*third, size)
    tokens = in_order(inputs, core)
    qkv = collect(after(first, tokens), (3 * width + LANES) // 2)
    second = far_rows(after(second, qkv), size)
    third = beside(*third, size)
    qkv = spread(*qkv, size)
    grad = in_order(cotangent, core)
    grad_flip = grad.T
    seg_col = jnp.broadcast_to(segment_ids[:, None], (length, LANES))
    seg_row = jnp.broadcast_to(segment_ids[None, :], (8, length))
    up_out = collect(after(second, qkv[1], qkv[5]), SIDE * (-(-second[0].shape[1] // (2 * SIDE))))
    third = far_rows(after(third, up_out), size)
    tokens, grad, grad_flip, seg_col, seg_row = after(
        (tokens, grad, grad_flip, seg_col, seg_row), up_out
    )
    up_out = spread(*up_out, size)

    one_flip, proj, qkv_whole, vectors = enter(rows, table, tokens, *qkv)
    proj = after(proj, up_out[1], up_out[5])
    att, lse = attend(proj, seg_col, seg_row, 0, width // LANES)
    down = collect(after(third, att), hidden // 2)
    att = after(att, down, up_out)
    down = last_stage(*down, size)
    part, out_whole = leave(table, att, *up_out[4:])
    far = swap_cores(part)
    middle, two_flip, act, slope, up_whole = feed_first(
        table, tokens, part, far, vectors, hidden, *up_out
    )
    down_parts = feed_weight(size, table, grad_flip, act)
    down = after(down, down_parts)
    down_parts = first_send(*down_parts, size)
    branch, pulled, pre = feed_tokens(table, grad, act, slope, up_whole, *down)
    up_parts = feed_weight(size, table, two_flip, pre)
    far = after(swap_cores(pulled), up_parts)
    up_parts = first_send(*up_parts, size)

    middle_grad, att_grad, *held, sums_two = middle_back(
        size, table, pulled, far, middle, grad, vectors, out_whole, att
    )
    pairs = width // LANES
    early = (2 * pairs + 2) // 3
    known = (proj, att, att_grad, lse, seg_col, seg_row)
    proj_grad = attend_back(*known, 0, early)
    parts = fold_half(after([down_parts, up_parts], proj_grad), size)
    proj_grad = after(proj_grad, parts)
    parts = second_send(*parts, size)
    proj_grad = attend_back(*known, early, pairs, (proj_grad,))
    tail = weight_back(size, table, proj_grad, one_flip, *held)
    proj_grad = after(proj_grad, tail)
    tail = first_send(*tail, size)
    pulled = token_back(proj_grad, qkv_whole)
    parts = fold_quarter(*after(parts, pulled), size)
    tail = fold_half([after(tail, parts)], size)
    parts = third_send(parts, size)
    far = after(swap_cores(pulled), tail)
    tail = second_send(*tail, size)
    input_grad, sums_one = leave_layer(
        core[None], pulled, far, tokens, middle_grad, vectors
    )
    tail = fold_quarter(*after(tail, input_grad), size)
    parts, branch, sums_one = after((parts, branch, sums_one), tail)
    tail = third_send(tail, size)

    def own_half(values):
        return lax.dynamic_slice_in_dim(values, core * half, half, 0)

    far = swap_cores(lax.dynamic_slice_in_dim(branch, (1 - core) * half, half, 0))
    outputs = own_half(middle) + (own_half(branch).astype(WIDE) + far.astype(WIDE))
    feed_grad = total_of(parts, size)
    sums = sum_near(jnp.concatenate([sums_one[:2], sums_two[:2]], axis=0), size)
    sums = sum_far(after(sums, tail), size)
    tail = total_of(tail, size)
    part = hidden // 2
    quarters = [feed_grad[:, k * part : (k + 1) * part] for k in range(4)]
    sums = lax.dynamic_slice_in_dim(sums, me * rows, rows, 1)
    qkv_grad = jnp.stack([tail[:, k * width : (k + 1) * width] for k in range(3)], axis=0)
    return (
        outputs,
        input_grad,
        qkv_grad,
        tail[:, 3 * width :].T,
        jnp.concatenate([quarters[1], quarters[3]], axis=1),
        jnp.concatenate([quarters[0].T, quarters[2].T], axis=0),
        sums[0],
        sums[1],
        sums[2],
        sums[3],
    )


def solution(mesh):
    tokens = P(("fsdp", "tensor"), None)
    split = P("fsdp")
    weights = (
        P(None, "fsdp", "tensor"),
        P("tensor", "fsdp"),
        P("fsdp", "tensor"),
        P("tensor", "fsdp"),
        split,
        split,
        split,
        split,
    )
    return jax.shard_map(
        functools.partial(body, mesh.shape["fsdp"]),
        mesh=mesh,
        in_specs=(tokens, split) + weights + (tokens,),
        out_specs=(tokens, tokens) + weights,
        check_vma=False,
    )
```

```python
import functools
import math

import jax
import jax.numpy as jnp
from jax import lax
from jax.experimental import pallas as pl
from jax.experimental.pallas import tpu as pltpu
from jax.sharding import PartitionSpec as P

HD = 64
EPS = 1e-05
LOW = jnp.bfloat16
WIDE = jnp.float32
BLOCKS = 16
ROWS = 256
TILE = 32
LANES = 128
LOG2E = math.log2(math.e)
LEFT, RIGHT, DOWN_LEFT, DOWN_RIGHT = (BLOCKS * k for k in range(4))
MASKED = -1e30


def nn(a, b):
    return jnp.dot(a, b, preferred_element_type=WIDE)


def nt(a, b):
    return lax.dot_general(a, b, (((1,), (1,)), ((), ())), preferred_element_type=WIDE)


def tn(a, b):
    return lax.dot_general(a, b, (((0,), (0,)), ((), ())), preferred_element_type=WIDE)


LONG = pl.CostEstimate(flops=10**13, bytes_accessed=10**9, transcendentals=0)


def params():
    return pltpu.CompilerParams(
        dimension_semantics=("arbitrary",), vmem_limit_bytes=24 * 1024 * 1024
    )


def fixed(shape):
    del shape
    return pl.BlockSpec(memory_space=pltpu.VMEM)


def kept(shape, index=None):
    place = index or (0,) * len(shape)
    return pl.BlockSpec(shape, lambda i, *_: place)


def by_row(width, rows=ROWS):
    return pl.BlockSpec((rows, width), lambda i, *_: (i, 0))


def hat_of(values):
    centre = values - jnp.mean(values, axis=-1, keepdims=True)
    rate = lax.rsqrt(jnp.mean(centre * centre, axis=-1, keepdims=True) + EPS)
    return centre * rate, rate


def tiles(rows):
    return [slice(start, start + TILE) for start in range(0, rows, TILE)]


def fold_rows(values):
    total = values[:8]
    for start in range(8, values.shape[0], 8):
        total = total + values[start : start + 8]
    return total


def norm_back(grad, hat, rate, gain):
    scaled = grad * gain
    return rate * (
        scaled
        - jnp.mean(scaled, axis=-1, keepdims=True)
        - hat * jnp.mean(scaled * hat, axis=-1, keepdims=True)
    )


def take(table, entry, rows, pieces, lanes=slice(None)):
    each = BLOCKS // len(pieces)
    place = table[entry]
    at = pl.ds(pl.multiple_of((place % each) * rows, 16), rows)
    block = pieces[0][at, lanes]
    for k in range(1, len(pieces)):
        block = jnp.where(place >= k * each, pieces[k][at, lanes], block)
    return block


def put(table, entry, bit, rows, keep, send, whole):
    for j in range(BLOCKS):
        if j & bit:
            continue
        blocks = [whole[k * rows : (k + 1) * rows] for k in (j, j | bit)]
        place = table[entry + j]
        stays = place < BLOCKS // 2
        at = pl.ds(pl.multiple_of((place % (BLOCKS // 2)) * rows, 16), rows)
        keep[at, :] = jnp.where(stays, blocks[0], blocks[1])
        send[at, :] = jnp.where(stays, blocks[1], blocks[0])


def side_bits(size):
    return (1, 2) if size == BLOCKS else (BLOCKS // 2, BLOCKS // 2)


def enter_kernel(
    share, table, tokens, wa, wb, wc, wd, we, wf, wg, wh, flip, proj, whole, vectors, loose, normed
):
    step = pl.program_id(0)
    lefts, rights = (wa, wb, wc, wd), (we, wf, wg, wh)
    rows = wa.shape[0] // (BLOCKS // 4)
    cut = wa.shape[1]
    rest = whole.shape[1] - cut

    @pl.when(step == 0)
    def _():
        for j in range(BLOCKS):
            to = slice(j * rows, (j + 1) * rows)
            whole[to, :cut] = take(table, LEFT + j, rows, lefts)
            late = take(table, RIGHT + j, rows, rights)
            whole[to, cut:] = late[:, :rest]
            loose[to, :] = late[:, rest:].astype(WIDE)
        total = jnp.zeros(vectors.shape, WIDE)
        beyond = jnp.zeros((4, vectors.shape[1] - LANES), WIDE)
        for start in range(0, vectors.shape[1], share):
            piece = jnp.concatenate([loose[start : start + 4, :], beyond], axis=1)
            piece = jnp.concatenate([piece, jnp.zeros_like(piece)], axis=0)
            total = total + pltpu.roll(piece, start, 1)
        vectors[...] = total

    for at in tiles(tokens.shape[0]):
        hat, _ = hat_of(tokens[at, :])
        normed[at, :] = (hat * vectors[0:1, :] + vectors[1:2, :]).astype(LOW)
    proj[...] = nn(normed[...], whole[...]).astype(LOW)
    flip[...] = normed[...].T


def enter(share, table, tokens, *pieces):
    length, width = tokens.shape
    total = pieces[0].shape[1] + pieces[4].shape[1] - LANES
    return pl.pallas_call(
        functools.partial(enter_kernel, share),
        grid_spec=pltpu.PrefetchScalarGridSpec(
            num_scalar_prefetch=1,
            grid=(length // ROWS,),
            in_specs=[by_row(width)] + [fixed(piece.shape) for piece in pieces],
            out_specs=[
                pl.BlockSpec((width, ROWS), lambda i, *_: (0, i)),
                by_row(total),
                kept((width, total)),
                kept((8, width)),
            ],
            scratch_shapes=[pltpu.VMEM((width, LANES), WIDE), pltpu.VMEM((ROWS, width), LOW)],
        ),
        out_shape=[
            jax.ShapeDtypeStruct((width, length), LOW),
            jax.ShapeDtypeStruct((length, total), LOW),
            jax.ShapeDtypeStruct((width, total), LOW),
            jax.ShapeDtypeStruct((8, width), WIDE),
        ],
        compiler_params=params(),
        cost_estimate=LONG,
        name="enter",
    )(table, tokens, *pieces)


def build_bias(bias, seg_col, seg_row):
    length = bias.shape[0]
    for start in range(0, length, ROWS):
        lanes = slice(start, start + ROWS)
        until = start + ROWS
        shape = (until, ROWS)
        key_at = lax.broadcasted_iota(jnp.int32, shape, 0)
        query_at = lax.broadcasted_iota(jnp.int32, shape, 1) + start
        same = jnp.broadcast_to(seg_col[:until, 0:1], shape) == jnp.broadcast_to(
            seg_row[0:1, lanes], shape
        )
        bias[:until, lanes] = jnp.where((key_at <= query_at) & same, 0.0, MASKED)


def one_head(flipped, head):
    empty = jnp.zeros((HD, flipped.shape[1]), flipped.dtype)
    if head == 0:
        return jnp.concatenate([flipped[:HD], empty], axis=0)
    return jnp.concatenate([empty, flipped[HD:]], axis=0)


def attend_kernel(queries, keys, values, seg_col, seg_row, *refs):
    out, lse, bias = refs[-3:]

    @pl.when(pl.program_id(0) == 0)
    def _():
        build_bias(bias, seg_col, seg_row)

    length = queries.shape[0]
    q_flip = queries[...].T
    v_flip = values[...].T
    sides = [one_head(q_flip, head) for head in range(2)]
    for start in range(0, length, ROWS):
        lanes = slice(start, start + ROWS)
        until = start + ROWS
        pieces = []
        for head in range(2):
            scores = nn(keys[:until], sides[head][:, lanes]) * (HD**-0.5 * LOG2E)
            scores = scores + bias[:until, lanes]
            top = jnp.max(scores, axis=0, keepdims=True)
            expo = jnp.exp2(scores - top)
            total = jnp.sum(expo, axis=0, keepdims=True)
            flat = nn(v_flip[head * HD : (head + 1) * HD, :until], expo.astype(LOW))
            pieces.append(flat / total)
            lse[head : head + 1, lanes] = top + jnp.log(total) * LOG2E
        out[lanes, :] = jnp.concatenate(pieces, axis=0).T.astype(LOW)


def attend(proj, seg_col, seg_row, begin, end, held=()):
    length = proj.shape[0]
    pairs = proj.shape[1] // (3 * LANES)

    def part(k):
        return pl.BlockSpec((length, LANES), lambda i: (0, k * pairs + begin + i))

    return pl.pallas_call(
        attend_kernel,
        grid=(end - begin,),
        in_specs=[part(0), part(1), part(2), fixed(seg_col.shape), fixed(seg_row.shape)]
        + [pl.BlockSpec(memory_space=pl.ANY) for _ in held],
        out_specs=[
            pl.BlockSpec((length, LANES), lambda i: (0, begin + i)),
            pl.BlockSpec((8, length), lambda i: (begin + i, 0)),
        ],
        out_shape=[
            jax.ShapeDtypeStruct((length, pairs * LANES), LOW),
            jax.ShapeDtypeStruct((8 * pairs, length), WIDE),
        ],
        input_output_aliases={5 + k: k for k in range(len(held))},
        scratch_shapes=[pltpu.VMEM((length, length), WIDE)],
        compiler_params=params(),
        cost_estimate=LONG,
        name="attend",
    )(proj, proj, proj, seg_col, seg_row, *held)


def attend_back_kernel(queries, keys, values, out, grad, lse, seg_col, seg_row, *refs):
    result, bias, soft, pull = refs[-4:]

    @pl.when(pl.program_id(0) == 0)
    def _():
        build_bias(bias, seg_col, seg_row)

    length = queries.shape[0]
    scale = HD**-0.5
    q_flip = queries[...].T
    k_flip = keys[...].T
    g_flip = grad[...].T
    product = out[...].T.astype(WIDE) * g_flip.astype(WIDE)
    first = lax.broadcasted_iota(jnp.int32, (ROWS, LANES), 1) < HD
    starts = range(0, length, ROWS)
    for head in range(2):
        q_side = one_head(q_flip, head)
        g_side = one_head(g_flip, head)
        centre = jnp.sum(product[head * HD : (head + 1) * HD], axis=0, keepdims=True)
        level = lse[head : head + 1, :]
        for low in starts:
            at = slice(low, low + ROWS)
            for start in range(low, length, ROWS):
                lanes = slice(start, start + ROWS)
                scores = nn(keys[at], q_side[:, lanes]) * (scale * LOG2E)
                probs = jnp.exp2(scores + bias[at, lanes] - level[:, lanes])
                soft[head, at, lanes] = probs.astype(LOW)
                drawn = nn(values[at], g_side[:, lanes])
                pull[head, at, lanes] = (probs * (drawn - centre[:, lanes])).astype(LOW)
    for low in starts:
        at = slice(low, low + ROWS)
        k_parts = [nn(pull[head, at, low:], queries[low:, :]) for head in range(2)]
        v_parts = [nn(soft[head, at, low:], grad[low:, :]) for head in range(2)]
        result[1, at] = (jnp.where(first, *k_parts) * scale).astype(LOW)
        result[2, at] = jnp.where(first, *v_parts).astype(LOW)
        until = low + ROWS
        pieces = [
            nn(k_flip[head * HD : (head + 1) * HD, :until], pull[head, :until, at])
            for head in range(2)
        ]
        result[0, at] = (jnp.concatenate(pieces, axis=0) * scale).T.astype(LOW)


def attend_back(proj, out, grad, lse, seg_col, seg_row, begin, end, held=()):
    length = proj.shape[0]
    pairs = proj.shape[1] // (3 * LANES)

    def part(k):
        return pl.BlockSpec((length, LANES), lambda i: (0, k * pairs + begin + i))

    return pl.pallas_call(
        attend_back_kernel,
        grid=(end - begin,),
        in_specs=[
            part(0),
            part(1),
            part(2),
            part(0),
            part(0),
            pl.BlockSpec((8, length), lambda i: (begin + i, 0)),
            fixed(seg_col.shape),
            fixed(seg_row.shape),
        ]
        + [pl.BlockSpec(memory_space=pl.ANY) for _ in held],
        out_specs=pl.BlockSpec((3, length, LANES), lambda i: (0, 0, begin + i)),
        out_shape=jax.ShapeDtypeStruct((3, length, pairs * LANES), LOW),
        input_output_aliases={8 + k: k for k in range(len(held))},
        scratch_shapes=[
            pltpu.VMEM((length, length), WIDE),
            pltpu.VMEM((2, length, length), LOW),
            pltpu.VMEM((2, length, length), LOW),
        ],
        compiler_params=params(),
        cost_estimate=LONG,
        name="attend_back",
    )(proj, proj, proj, out, grad, lse, seg_col, seg_row, *held)


def leave_kernel(table, att, wa, wb, wc, wd, part, whole):
    rows = wa.shape[0] // (BLOCKS // 4)
    lanes = slice(wa.shape[1] - whole.shape[1], None)

    @pl.when(pl.program_id(0) == 0)
    def _():
        for j in range(BLOCKS):
            whole[j * rows : (j + 1) * rows, :] = take(
                table, RIGHT + j, rows, (wa, wb, wc, wd), lanes
            )

    part[...] = nt(att[...], whole[...]).astype(LOW)


def leave(table, att, *pieces):
    length, inner = att.shape
    width = pieces[0].shape[0] * 4
    return pl.pallas_call(
        leave_kernel,
        grid_spec=pltpu.PrefetchScalarGridSpec(
            num_scalar_prefetch=1,
            grid=(length // ROWS,),
            in_specs=[by_row(inner)] + [fixed(piece.shape) for piece in pieces],
            out_specs=[by_row(width), kept((width, inner))],
        ),
        out_shape=[
            jax.ShapeDtypeStruct((length, width), LOW),
            jax.ShapeDtypeStruct((width, inner), LOW),
        ],
        compiler_params=params(),
        cost_estimate=LONG,
        name="leave",
    )(table, att, *pieces)


SIDE = 256


def unpack(table, whole, left, right, lefts, rights):
    rows = whole.shape[0] // BLOCKS
    cut = min(lefts[0].shape[1], whole.shape[1])
    for j in range(BLOCKS):
        to = slice(j * rows, (j + 1) * rows)
        whole[to, :cut] = take(table, left + j, rows, lefts)
        lanes = slice(0, whole.shape[1] - cut)
        whole[to, cut:] = take(table, right + j, rows, rights, lanes)


def feed_first_kernel(
    table,
    tokens,
    part,
    far,
    vectors,
    wa,
    wb,
    wc,
    wd,
    we,
    wf,
    wg,
    wh,
    middle,
    flip,
    act,
    slope,
    whole,
    normed,
):
    @pl.when(pl.program_id(0) == 0)
    def _():
        unpack(table, whole, LEFT, RIGHT, (wa, wb, wc, wd), (we, wf, wg, wh))

    for at in tiles(tokens.shape[0]):
        values = tokens[at, :] + (part[at, :].astype(WIDE) + far[at, :].astype(WIDE))
        middle[at, :] = values
        hat, _ = hat_of(values)
        normed[at, :] = (hat * vectors[2:3, :] + vectors[3:4, :]).astype(LOW)
    root = math.sqrt(2.0 / math.pi)
    for start in range(0, whole.shape[1], SIDE):
        lanes = slice(start, start + SIDE)
        wide = nn(normed[...], whole[:, lanes])
        square = wide * wide
        bend = jnp.tanh(wide * (root + root * 0.044715 * square))
        share = 0.5 + 0.5 * bend
        act[:, lanes] = (wide * share).astype(LOW)
        slope[:, lanes] = (
            share + 0.5 * wide * (1.0 - bend * bend) * (root + 3.0 * root * 0.044715 * square)
        ).astype(LOW)
    flip[...] = normed[...].T


def feed_first(table, tokens, part, far, vectors, hidden, *pieces):
    length, width = part.shape
    return pl.pallas_call(
        feed_first_kernel,
        grid_spec=pltpu.PrefetchScalarGridSpec(
            num_scalar_prefetch=1,
            grid=(length // ROWS,),
            in_specs=[by_row(width), by_row(width), by_row(width), fixed((8, width))]
            + [fixed(piece.shape) for piece in pieces],
            out_specs=[
                by_row(width),
                pl.BlockSpec((width, ROWS), lambda i, *_: (0, i)),
                by_row(hidden),
                by_row(hidden),
                kept((width, hidden)),
            ],
            scratch_shapes=[pltpu.VMEM((ROWS, width), LOW)],
        ),
        out_shape=[
            jax.ShapeDtypeStruct((length, width), WIDE),
            jax.ShapeDtypeStruct((width, length), LOW),
            jax.ShapeDtypeStruct((length, hidden), LOW),
            jax.ShapeDtypeStruct((length, hidden), LOW),
            jax.ShapeDtypeStruct((width, hidden), LOW),
        ],
        compiler_params=params(),
        cost_estimate=LONG,
        name="feed_first",
    )(table, tokens, part, far, vectors, *pieces)


def feed_tokens_kernel(
    table,
    grad,
    act,
    slope,
    up,
    down_a,
    down_a2,
    down_b,
    down_b2,
    branch,
    pulled,
    pre,
    whole,
):
    @pl.when(pl.program_id(0) == 0)
    def _():
        unpack(
            table, whole, DOWN_LEFT, DOWN_RIGHT, (down_a, down_a2), (down_b, down_b2)
        )

    for start in range(0, whole.shape[1], SIDE):
        lanes = slice(start, start + SIDE)
        drawn = nn(grad[...], whole[:, lanes])
        pre[:, lanes] = (drawn * slope[:, lanes].astype(WIDE)).astype(LOW)
    for start in range(0, whole.shape[0], SIDE):
        lanes = slice(start, start + SIDE)
        branch[:, lanes] = nt(act[...], whole[lanes, :]).astype(LOW)
        pulled[:, lanes] = nt(pre[...], up[lanes, :]).astype(LOW)


def feed_tokens(table, grad, act, slope, up, *pieces):
    length, width = grad.shape
    hidden = act.shape[1]
    return pl.pallas_call(
        feed_tokens_kernel,
        grid_spec=pltpu.PrefetchScalarGridSpec(
            num_scalar_prefetch=1,
            grid=(length // ROWS,),
            in_specs=[by_row(width), by_row(hidden), by_row(hidden), fixed(up.shape)]
            + [fixed(piece.shape) for piece in pieces],
            out_specs=[by_row(width), by_row(width), by_row(hidden)],
            scratch_shapes=[pltpu.VMEM((width, hidden), LOW)],
        ),
        out_shape=[
            jax.ShapeDtypeStruct((length, width), LOW),
            jax.ShapeDtypeStruct((length, width), LOW),
            jax.ShapeDtypeStruct((length, hidden), LOW),
        ],
        compiler_params=params(),
        cost_estimate=LONG,
        name="feed_tokens",
    )(table, grad, act, slope, up, *pieces)


def feed_weight_kernel(bits, table, flip, side, left_keep, left_send, right_keep, right_send):
    step = pl.program_id(0)
    rows = flip.shape[0] // BLOCKS
    middle = pl.num_programs(0) // 2

    @pl.when(step < middle)
    def _():
        whole = nn(flip[...], side[...]).astype(LOW)
        put(table, LEFT, bits[0], rows, left_keep, left_send, whole)

    @pl.when(step >= middle)
    def _():
        whole = nn(flip[...], side[...]).astype(LOW)
        put(table, RIGHT, bits[1], rows, right_keep, right_send, whole)


def feed_weight(size, table, flip, side):
    width, length = flip.shape
    hidden = side.shape[1]
    middle = hidden // SIDE // 2
    left = pl.BlockSpec((width // 2, SIDE), lambda i, *_: (0, jnp.minimum(i, middle - 1)))
    right = pl.BlockSpec((width // 2, SIDE), lambda i, *_: (0, jnp.maximum(i - middle, 0)))
    return pl.pallas_call(
        functools.partial(feed_weight_kernel, side_bits(size)),
        grid_spec=pltpu.PrefetchScalarGridSpec(
            num_scalar_prefetch=1,
            grid=(hidden // SIDE,),
            in_specs=[fixed((width, length)), pl.BlockSpec((length, SIDE), lambda i, *_: (0, i))],
            out_specs=[left, left, right, right],
        ),
        out_shape=[jax.ShapeDtypeStruct((width // 2, hidden // 2), LOW)] * 4,
        compiler_params=params(),
        cost_estimate=LONG,
        name="feed_weight",
    )(table, flip, side)


def middle_back_kernel(
    bits,
    table,
    pulled,
    far,
    middle,
    grad,
    vectors,
    out_whole,
    att,
    middle_grad,
    att_grad,
    out_keep,
    out_send,
    sums,
    out_sum,
    low,
    gathered,
):
    step = pl.program_id(0)
    rows = out_whole.shape[0] // BLOCKS

    @pl.when(step == 0)
    def _():
        out_sum[...] = jnp.zeros_like(out_sum)
        gathered[...] = jnp.zeros_like(gathered)

    gains, shifts = gathered[:8, :], gathered[8:, :]
    for at in tiles(middle.shape[0]):
        pull = pulled[at, :].astype(WIDE) + far[at, :].astype(WIDE)
        hat, rate = hat_of(middle[at, :])
        whole = grad[at, :].astype(WIDE) + norm_back(pull, hat, rate, vectors[2:3, :])
        middle_grad[at, :] = whole
        low[at, :] = whole.astype(LOW)
        gains += fold_rows(pull * hat)
        shifts += fold_rows(pull)
    gathered[:8, :] = gains
    gathered[8:, :] = shifts
    att_grad[...] = nn(low[...], out_whole[...]).astype(LOW)
    out_sum[...] += tn(low[...], att[...])

    @pl.when(step == pl.num_programs(0) - 1)
    def _():
        put(table, RIGHT, bits[1], rows, out_keep, out_send, out_sum[...].astype(LOW))
        sums[0:1, :] = jnp.sum(gathered[:8, :], axis=0, keepdims=True)
        sums[1:2, :] = jnp.sum(gathered[8:, :], axis=0, keepdims=True)


def middle_back(size, table, pulled, far, middle, grad, vectors, out_whole, att):
    length, width = middle.shape
    inner = att.shape[1]
    return pl.pallas_call(
        functools.partial(middle_back_kernel, side_bits(size)),
        grid_spec=pltpu.PrefetchScalarGridSpec(
            num_scalar_prefetch=1,
            grid=(length // ROWS,),
            in_specs=[
                by_row(width),
                by_row(width),
                by_row(width),
                by_row(width),
                fixed((8, width)),
                fixed((width, inner)),
                by_row(inner),
            ],
            out_specs=[
                by_row(width),
                by_row(inner),
                kept((width // 2, inner), (0, 1)),
                kept((width // 2, inner), (0, 1)),
                kept((8, width)),
            ],
            scratch_shapes=[
                pltpu.VMEM((width, inner), WIDE),
                pltpu.VMEM((ROWS, width), LOW),
                pltpu.VMEM((16, width), WIDE),
            ],
        ),
        out_shape=[
            jax.ShapeDtypeStruct((length, width), WIDE),
            jax.ShapeDtypeStruct((length, inner), LOW),
            jax.ShapeDtypeStruct((width // 2, 2 * inner), LOW),
            jax.ShapeDtypeStruct((width // 2, 2 * inner), LOW),
            jax.ShapeDtypeStruct((8, width), WIDE),
        ],
        compiler_params=params(),
        cost_estimate=LONG,
        name="middle_back",
    )(table, pulled, far, middle, grad, vectors, out_whole, att)


def weight_back_kernel(
    bits,
    table,
    proj_grad,
    normed_flip,
    held_keep,
    held_send,
    left_keep,
    left_send,
    right_keep,
    right_send,
):
    step = pl.program_id(0)
    rows = normed_flip.shape[0] // BLOCKS

    @pl.when(step < 2)
    def _():
        weight = nn(normed_flip[...], proj_grad[0]).astype(LOW)
        put(table, LEFT, bits[0], rows, left_keep, left_send, weight)

    @pl.when(step == 2)
    def _():
        weight = nn(normed_flip[...], proj_grad[0]).astype(LOW)
        put(table, RIGHT, bits[1], rows, right_keep, right_send, weight)


def weight_back(size, table, proj_grad, normed_flip, held_keep, held_send):
    width, length = normed_flip.shape
    inner = proj_grad.shape[2]
    early = pl.BlockSpec((width // 2, inner), lambda i, *_: (0, jnp.minimum(i, 1)))
    late = kept((width // 2, inner))
    return pl.pallas_call(
        functools.partial(weight_back_kernel, side_bits(size)),
        grid_spec=pltpu.PrefetchScalarGridSpec(
            num_scalar_prefetch=1,
            grid=(3,),
            in_specs=[
                pl.BlockSpec((1, length, inner), lambda i, *_: (i, 0, 0)),
                fixed((width, length)),
                pl.BlockSpec(memory_space=pl.ANY),
                pl.BlockSpec(memory_space=pl.ANY),
            ],
            out_specs=[early, early, late, late],
        ),
        out_shape=[jax.ShapeDtypeStruct((width // 2, 2 * inner), LOW)] * 4,
        input_output_aliases={3: 2, 4: 3},
        compiler_params=params(),
        cost_estimate=LONG,
        name="weight_back",
    )(table, proj_grad, normed_flip, held_keep, held_send)


def token_back_kernel(proj_grad, whole, pulled):
    inner = proj_grad.shape[2]
    total = nt(proj_grad[0], whole[:, :inner])
    for c in range(1, 3):
        total += nt(proj_grad[c], whole[:, c * inner : (c + 1) * inner])
    pulled[...] = total.astype(LOW)


def token_back(proj_grad, whole):
    length, inner = proj_grad.shape[1:]
    width = whole.shape[0]
    return pl.pallas_call(
        token_back_kernel,
        grid=(length // ROWS,),
        in_specs=[
            pl.BlockSpec((3, ROWS, inner), lambda i: (0, i, 0)),
            fixed(whole.shape),
        ],
        out_specs=by_row(width),
        out_shape=jax.ShapeDtypeStruct((length, width), LOW),
        compiler_params=params(),
        cost_estimate=LONG,
        name="token_back",
    )(proj_grad, whole)


def exit_kernel(core, pulled, far, tokens, middle_grad, vectors, result, sums, gathered):
    step = pl.program_id(0)

    @pl.when(step == 0)
    def _():
        gathered[...] = jnp.zeros_like(gathered)

    gains, shifts = gathered[:8, :], gathered[8:, :]
    for at in tiles(tokens.shape[0]):
        pull = pulled[at, :].astype(WIDE) + far[at, :].astype(WIDE)
        hat, rate = hat_of(tokens[at, :])
        gains += fold_rows(pull * hat)
        shifts += fold_rows(pull)
        result[at, :] = middle_grad[at, :] + norm_back(pull, hat, rate, vectors[0:1, :])
    gathered[:8, :] = gains
    gathered[8:, :] = shifts

    @pl.when(step == pl.num_programs(0) - 1)
    def _():
        sums[0:1, :] = jnp.sum(gathered[:8, :], axis=0, keepdims=True)
        sums[1:2, :] = jnp.sum(gathered[8:, :], axis=0, keepdims=True)


def leave_layer(core, pulled, far, tokens, middle_grad, vectors):
    length, width = pulled.shape
    steps = length // ROWS
    part = steps // 2

    def turned(i, place):
        return ((i + part * (1 - place[0])) % steps, 0)

    row = pl.BlockSpec((ROWS, width), turned)
    return pl.pallas_call(
        exit_kernel,
        grid_spec=pltpu.PrefetchScalarGridSpec(
            num_scalar_prefetch=1,
            grid=(steps,),
            in_specs=[row, row, row, row, fixed((8, width))],
            out_specs=[
                pl.BlockSpec((ROWS, width), lambda i, *_: (jnp.maximum(i - part, 0), 0)),
                kept((8, width)),
            ],
            scratch_shapes=[pltpu.VMEM((16, width), WIDE)],
        ),
        out_shape=[
            jax.ShapeDtypeStruct((length // 2, width), WIDE),
            jax.ShapeDtypeStruct((8, width), WIDE),
        ],
        compiler_params=params(),
        cost_estimate=LONG,
        name="leave_layer",
    )(core, pulled, far, tokens, middle_grad, vectors)


def swap_cores(values):
    return lax.ppermute(values, "tensor", [(0, 1), (1, 0)])


def hop(values, bits, size):
    return lax.ppermute(values, "fsdp", [(i, i ^ bits) for i in range(size)])


def block_places(size, me):
    spots = jnp.arange(BLOCKS, dtype=jnp.int32)
    if size != BLOCKS:
        return jnp.concatenate([spots] * 4)
    away = me ^ spots
    low, mid, high = away & 1, (away >> 1) & 1, away >> 2
    return jnp.concatenate(
        [
            low * 8 + mid * 4 + high,
            mid * 8 + low * 4 + high,
            mid * 8 + high * 2 + low,
            low * 8 + high * 2 + mid,
        ]
    )


def vmem_call(kernel, shapes, args, name):
    return pl.pallas_call(
        kernel,
        out_shape=shapes,
        compiler_params=pltpu.CompilerParams(vmem_limit_bytes=8 * 1024 * 1024),
        cost_estimate=LONG,
        name=name,
    )(*args)


def collect(pieces, cut):
    rows, width = pieces[0].shape

    def kernel(*refs):
        left, right = refs[len(pieces) :]
        for k, piece in enumerate(refs[: len(pieces)]):
            at = slice(k * rows, (k + 1) * rows)
            left[at, :] = piece[:, :cut]
            right[at, :] = piece[:, cut:]

    total = rows * len(pieces)
    return vmem_call(
        kernel,
        [jax.ShapeDtypeStruct((total, cut), LOW), jax.ShapeDtypeStruct((total, width - cut), LOW)],
        pieces,
        "collect",
    )


def far_rows(values, size):
    if size != BLOCKS:
        whole = lax.all_gather(values, "fsdp", axis=0, tiled=True)
        rows = whole.shape[0] // 4
        return [whole[k * rows : (k + 1) * rows] for k in range(4)]
    return [values] + [hop(values, 4 * k, size) for k in range(1, 4)]


def after(values, *done):
    return lax.optimization_barrier((values, done))[0]


def halves(whole):
    half = whole.shape[0] // 2
    return whole[:half], whole[half:]


def down_stage(left, right, size):
    if size != BLOCKS:
        return left, None, right, None
    return left, hop(left, 1, size), right, hop(right, 2, size)


def beside(left, left_far, right, right_far, size):
    if size != BLOCKS:
        return jnp.concatenate([left, right], axis=1)
    rows, cut = left.shape

    def kernel(one, one_far, two, two_far, out):
        out[:rows, :cut] = one[...]
        out[rows:, :cut] = one_far[...]
        out[:rows, cut:] = two[...]
        out[rows:, cut:] = two_far[...]

    shape = jax.ShapeDtypeStruct((2 * rows, 2 * cut), LOW)
    return vmem_call(kernel, [shape], (left, left_far, right, right_far), "beside")[0]


def in_order(own, core):
    other = swap_cores(own)
    return jnp.where(
        core == 0,
        jnp.concatenate([own, other], axis=0),
        jnp.concatenate([other, own], axis=0),
    )


def quarters(whole):
    rows = whole.shape[0] // 4
    return [whole[k * rows : (k + 1) * rows] for k in range(4)]


def spread(left, right, size):
    if size != BLOCKS:
        return quarters(left) + quarters(right)
    left_next, right_next = hop(left, 2, size), hop(right, 1, size)
    return [
        left,
        left_next,
        hop(left, 1, size),
        hop(left_next, 1, size),
        right,
        right_next,
        hop(right, 2, size),
        hop(right_next, 2, size),
    ]


def last_stage(left, right, size):
    if size != BLOCKS:
        return halves(left) + halves(right)
    return left, hop(left, 2, size), right, hop(right, 1, size)


def fold_half(groups, size):
    if size != BLOCKS:
        return [jnp.concatenate(part, axis=1) for part in zip(*groups)]
    count = len(groups)

    def kernel(*refs):
        low, high, low_two, high_two = refs[4 * count :]
        rows = low.shape[0]
        start = 0
        for k in range(count):
            one, one_far, two, two_far = refs[4 * k : 4 * k + 4]
            for a, b, to_low, to_high in (
                (one, one_far, low, high),
                (two, two_far, low_two, high_two),
            ):
                at = slice(start, start + a.shape[1]) if count > 1 else slice(None)
                to_low[:, at] = (a[:rows, :].astype(WIDE) + b[:rows, :].astype(WIDE)).astype(LOW)
                to_high[:, at] = (a[rows:, :].astype(WIDE) + b[rows:, :].astype(WIDE)).astype(LOW)
            start += one.shape[1]

    rows = groups[0][0].shape[0] // 2
    left = sum(group[0].shape[1] for group in groups)
    right = sum(group[2].shape[1] for group in groups)
    shapes = [jax.ShapeDtypeStruct((rows, n), LOW) for n in (left, left, right, right)]
    return vmem_call(kernel, shapes, [v for group in groups for v in group], "fold_half")


def fold_quarter(left, left_far, right, right_far, size):
    if size != BLOCKS:
        whole = jnp.concatenate(
            [jnp.concatenate([left, left_far], 0), jnp.concatenate([right, right_far], 0)], 1
        )
        return halves(whole)

    cut = left.shape[1]
    rows = left.shape[0] // 4

    def kernel(one, one_far, two, two_far, *outs):
        for k, out in enumerate(outs):
            at = slice(k * rows, (k + 1) * rows)
            out[:, :cut] = (one[at, :].astype(WIDE) + one_far[at, :].astype(WIDE)).astype(LOW)
            out[:, cut:] = (two[at, :].astype(WIDE) + two_far[at, :].astype(WIDE)).astype(LOW)

    shapes = [jax.ShapeDtypeStruct((rows, cut + right.shape[1]), LOW)] * 4
    return vmem_call(kernel, shapes, (left, left_far, right, right_far), "fold_quarter")


def first_send(left, left_send, right, right_send, size):
    if size != BLOCKS:
        return left, left_send, right, right_send
    return left, hop(left_send, 1, size), right, hop(right_send, 2, size)


def second_send(left, left_send, right, right_send, size):
    if size != BLOCKS:
        return left, left_send, right, right_send
    return left, hop(left_send, 2, size), right, hop(right_send, 1, size)


def third_send(parts, size):
    if size != BLOCKS:
        return parts
    return [parts[0]] + [hop(parts[k], 4 * k, size) for k in (3, 2, 1)]


def total_of(parts, size):
    if size != BLOCKS:
        whole = jnp.concatenate(parts, axis=0).astype(WIDE)
        return lax.psum_scatter(whole, "fsdp", scatter_dimension=0, tiled=True)
    total = parts[0].astype(WIDE)
    for part in parts[1:]:
        total = total + part.astype(WIDE)
    return total


def sum_near(values, size):
    if size != BLOCKS:
        return values
    for k in range(2):
        values = values + hop(values, 1 << k, size)
    return values


def sum_far(values, size):
    if size != BLOCKS:
        return lax.psum(values, "fsdp")
    for other in [hop(values, 4 * k, size) for k in range(1, 4)]:
        values = values + other
    return values


def body(
    size,
    inputs,
    segment_ids,
    qkv_weight,
    out_weight,
    up_weight,
    down_weight,
    gain_one,
    shift_one,
    gain_two,
    shift_two,
    cotangent,
):
    me = lax.axis_index("fsdp")
    core = lax.axis_index("tensor")
    rows, width = qkv_weight.shape[1:]
    half = inputs.shape[0]
    length = 2 * half
    table = block_places(size, me)

    norms = jnp.stack([gain_one, shift_one, gain_two, shift_two], axis=0)
    first = jnp.concatenate(
        [qkv_weight[0], qkv_weight[1], qkv_weight[2]]
        + [jnp.pad(norms, ((0, rows - 4), (0, LANES - rows)))],
        axis=1,
    ).astype(LOW)
    second = jnp.concatenate([up_weight, out_weight.T], axis=1).astype(LOW)
    hidden = down_weight.shape[0]
    third = [v.T.astype(LOW) for v in (down_weight[: hidden // 2], down_weight[hidden // 2 :])]
    first = far_rows(first, size)
    third = down_stage(*third, size)
    tokens = in_order(inputs, core)
    qkv = collect(after(first, tokens), (3 * width + LANES) // 2)
    second = far_rows(after(second, qkv), size)
    third = beside(*third, size)
    qkv = spread(*qkv, size)
    grad = in_order(cotangent, core)
    grad_flip = grad.T
    seg_col = jnp.broadcast_to(segment_ids[:, None], (length, LANES))
    seg_row = jnp.broadcast_to(segment_ids[None, :], (8, length))
    up_out = collect(after(second, qkv[1], qkv[5]), SIDE * (-(-second[0].shape[1] // (2 * SIDE))))
    third = far_rows(after(third, up_out), size)
    tokens, grad, grad_flip, seg_col, seg_row = after(
        (tokens, grad, grad_flip, seg_col, seg_row), up_out
    )
    up_out = spread(*up_out, size)

    one_flip, proj, qkv_whole, vectors = enter(rows, table, tokens, *qkv)
    proj = after(proj, up_out[1], up_out[5])
    att, lse = attend(proj, seg_col, seg_row, 0, width // LANES)
    down = collect(after(third, att), hidden // 2)
    att = after(att, down, up_out)
    down = last_stage(*down, size)
    part, out_whole = leave(table, att, *up_out[4:])
    far = swap_cores(part)
    middle, two_flip, act, slope, up_whole = feed_first(
        table, tokens, part, far, vectors, hidden, *up_out
    )
    down_parts = feed_weight(size, table, grad_flip, act)
    down = after(down, down_parts)
    down_parts = first_send(*down_parts, size)
    branch, pulled, pre = feed_tokens(table, grad, act, slope, up_whole, *down)
    up_parts = feed_weight(size, table, two_flip, pre)
    far = after(swap_cores(pulled), up_parts)
    up_parts = first_send(*up_parts, size)

    middle_grad, att_grad, *held, sums_two = middle_back(
        size, table, pulled, far, middle, grad, vectors, out_whole, att
    )
    pairs = width // LANES
    early = (2 * pairs + 2) // 3
    known = (proj, att, att_grad, lse, seg_col, seg_row)
    proj_grad = attend_back(*known, 0, early)
    parts = fold_half(after([down_parts, up_parts], proj_grad), size)
    proj_grad = after(proj_grad, parts)
    parts = second_send(*parts, size)
    proj_grad = attend_back(*known, early, pairs, (proj_grad,))
    tail = weight_back(size, table, proj_grad, one_flip, *held)
    proj_grad = after(proj_grad, tail)
    tail = first_send(*tail, size)
    pulled = token_back(proj_grad, qkv_whole)
    parts = fold_quarter(*after(parts, pulled), size)
    tail = fold_half([after(tail, parts)], size)
    parts = third_send(parts, size)
    far = after(swap_cores(pulled), tail)
    tail = second_send(*tail, size)
    input_grad, sums_one = leave_layer(
        core[None], pulled, far, tokens, middle_grad, vectors
    )
    tail = fold_quarter(*after(tail, input_grad), size)
    parts, branch, sums_one = after((parts, branch, sums_one), tail)
    tail = third_send(tail, size)

    def own_half(values):
        return lax.dynamic_slice_in_dim(values, core * half, half, 0)

    far = swap_cores(lax.dynamic_slice_in_dim(branch, (1 - core) * half, half, 0))
    outputs = own_half(middle) + (own_half(branch).astype(WIDE) + far.astype(WIDE))
    feed_grad = total_of(parts, size)
    sums = sum_near(jnp.concatenate([sums_one[:2], sums_two[:2]], axis=0), size)
    sums = sum_far(after(sums, tail), size)
    tail = total_of(tail, size)
    part = hidden // 2
    quarters = [feed_grad[:, k * part : (k + 1) * part] for k in range(4)]
    sums = lax.dynamic_slice_in_dim(sums, me * rows, rows, 1)
    qkv_grad = jnp.stack([tail[:, k * width : (k + 1) * width] for k in range(3)], axis=0)
    return (
        outputs,
        input_grad,
        qkv_grad,
        tail[:, 3 * width :].T,
        jnp.concatenate([quarters[1], quarters[3]], axis=1),
        jnp.concatenate([quarters[0].T, quarters[2].T], axis=0),
        sums[0],
        sums[1],
        sums[2],
        sums[3],
    )


def solution(mesh):
    tokens = P(("fsdp", "tensor"), None)
    split = P("fsdp")
    weights = (
        P(None, "fsdp", "tensor"),
        P("tensor", "fsdp"),
        P("fsdp", "tensor"),
        P("tensor", "fsdp"),
        split,
        split,
        split,
        split,
    )
    return jax.shard_map(
        functools.partial(body, mesh.shape["fsdp"]),
        mesh=mesh,
        in_specs=(tokens, split) + weights + (tokens,),
        out_specs=(tokens, tokens) + weights,
        check_vma=False,
    )
```
